128 devices in a mesh: seq: 32 (over y, z, x_lo), rep: 2 (over x_hi), own: 2 (over core).
Axes of the slice: x: 4 (x_hi: 2, x_lo: 2; x = x_hi * 2 + x_lo), y: 4, z: 4, core: 2. Of those that a mesh axis runs over, the one named last changes fastest.
Arguments:
- latent: bfloat16 [4096, 8, 1280], P('seq', ('rep', 'own')), may hold values from -40 to 40
- cotangent: bfloat16 [4096, 8, 1280], P('seq', ('rep', 'own')), may hold values from -16 to 16
- norm_gain: float32 [1280], replicated, may hold values from 0.1 to 1.9
- norm_shift: float32 [1280], replicated, may hold values from -3 to 3
- proj_qkv: bfloat16 [1280, 3072], P('own'), may hold values from -1 to 1
- proj_out: bfloat16 [1024, 1280], P('own'), may hold values from -0.1875 to 0.1875
Outputs:
- mixed: bfloat16 [4096, 8, 1280], P('seq', ('rep', 'own'))
- grad_latent: bfloat16 [4096, 8, 1280], P('seq', ('rep', 'own'))
- grad_proj_qkv: float32 [1280, 3072], P(('seq', 'rep', 'own'))
- grad_proj_out: float32 [1024, 1280], P(('seq', 'rep', 'own'))
The draws below stay inside these ranges and needn't reach their ends.
All inputs are finite; a program needn't handle non-finite values.
Results may differ from the reference program's by a relative error of at most 0.0055.
The reference program's roundings to bfloat16 on the way (of `normed`, `projected`, `probs_low`, `attended`, `grad_attended`, `dscores` and `grad_projected`) count: a program that leaves them out, or rounds other values in their place, can miss the bound.
Values may be sent and summed in bfloat16 or wider, within the bound.
A program may use at most 192 MiB of HBM per device.

```python
import math
import jax
import jax.numpy as jnp
from jax import lax

C = 1280
HEADS = 16
HEAD = 64
GROUPS = 32
L = 4096
BATCH = 8


def draw_latent(key, part):
    key_row, key_col, key_base = jax.random.split(key, 3)
    position = jnp.arange(L, dtype=jnp.float32) / L
    row_scale = 0.35 * jnp.exp(math.log(3.0) * position + jax.random.uniform(key_row, (L,), minval=-0.6, maxval=0.6))
    col_scale = jnp.exp(jax.random.uniform(key_col, (C,), minval=math.log(0.3), maxval=math.log(3.0)))
    values = jax.random.normal(key_base, (L, BATCH, C)) * row_scale[:, None, None] * col_scale[None, None, :]
    return jnp.clip(values, -40.0, 40.0).astype(jnp.bfloat16)


def draw_cotangent(key, part):
    key_row, key_base, key_common = jax.random.split(jax.random.fold_in(key, 7), 3)
    position = jnp.arange(L, dtype=jnp.float32) / L
    jitter = jax.random.uniform(key_row, (L,), minval=-0.3, maxval=0.3)
    row_scale = 0.5 * jnp.exp(math.log(3.0) * position + jitter)
    base = jax.random.normal(key_base, (L, BATCH, C))
    common = 1.2 * jax.random.normal(key_common, (1, BATCH, C))
    values = (base + common) * row_scale[:, None, None]
    return jnp.clip(values, -16.0, 16.0).astype(jnp.bfloat16)


def draw_proj_qkv(key, part):
    key_query, key_key, key_value = jax.random.split(key, 3)
    inner_width = HEADS * HEAD
    sharp = 1.6 / math.sqrt(C)
    drawn = 1.0 / math.sqrt(C)
    query_part = jax.random.normal(key_query, (C, inner_width)) * sharp
    key_part = jax.random.normal(key_key, (C, inner_width)) * sharp
    value_part = jax.random.normal(key_value, (C, inner_width)) * drawn
    return jnp.clip(jnp.concatenate([query_part, key_part, value_part], axis=1), -1.0, 1.0).astype(jnp.bfloat16)


def levels(stream_key, extent, cuts, least, top_value):
    loudness, own = 1.0, jax.random.fold_in(stream_key, 6)
    for dim, blocks in cuts:
        steps = jnp.exp(jax.random.uniform(jax.random.fold_in(own, dim), (blocks,), jnp.float32, least / len(cuts), top_value / len(cuts)))
        loudness = loudness * jnp.repeat(steps, extent[dim] // blocks).reshape([-1 if axis == dim else 1 for axis in range(len(extent))])
    return loudness


def bell_draw(rng, dims, width, limit, shards=(), kind=jnp.bfloat16):
    values = jax.random.normal(rng, dims, jnp.float32) * width
    if len(shards) > 0:
        values = levels(rng, dims, shards, -0.22, 0.18) * values
    return jnp.clip(values, min=-limit, max=limit).astype(kind)


def setup_inputs(seed: int = 0) -> dict:
    keys = jax.random.split(jax.random.key(seed), 7)
    return {
        "latent": draw_latent(jax.random.fold_in(keys[6], 71), 0),
        "cotangent": draw_cotangent(jax.random.fold_in(keys[6], 71), 0),
        "norm_gain": jnp.clip(1.0 + 0.18 * jax.random.normal(keys[2], (C,), jnp.float32), 0.1, 1.9),
        "norm_shift": bell_draw(keys[3], (C,), 0.5, 3.0, (), jnp.float32),
        "proj_qkv": draw_proj_qkv(jax.random.fold_in(keys[6], 71), 0),
        "proj_out": bell_draw(keys[5], (HEADS * HEAD, C), (HEADS * HEAD) ** -0.5, 0.1875, ((0, 2),)),
    }


def reference(latent, cotangent, norm_gain, norm_shift, proj_qkv, proj_out):
    length, images, channels = latent.shape
    per_group = channels // GROUPS
    inner_width = HEADS * HEAD
    score_scale = HEAD ** (-0.5)
    total_count = length * per_group
    values = latent.astype(jnp.float32)
    grouped = values.reshape(length, images, GROUPS, per_group)
    group_mean = lax.optimization_barrier(jnp.sum(grouped, axis=(0, 3))) / total_count
    group_meansq = lax.optimization_barrier(jnp.sum(grouped * grouped, axis=(0, 3))) / total_count
    inv_std = lax.rsqrt(group_meansq - group_mean * group_mean + 1e-06)
    centred = (grouped - group_mean[None, :, :, None]) * inv_std[None, :, :, None]
    normed = (centred.reshape(length, images, channels) * norm_gain + norm_shift).astype(jnp.bfloat16)
    normed_rows = normed.reshape(length * images, channels)
    projected = jnp.dot(normed_rows, proj_qkv, preferred_element_type=jnp.float32).astype(jnp.bfloat16)
    projected = projected.reshape(length, images, 3, HEADS, HEAD)
    grad_rows = cotangent.reshape(length * images, channels)
    grad_attended = jnp.dot(grad_rows, proj_out.T, preferred_element_type=jnp.float32).astype(jnp.bfloat16)
    grad_attended = grad_attended.reshape(length, images, HEADS, HEAD)

    def to_pairs(array):
        return array.transpose(1, 2, 0, 3).reshape(images * HEADS, length, HEAD)

    def from_pairs(array):
        return array.reshape(images, HEADS, length, HEAD).transpose(2, 0, 1, 3).reshape(length * images, inner_width)

    def one_pair(operands):
        query, key_rows, value_rows, grad_block = operands
        scores = jnp.dot(query, key_rows.T, preferred_element_type=jnp.float32) * score_scale
        row_max = lax.optimization_barrier(jnp.max(scores, axis=-1, keepdims=True))
        weights = jnp.exp(scores - row_max)
        probs = weights / lax.optimization_barrier(jnp.sum(weights, axis=-1, keepdims=True))
        probs_low = probs.astype(jnp.bfloat16)
        attended = jnp.dot(probs_low, value_rows, preferred_element_type=jnp.float32).astype(jnp.bfloat16)
        dprobs = jnp.dot(grad_block, value_rows.T, preferred_element_type=jnp.float32)
        row_delta = lax.optimization_barrier(jnp.sum(probs * dprobs, axis=-1, keepdims=True))
        dscores = (probs * (dprobs - row_delta) * score_scale).astype(jnp.bfloat16)
        grad_query = jnp.dot(dscores, key_rows, preferred_element_type=jnp.float32).astype(jnp.bfloat16)
        grad_key = jnp.dot(dscores.T, query, preferred_element_type=jnp.float32).astype(jnp.bfloat16)
        grad_value = jnp.dot(probs_low.T, grad_block, preferred_element_type=jnp.float32).astype(jnp.bfloat16)
        return (attended, grad_query, grad_key, grad_value)
    results = lax.map(one_pair, (to_pairs(projected[:, :, 0]), to_pairs(projected[:, :, 1]), to_pairs(projected[:, :, 2]), to_pairs(grad_attended)))
    attended_rows = from_pairs(results[0])
    mixed = (values + jnp.dot(attended_rows, proj_out, preferred_element_type=jnp.float32).reshape(length, images, channels)).astype(jnp.bfloat16)
    grad_proj_out = jnp.dot(attended_rows.T, grad_rows, preferred_element_type=jnp.float32)
    grad_projected = jnp.stack([from_pairs(results[1]).reshape(length, images, inner_width), from_pairs(results[2]).reshape(length, images, inner_width), from_pairs(results[3]).reshape(length, images, inner_width)], axis=2)
    grad_projected = grad_projected.reshape(length * images, 3 * inner_width)
    grad_proj_qkv = jnp.dot(normed_rows.T, grad_projected, preferred_element_type=jnp.float32)
    grad_normed = jnp.dot(grad_projected, proj_qkv.T, preferred_element_type=jnp.float32)
    grad_centred = (grad_normed.reshape(length, images, channels) * norm_gain).reshape(length, images, GROUPS, per_group)
    mean_one = lax.optimization_barrier(jnp.sum(grad_centred, axis=(0, 3))) / total_count
    mean_two = lax.optimization_barrier(jnp.sum(grad_centred * centred, axis=(0, 3))) / total_count
    grad_values = inv_std[None, :, :, None] * (grad_centred - mean_one[None, :, :, None] - centred * mean_two[None, :, :, None])
    grad_latent = (cotangent.astype(jnp.float32) + grad_values.reshape(length, images, channels)).astype(jnp.bfloat16)
    return (mixed, grad_latent, grad_proj_qkv, grad_proj_out)
```

```python
import functools

import jax
import jax.numpy as jnp
from jax import lax
from jax.experimental import pallas as pl
from jax.experimental.pallas import tpu as pltpu
from jax.sharding import Mesh
from jax.sharding import PartitionSpec as P

HEADS = 16
HEAD = 64
GROUPS = 32
SCALE = HEAD ** (-0.5)
SEQ = ("y", "z", "xl")
LINE = ("y", "z", "xl", "rep")
ALL = ("y", "z", "xl", "rep", "own")
F32, BF16 = jnp.float32, jnp.bfloat16
VMEM = 60 << 20


def members(channels):
    channel = lax.broadcasted_iota(jnp.int32, (channels, 128), 0)
    group = lax.broadcasted_iota(jnp.int32, (channels, 128), 1)
    first = group * (channels // GROUPS)
    return ((channel >= first) & (channel < first + channels // GROUPS)).astype(F32)


def by_group(rows, table):
    return lax.dot_general(
        rows, table, (((1,), (0,)), ((), ())),
        precision=lax.Precision.HIGHEST, preferred_element_type=F32,
    )


def by_channel(rows, table):
    return lax.dot_general(
        rows, table, (((1,), (1,)), ((), ())),
        precision=lax.Precision.HIGHEST, preferred_element_type=F32,
    )


def four_rows(rows):
    width = rows[0].shape[1]
    return jnp.concatenate([*rows, jnp.zeros((4, width), F32)], axis=0)


def stats_kernel(lat_ref, out_ref):
    rows = []
    values = [lat_ref[i].astype(F32) for i in range(2)]
    rows = [jnp.sum(v, axis=0, keepdims=True) for v in values]
    rows += [jnp.sum(v * v, axis=0, keepdims=True) for v in values]
    out_ref[...] = by_group(four_rows(rows), members(lat_ref.shape[2]))


def stats(lat):
    return pl.pallas_call(
        stats_kernel,
        out_shape=jax.ShapeDtypeStruct((8, 128), F32),
        compiler_params=pltpu.CompilerParams(vmem_limit_bytes=VMEM),
        cost_estimate=pl.CostEstimate(flops=1 << 20, bytes_accessed=lat.size * 2, transcendentals=0),
    )(lat)


def moments(sums, count):
    means = sums / count
    var = means[2:4] - means[0:2] * means[0:2]
    return jnp.concatenate([means[0:2], lax.rsqrt(var + 1e-06), jnp.zeros((4, 128), F32)], axis=0)


def project_kernel(count, own_ref, lat_ref, sums_ref, gain_ref, shift_ref, *refs):
    mine, other = refs[0:3], refs[3:6]
    out_ref, chan_ref, normed_ref = refs[6:]
    own = own_ref[0]
    half = mine[0].shape[0]

    @pl.when(pl.program_id(0) == 0)
    def _():
        table = members(lat_ref.shape[2])
        chan = by_channel(moments(jnp.sum(sums_ref[...], axis=0), count), table)
        chan_ref[...] = chan
        for i in range(2):
            centred = (lat_ref[i].astype(F32) - chan[i : i + 1]) * chan[2 + i : 3 + i]
            normed_ref[i * 128 : (i + 1) * 128] = (centred * gain_ref[...] + shift_ref[...]).astype(BF16)

    near = normed_ref[:, pl.ds(pl.multiple_of(own * half, 128), half)]
    far = normed_ref[:, pl.ds(pl.multiple_of((1 - own) * half, 128), half)]
    query, key, value = [
        jnp.dot(near, a[...], preferred_element_type=F32) + jnp.dot(far, b[...], preferred_element_type=F32)
        for a, b in zip(mine, other)
    ]
    low = lax.broadcasted_iota(jnp.int32, (128, 128), 1) < HEAD
    for h in range(0, query.shape[1] // HEAD, 2):
        for i in range(2):
            rows, lanes = slice(i * 128, (i + 1) * 128), slice(h * HEAD, (h + 2) * HEAD)
            q, k, v = query[rows, lanes], key[rows, lanes], value[rows, lanes]
            k_roll, v_roll = pltpu.roll(k, HEAD, 1), pltpu.roll(v, HEAD, 1)
            out_ref[h, i, :128] = jnp.where(low, k, v_roll).astype(BF16)
            out_ref[h + 1, i, :128] = jnp.where(low, k_roll, v).astype(BF16)
            first, second = q[:64], q[64:]
            out_ref[h, i, 128:] = jnp.where(low[:64], first, pltpu.roll(second, HEAD, 1)).astype(BF16)
            out_ref[h + 1, i, 128:] = jnp.where(low[:64], pltpu.roll(first, HEAD, 1), second).astype(BF16)


def project(own, lat, sums, gain, shift, mine, other, count):
    channels = lat.shape[2]
    cols, half = HEADS * HEAD // 256, mine.shape[0]

    def weight(part):
        return pl.BlockSpec((half, 256), lambda s, own: (0, part * cols + s))

    def whole(*shape):
        return pl.BlockSpec(shape, lambda s, own: (0,) * len(shape))

    return pl.pallas_call(
        functools.partial(project_kernel, count),
        grid_spec=pltpu.PrefetchScalarGridSpec(
            num_scalar_prefetch=1,
            grid=(cols,),
            in_specs=[whole(*lat.shape), whole(*sums.shape), whole(1, channels), whole(1, channels)]
            + [weight(p) for p in range(3)] * 2,
            out_specs=[pl.BlockSpec((4, 2, 192, 128), lambda s, own: (s, 0, 0, 0)), whole(8, channels)],
            scratch_shapes=[pltpu.VMEM((256, channels), BF16)],
        ),
        out_shape=[
            jax.ShapeDtypeStruct((HEADS, 2, 192, 128), BF16),
            jax.ShapeDtypeStruct((8, channels), F32),
        ],
        compiler_params=pltpu.CompilerParams(vmem_limit_bytes=VMEM),
        cost_estimate=pl.CostEstimate(flops=2 * 256 * 1280 * 3072, bytes_accessed=12 << 20, transcendentals=0),
    )(own, lat, sums, gain, shift, mine, mine, mine, other, other, other)


def attended_grad_kernel(own_ref, cot_ref, w_ref, out_ref):
    rows = cot_ref[...].reshape(256, cot_ref.shape[2])
    grad = lax.dot_general(rows, w_ref[...], (((1,), (1,)), ((), ())), preferred_element_type=F32)
    low = lax.broadcasted_iota(jnp.int32, (64, 128), 1) < HEAD
    for h in range(0, grad.shape[1] // HEAD, 2):
        for i in range(2):
            first = grad[i * 128 : i * 128 + 64, h * HEAD : (h + 2) * HEAD]
            second = grad[i * 128 + 64 : (i + 1) * 128, h * HEAD : (h + 2) * HEAD]
            out_ref[h, i] = jnp.where(low, first, pltpu.roll(second, HEAD, 1)).astype(BF16)
            out_ref[h + 1, i] = jnp.where(low, pltpu.roll(first, HEAD, 1), second).astype(BF16)


def attended_grad(own, cot, halves):
    channels = cot.shape[2]
    per = halves.shape[1] // 256

    return pl.pallas_call(
        attended_grad_kernel,
        grid_spec=pltpu.PrefetchScalarGridSpec(
            num_scalar_prefetch=1,
            grid=(2 * per,),
            in_specs=[
                pl.BlockSpec(cot.shape, lambda s, own: (0, 0, 0)),
                pl.BlockSpec((None, 256, channels), lambda s, own: (s // per, s % per, 0)),
            ],
            out_specs=pl.BlockSpec(
                (4, 2, 64, 128),
                lambda s, own: ((s // per + own[0] - 2 * own[0] * (s // per)) * per + s % per, 0, 0, 0),
            ),
        ),
        out_shape=jax.ShapeDtypeStruct((HEADS, 2, 64, 128), BF16),
        compiler_params=pltpu.CompilerParams(vmem_limit_bytes=VMEM),
        cost_estimate=pl.CostEstimate(flops=2 * 256 * 1280 * 1024, bytes_accessed=4 << 20, transcendentals=0),
    )(own, cot, halves)


def attention_kernel(ck, kvq_ref, g_ref, dqo_ref, dkv_ref, s_ref, x_ref, y_ref, acc_ref):
    step, last = pl.program_id(0), pl.num_programs(0) - 1
    sources, _, width = kvq_ref.shape
    keys = sources * 128
    here = dqo_ref.shape[0]
    rows = here * 128
    half = rows // 2

    @pl.when(step == 0)
    def _():
        acc_ref[...] = jnp.zeros_like(acc_ref)

    low = lax.broadcasted_iota(jnp.int32, (half, width), 1) < HEAD
    xq = kvq_ref[pl.ds(step * here, here), 128:192, :].reshape(half, width).astype(F32) * SCALE
    xg = g_ref[pl.ds(step * here, here), :, :].reshape(half, width).astype(F32)
    zero = jnp.zeros_like(xq)
    y_ref[0 * half : 1 * half] = jnp.where(low, xq, zero).astype(BF16)
    y_ref[1 * half : 2 * half] = jnp.where(low, pltpu.roll(xq, HEAD, 1), zero).astype(BF16)
    y_ref[2 * half : 3 * half] = jnp.where(low, zero, pltpu.roll(xg, HEAD, 1)).astype(BF16)
    y_ref[3 * half : 4 * half] = jnp.where(low, zero, xg).astype(BF16)
    y = y_ref[...]
    spans = [(c, c + ck) for c in range(0, keys, ck)]

    def kv_chunk(a, b):
        return kvq_ref[a // 128 : b // 128, :128, :].reshape(b - a, width)

    top = None
    for a, b in spans:
        both = lax.dot_general(y, kv_chunk(a, b), (((1,), (1,)), ((), ())), preferred_element_type=F32)
        s_ref[:, a:b] = both
        for t in range(0, ck, 128):
            piece = both[:rows, t : t + 128]
            top = piece if top is None else jnp.maximum(top, piece)
    top = jnp.max(top, axis=1, keepdims=True)
    total = jnp.zeros((rows, 128), F32)
    delta = jnp.zeros((rows, 128), F32)
    for a, b in spans:
        weights = jnp.exp(s_ref[:rows, a:b] - top)
        s_ref[:rows, a:b] = weights
        fold = weights * s_ref[rows:, a:b]
        for t in range(0, ck, 128):
            total = total + weights[:, t : t + 128]
            delta = delta + fold[:, t : t + 128]
    inverse = 1.0 / jnp.sum(total, axis=1, keepdims=True)
    delta = jnp.sum(delta, axis=1, keepdims=True) * inverse
    out = jnp.zeros((2 * rows, width), F32)
    for a, b in spans:
        probs = s_ref[:rows, a:b] * inverse
        x_ref[rows:, a:b] = probs.astype(BF16)
        x_ref[:rows, a:b] = (probs * (s_ref[rows:, a:b] - delta)).astype(BF16)
        x = x_ref[:, a:b]
        out = out + jnp.dot(x, kv_chunk(a, b), preferred_element_type=F32)
        acc_ref[a:b, :] += lax.dot_general(x, y, (((0,), (0,)), ((), ())), preferred_element_type=F32)
    lows = lax.broadcasted_iota(jnp.int32, (rows, width), 1) < HEAD
    res = jnp.where(lows, out[:rows] * SCALE, out[rows:]).astype(BF16)
    for h in range(2):
        for a in range(here):
            at = h * half + a * 64
            dqo_ref[a, h * 64 : (h + 1) * 64, :] = res[at : at + 64]

    @pl.when(step == last)
    def _():
        dkv_ref[...] = acc_ref[...].reshape(sources, 128, width).astype(BF16)


def attention(kvq, g, here=2, ck=1024):
    sources = kvq.shape[0]
    keys, rows = sources * 128, here * 128
    return pl.pallas_call(
        functools.partial(attention_kernel, ck),
        grid=(sources // here,),
        in_specs=[
            pl.BlockSpec((sources, 192, 128), lambda i: (0, 0, 0), pipeline_mode=pl.Buffered(1)),
            pl.BlockSpec((sources, 64, 128), lambda i: (0, 0, 0), pipeline_mode=pl.Buffered(1)),
        ],
        out_specs=[
            pl.BlockSpec((here, 128, 128), lambda i: (i, 0, 0)),
            pl.BlockSpec((sources, 128, 128), lambda i: (0, 0, 0)),
        ],
        out_shape=[
            jax.ShapeDtypeStruct((sources, 128, 128), BF16),
            jax.ShapeDtypeStruct((sources, 128, 128), BF16),
        ],
        scratch_shapes=[
            pltpu.VMEM((2 * rows, keys), F32),
            pltpu.VMEM((2 * rows, keys), BF16),
            pltpu.VMEM((2 * rows, 128), BF16),
            pltpu.VMEM((keys, 128), F32),
        ],
        compiler_params=pltpu.CompilerParams(vmem_limit_bytes=VMEM),
        cost_estimate=pl.CostEstimate(flops=48 * keys * keys * HEAD, bytes_accessed=4 << 20, transcendentals=keys * keys),
    )(kvq, g)


def in_weight_kernel(lat_ref, chan_ref, gain_ref, shift_ref, dqo_ref, dkv_ref, out_ref, acc_ref, turned_ref):
    step, last = pl.program_id(0), pl.num_programs(0) - 1
    sources, _, channels = lat_ref.shape
    rows = sources * 128

    @pl.when(step == 0)
    def _():
        acc_ref[...] = jnp.zeros_like(acc_ref)

    lat = lat_ref[...].reshape(rows, channels).astype(F32)
    centred = (lat - chan_ref[0:1]) * chan_ref[1:2]
    normed = (centred * gain_ref[...] + shift_ref[...]).astype(BF16)
    grads = jnp.concatenate(
        [dqo_ref[...].reshape(rows, 128), dkv_ref[...].reshape(rows, 128)], axis=1
    )
    acc_ref[...] += lax.dot_general(grads, normed, (((0,), (0,)), ((), ())), preferred_element_type=F32)

    @pl.when(step == last)
    def _():
        turned_ref[...] = acc_ref[...].T
        low = lax.broadcasted_iota(jnp.int32, (5, 128), 1) < HEAD
        for d in range(channels // 10):
            at = d * 10
            out_ref[d, 0:10] = turned_ref[at : at + 10, 128:256]
            first, second = turned_ref[at : at + 5, 0:128], turned_ref[at + 5 : at + 10, 0:128]
            out_ref[d, 10:15] = jnp.where(low, first, pltpu.roll(second, HEAD, 1))
            out_ref[d, 15:16] = jnp.zeros((1, 128), F32)


def in_weight(lat, chan, gain, shift, dqo, dkv, here=4):
    sources, _, channels = lat.shape
    return pl.pallas_call(
        in_weight_kernel,
        grid=(sources // here,),
        in_specs=[
            pl.BlockSpec((here, 128, channels), lambda i: (i, 0, 0)),
            pl.BlockSpec((2, channels), lambda i: (0, 0)),
            pl.BlockSpec((1, channels), lambda i: (0, 0)),
            pl.BlockSpec((1, channels), lambda i: (0, 0)),
            pl.BlockSpec((here, 128, 128), lambda i: (i, 0, 0)),
            pl.BlockSpec((here, 128, 128), lambda i: (i, 0, 0)),
        ],
        out_specs=pl.BlockSpec((channels // 10, 16, 128), lambda i: (0, 0, 0)),
        out_shape=jax.ShapeDtypeStruct((channels // 10, 16, 128), F32),
        scratch_shapes=[pltpu.VMEM((256, channels), F32), pltpu.VMEM((channels, 256), F32)],
        compiler_params=pltpu.CompilerParams(vmem_limit_bytes=VMEM),
        cost_estimate=pl.CostEstimate(flops=2 * 4096 * 1280 * 256, bytes_accessed=14 << 20, transcendentals=0),
    )(lat, chan, gain, shift, dqo, dkv)


def paired(first, second, low, upper):
    if upper:
        return jnp.where(low, pltpu.roll(first.astype(F32), HEAD, 1), second.astype(F32)).astype(BF16)
    return jnp.where(low, first.astype(F32), pltpu.roll(second.astype(F32), HEAD, 1)).astype(BF16)


def mixed_kernel(own_ref, dqo_ref, lat_ref, w_ref, mixed_ref, att_ref):
    half = w_ref.shape[1]
    low = lax.broadcasted_iota(jnp.int32, (128, 128), 1) < HEAD
    for h in range(0, HEADS, 2):
        for i in range(2):
            att_ref[i, :, h * HEAD : (h + 2) * HEAD] = paired(dqo_ref[h, i], dqo_ref[h + 1, i], low, True)
    own = own_ref[0]
    for i in range(2):
        near = att_ref[i, :, pl.ds(pl.multiple_of(own * half, 128), half)]
        far = att_ref[i, :, pl.ds(pl.multiple_of((1 - own) * half, 128), half)]
        total = jnp.dot(near, w_ref[0], preferred_element_type=F32)
        total = total + jnp.dot(far, w_ref[1], preferred_element_type=F32)
        mixed_ref[i] = (lat_ref[i].astype(F32) + total).astype(BF16)


def mix(own, dqo, lat, halves):
    channels = lat.shape[2]

    def whole(*shape):
        return pl.BlockSpec(shape, lambda s, own: (0,) * len(shape))

    return pl.pallas_call(
        mixed_kernel,
        grid_spec=pltpu.PrefetchScalarGridSpec(
            num_scalar_prefetch=1,
            grid=(1,),
            in_specs=[whole(*dqo.shape), whole(*lat.shape), whole(*halves.shape)],
            out_specs=[whole(*lat.shape), whole(2, 128, HEADS * HEAD)],
        ),
        out_shape=[
            jax.ShapeDtypeStruct(lat.shape, BF16),
            jax.ShapeDtypeStruct((2, 128, HEADS * HEAD), BF16),
        ],
        compiler_params=pltpu.CompilerParams(vmem_limit_bytes=VMEM),
        cost_estimate=pl.CostEstimate(flops=2 * 256 * 1280 * 1024, bytes_accessed=6 << 20, transcendentals=0),
    )(own, dqo, lat, halves)


def out_weight_kernel(own_ref, att_ref, att_far_ref, cot_ref, cot_far_ref, out_ref):
    channels = cot_ref.shape[2]
    wide = att_ref.shape[2]
    att = jnp.concatenate([att_ref[...].reshape(256, wide), att_far_ref[...].reshape(256, wide)], axis=0)
    cot = jnp.concatenate([cot_ref[...].reshape(256, channels), cot_far_ref[...].reshape(256, channels)], axis=0)
    total = lax.dot_general(att, cot, (((0,), (0,)), ((), ())), preferred_element_type=F32)
    blocks = total.reshape(wide // 16, 2, 8, channels)
    own = own_ref[0]
    out_ref[...] = jnp.where(own == 0, blocks[:, 0], blocks[:, 1])


def out_weight(own, att, att_far, cot, cot_far):
    channels, wide = cot.shape[2], att.shape[2]
    tile = 256
    side = pl.BlockSpec((2, 128, tile), lambda s, own: (0, 0, s))
    full = pl.BlockSpec(cot.shape, lambda s, own: (0, 0, 0))
    return pl.pallas_call(
        out_weight_kernel,
        grid_spec=pltpu.PrefetchScalarGridSpec(
            num_scalar_prefetch=1,
            grid=(wide // tile,),
            in_specs=[side, side, full, full],
            out_specs=pl.BlockSpec((tile // 16, 8, channels), lambda s, own: (s, 0, 0)),
        ),
        out_shape=jax.ShapeDtypeStruct((wide // 16, 8, channels), F32),
        compiler_params=pltpu.CompilerParams(vmem_limit_bytes=VMEM),
        cost_estimate=pl.CostEstimate(flops=4 * 256 * 1280 * 1024, bytes_accessed=6 << 20, transcendentals=0),
    )(own, att, att_far, cot, cot_far)


def back_kernel(own_ref, dqo_ref, dkv_ref, mine_ref, other_ref, lat_ref, chan_ref, gain_ref, grad_ref, sums_ref, rows_ref):
    own = own_ref[0]
    inner, half = HEADS * HEAD, mine_ref.shape[0]
    low = lax.broadcasted_iota(jnp.int32, (128, 128), 1) < HEAD
    for h in range(0, HEADS, 2):
        for i in range(2):
            rows, at = slice(i * 128, (i + 1) * 128), h * HEAD
            dq, dk = (dqo_ref[h, i], dqo_ref[h + 1, i]), (dkv_ref[h, i], dkv_ref[h + 1, i])
            rows_ref[rows, at : at + 128] = paired(*dq, low, False)
            rows_ref[rows, inner + at : inner + at + 128] = paired(*dk, low, False)
            rows_ref[rows, 2 * inner + at : 2 * inner + at + 128] = paired(*dk, low, True)
    grads = rows_ref[...]
    for side, w_ref in ((own, mine_ref), (1 - own, other_ref)):
        part = lax.dot_general(grads, w_ref[...], (((1,), (1,)), ((), ())), preferred_element_type=F32)
        lanes = pl.ds(pl.multiple_of(side * half, 128), half)
        for i in range(2):
            grad_ref[i, :, lanes] = part[i * 128 : (i + 1) * 128]
    ones, twos = [], []
    for i in range(2):
        grad = grad_ref[i] * gain_ref[...]
        grad_ref[i] = grad
        centred = (lat_ref[i].astype(F32) - chan_ref[i : i + 1]) * chan_ref[2 + i : 3 + i]
        ones.append(jnp.sum(grad, axis=0, keepdims=True))
        twos.append(jnp.sum(grad * centred, axis=0, keepdims=True))
    sums_ref[...] = by_group(four_rows(ones + twos), members(lat_ref.shape[2]))


def back(own, dqo, dkv, mine, other, lat, chan, gain):
    def whole(shape):
        return pl.BlockSpec(shape, lambda s, own: (0,) * len(shape), pipeline_mode=pl.Buffered(1))

    operands = (dqo, dkv, mine, other, lat, chan, gain)
    return pl.pallas_call(
        back_kernel,
        grid_spec=pltpu.PrefetchScalarGridSpec(
            num_scalar_prefetch=1,
            grid=(1,),
            in_specs=[whole(a.shape) for a in operands],
            out_specs=[whole(lat.shape), whole((8, 128))],
            scratch_shapes=[pltpu.VMEM((256, 3 * HEADS * HEAD), BF16)],
        ),
        out_shape=[jax.ShapeDtypeStruct(lat.shape, F32), jax.ShapeDtypeStruct((8, 128), F32)],
        compiler_params=pltpu.CompilerParams(vmem_limit_bytes=VMEM),
        cost_estimate=pl.CostEstimate(flops=2 * 256 * 1280 * 3072, bytes_accessed=14 << 20, transcendentals=0),
    )(own, *operands)


def final_kernel(count, grad_ref, sums_ref, lat_ref, cot_ref, chan_ref, out_ref):
    table = members(lat_ref.shape[2])
    means = by_channel(jnp.sum(sums_ref[...], axis=0) / count, table)
    for i in range(2):
        inv = chan_ref[2 + i : 3 + i]
        centred = (lat_ref[i].astype(F32) - chan_ref[i : i + 1]) * inv
        grad = inv * (grad_ref[i] - means[i : i + 1] - centred * means[2 + i : 3 + i])
        out_ref[i] = (cot_ref[i].astype(F32) + grad).astype(BF16)


def final(grad, sums, lat, cot, chan, count):
    return pl.pallas_call(
        functools.partial(final_kernel, count),
        out_shape=jax.ShapeDtypeStruct(lat.shape, BF16),
        compiler_params=pltpu.CompilerParams(vmem_limit_bytes=VMEM),
        cost_estimate=pl.CostEstimate(flops=4 << 20, bytes_accessed=4 << 20, transcendentals=0),
    )(grad, sums, lat, cot, chan)


def swapped(value, axis):
    return lax.ppermute(value, axis, [(0, 1), (1, 0)])


def exchanged(value, axes):
    return lax.all_to_all(value, axes, 0, 0, tiled=True)


def shared(value, axes):
    return exchanged(jnp.broadcast_to(value[None], (lax.axis_size(axes), *value.shape)), axes)


def shards(latent, cotangent, norm_gain, norm_shift, proj_qkv, proj_out):
    local_len, images, channels = latent.shape
    seq_count = lax.axis_size(SEQ)
    count = local_len * seq_count * (channels // GROUPS)
    own = lax.axis_index("own").reshape(1)
    gain, shift = norm_gain.reshape(1, channels), norm_shift.reshape(1, channels)

    other_out = swapped(proj_out, "own")
    other_qkv = swapped(proj_qkv, "own")
    lat, cot = latent.transpose(1, 0, 2), cotangent.transpose(1, 0, 2)
    image_lat = lax.all_gather(exchanged(lat, "xl"), ("y", "z"), tiled=True)
    sums = shared(stats(lat), SEQ)
    halves_out = jnp.stack([proj_out, other_out])
    cot_far = swapped(cot, "own")
    g_send = attended_grad(own, cot, halves_out)
    g = exchanged(g_send.reshape(seq_count, 64, 128), SEQ)
    kvq_send, chan = project(own, lat, sums, gain, shift, proj_qkv, other_qkv, count)
    kvq = exchanged(kvq_send.reshape(seq_count, 192, 128), SEQ)

    dqo, dkv = attention(kvq, g)

    dqo_tok = exchanged(dqo, SEQ).reshape(HEADS, images, 128, 128)
    dkv_tok = exchanged(dkv, SEQ).reshape(HEADS, images, 128, 128)
    image = lax.axis_index("xl")
    chan_image = lax.dynamic_slice_in_dim(chan[:4].reshape(2, 2, channels), image, 1, 1).reshape(2, channels)
    in_part = in_weight(image_lat, chan_image, gain, shift, dqo, dkv)
    mixed, att = mix(own, dqo_tok, lat, halves_out)
    out_part = out_weight(own, att, swapped(att, "own"), cot, cot_far)
    out_blocks = exchanged(out_part, LINE)
    in_blocks = exchanged(in_part, ALL)
    grad, back_sums = back(own, dqo_tok, dkv_tok, proj_qkv, other_qkv, lat, chan, gain)
    grad_latent = final(grad, shared(back_sums, SEQ), lat, cot, chan, count)

    grad_out = jnp.sum(out_blocks, axis=0)
    summed = jnp.sum(in_blocks.reshape(HEADS, 8, 16, 128), axis=1)
    dq = summed[:, 10:15].reshape(HEADS, 5, 2, HEAD).transpose(2, 1, 0, 3).reshape(10, HEADS * HEAD)
    dk = summed[:, :10, :HEAD].transpose(1, 0, 2).reshape(10, HEADS * HEAD)
    dv = summed[:, :10, HEAD:].transpose(1, 0, 2).reshape(10, HEADS * HEAD)
    grad_qkv = jnp.concatenate([dq, dk, dv], axis=1)
    return (mixed.transpose(1, 0, 2), grad_latent.transpose(1, 0, 2), grad_qkv, grad_out)


def solution(mesh):
    fine = Mesh(mesh.devices.reshape(4, 4, 2, 2, 2), ALL)
    tokens = P(SEQ, ("rep", "own"), None)
    return jax.shard_map(
        shards,
        mesh=fine,
        in_specs=(tokens, tokens, P(), P(), P("own", None), P("own", None)),
        out_specs=(tokens, tokens, P(ALL, None), P(ALL, None)),
        check_vma=False,
    )
```

```python
import functools

import jax
import jax.numpy as jnp
from jax import lax
from jax.experimental import pallas as pl
from jax.experimental.pallas import tpu as pltpu
from jax.sharding import Mesh
from jax.sharding import PartitionSpec as P

HEADS = 16
HEAD = 64
GROUPS = 32
SCALE = HEAD ** (-0.5)
SEQ = ("y", "z", "xl")
LINE = ("y", "z", "xl", "rep")
ALL = ("y", "z", "xl", "rep", "own")
F32, BF16 = jnp.float32, jnp.bfloat16
VMEM = 60 << 20


def members(channels):
    channel = lax.broadcasted_iota(jnp.int32, (channels, 128), 0)
    group = lax.broadcasted_iota(jnp.int32, (channels, 128), 1)
    first = group * (channels // GROUPS)
    return ((channel >= first) & (channel < first + channels // GROUPS)).astype(F32)


def by_group(rows, table):
    return lax.dot_general(
        rows, table, (((1,), (0,)), ((), ())),
        precision=lax.Precision.HIGHEST, preferred_element_type=F32,
    )


def by_channel(rows, table):
    return lax.dot_general(
        rows, table, (((1,), (1,)), ((), ())),
        precision=lax.Precision.HIGHEST, preferred_element_type=F32,
    )


def four_rows(rows):
    width = rows[0].shape[1]
    return jnp.concatenate([*rows, jnp.zeros((4, width), F32)], axis=0)


def stats_kernel(lat_ref, out_ref):
    values = [lat_ref[i].astype(F32) for i in range(2)]
    rows = [jnp.sum(v, axis=0, keepdims=True) for v in values]
    rows += [jnp.sum(v * v, axis=0, keepdims=True) for v in values]
    out_ref[...] = jnp.broadcast_to(by_group(four_rows(rows), members(lat_ref.shape[2]))[None], out_ref.shape)


def stats(lat, copies):
    return pl.pallas_call(
        stats_kernel,
        out_shape=jax.ShapeDtypeStruct((copies, 8, 128), F32),
        compiler_params=pltpu.CompilerParams(vmem_limit_bytes=VMEM),
        cost_estimate=pl.CostEstimate(flops=1 << 20, bytes_accessed=lat.size * 2, transcendentals=0),
    )(lat)


def moments(sums, count):
    means = sums / count
    var = means[2:4] - means[0:2] * means[0:2]
    return jnp.concatenate([means[0:2], lax.rsqrt(var + 1e-06), jnp.zeros((4, 128), F32)], axis=0)


def project_kernel(count, own_ref, lat_ref, sums_ref, gain_ref, shift_ref, g_ref, *refs):
    mine, other = refs[0:3], refs[3:6]
    out_ref, chan_ref, normed_ref = refs[6:]
    own = own_ref[0]
    half = mine[0].shape[0]

    @pl.when(pl.program_id(0) == 0)
    def _():
        table = members(lat_ref.shape[2])
        chan = by_channel(moments(jnp.sum(sums_ref[...], axis=0), count), table)
        chan_ref[...] = chan
        for i in range(2):
            centred = (lat_ref[i].astype(F32) - chan[i : i + 1]) * chan[2 + i : 3 + i]
            normed_ref[i * 128 : (i + 1) * 128] = (centred * gain_ref[...] + shift_ref[...]).astype(BF16)

    out_ref[:, :, 192:256] = g_ref[...]
    near = normed_ref[:, pl.ds(pl.multiple_of(own * half, 128), half)]
    far = normed_ref[:, pl.ds(pl.multiple_of((1 - own) * half, 128), half)]
    query, key, value = [
        jnp.dot(near, a[...], preferred_element_type=F32) + jnp.dot(far, b[...], preferred_element_type=F32)
        for a, b in zip(mine, other)
    ]
    low = lax.broadcasted_iota(jnp.int32, (128, 128), 1) < HEAD
    for h in range(0, query.shape[1] // HEAD, 2):
        for i in range(2):
            rows, lanes = slice(i * 128, (i + 1) * 128), slice(h * HEAD, (h + 2) * HEAD)
            q, k, v = query[rows, lanes], key[rows, lanes], value[rows, lanes]
            k_roll, v_roll = pltpu.roll(k, HEAD, 1), pltpu.roll(v, HEAD, 1)
            out_ref[h, i, :128] = jnp.where(low, k, v_roll).astype(BF16)
            out_ref[h + 1, i, :128] = jnp.where(low, k_roll, v).astype(BF16)
            first, second = q[:64], q[64:]
            out_ref[h, i, 128:192] = jnp.where(low[:64], first, pltpu.roll(second, HEAD, 1)).astype(BF16)
            out_ref[h + 1, i, 128:192] = jnp.where(low[:64], pltpu.roll(first, HEAD, 1), second).astype(BF16)


def project(own, lat, sums, gain, shift, g, mine, other, count):
    channels = lat.shape[2]
    cols, half = HEADS * HEAD // 256, mine.shape[0]

    def weight(part):
        return pl.BlockSpec((half, 256), lambda s, own: (0, part * cols + s))

    def whole(*shape):
        return pl.BlockSpec(shape, lambda s, own: (0,) * len(shape))

    return pl.pallas_call(
        functools.partial(project_kernel, count),
        grid_spec=pltpu.PrefetchScalarGridSpec(
            num_scalar_prefetch=1,
            grid=(cols,),
            in_specs=[whole(*lat.shape), whole(*sums.shape), whole(1, channels), whole(1, channels)]
            + [pl.BlockSpec((4, 2, 64, 128), lambda s, own: (s, 0, 0, 0))]
            + [weight(p) for p in range(3)] * 2,
            out_specs=[pl.BlockSpec((4, 2, 256, 128), lambda s, own: (s, 0, 0, 0)), whole(8, channels)],
            scratch_shapes=[pltpu.VMEM((256, channels), BF16)],
        ),
        out_shape=[
            jax.ShapeDtypeStruct((HEADS, 2, 256, 128), BF16),
            jax.ShapeDtypeStruct((8, channels), F32),
        ],
        compiler_params=pltpu.CompilerParams(vmem_limit_bytes=VMEM),
        cost_estimate=pl.CostEstimate(flops=2 * 256 * 1280 * 3072, bytes_accessed=12 << 20, transcendentals=0),
    )(own, lat, sums, gain, shift, g, mine, mine, mine, other, other, other)


def attended_grad_kernel(own_ref, cot_ref, w_ref, out_ref):
    rows = cot_ref[...].reshape(256, cot_ref.shape[2])
    grad = lax.dot_general(rows, w_ref[...], (((1,), (1,)), ((), ())), preferred_element_type=F32)
    low = lax.broadcasted_iota(jnp.int32, (64, 128), 1) < HEAD
    for h in range(0, grad.shape[1] // HEAD, 2):
        for i in range(2):
            first = grad[i * 128 : i * 128 + 64, h * HEAD : (h + 2) * HEAD]
            second = grad[i * 128 + 64 : (i + 1) * 128, h * HEAD : (h + 2) * HEAD]
            out_ref[h, i] = jnp.where(low, first, pltpu.roll(second, HEAD, 1)).astype(BF16)
            out_ref[h + 1, i] = jnp.where(low, pltpu.roll(first, HEAD, 1), second).astype(BF16)


def attended_grad(own, cot, halves):
    channels = cot.shape[2]
    per = halves.shape[1] // 256

    return pl.pallas_call(
        attended_grad_kernel,
        grid_spec=pltpu.PrefetchScalarGridSpec(
            num_scalar_prefetch=1,
            grid=(2 * per,),
            in_specs=[
                pl.BlockSpec(cot.shape, lambda s, own: (0, 0, 0)),
                pl.BlockSpec((None, 256, channels), lambda s, own: (s // per, s % per, 0)),
            ],
            out_specs=pl.BlockSpec(
                (4, 2, 64, 128),
                lambda s, own: ((s // per + own[0] - 2 * own[0] * (s // per)) * per + s % per, 0, 0, 0),
            ),
        ),
        out_shape=jax.ShapeDtypeStruct((HEADS, 2, 64, 128), BF16),
        compiler_params=pltpu.CompilerParams(vmem_limit_bytes=VMEM),
        cost_estimate=pl.CostEstimate(flops=2 * 256 * 1280 * 1024, bytes_accessed=4 << 20, transcendentals=0),
    )(own, cot, halves)


def attention_kernel(ck, kvq_ref, dqo_ref, dkv_ref, s_ref, x_ref, y_ref, acc_ref):
    step, last = pl.program_id(0), pl.num_programs(0) - 1
    sources, _, width = kvq_ref.shape
    keys = sources * 128
    here = dqo_ref.shape[0]
    rows = here * 128
    half = rows // 2

    @pl.when(step == 0)
    def _():
        acc_ref[...] = jnp.zeros_like(acc_ref)

    low = lax.broadcasted_iota(jnp.int32, (half, width), 1) < HEAD
    xq = kvq_ref[pl.ds(step * here, here), 128:192, :].reshape(half, width).astype(F32) * SCALE
    xg = kvq_ref[pl.ds(step * here, here), 192:256, :].reshape(half, width).astype(F32)
    zero = jnp.zeros_like(xq)
    y_ref[0 * half : 1 * half] = jnp.where(low, xq, zero).astype(BF16)
    y_ref[1 * half : 2 * half] = jnp.where(low, pltpu.roll(xq, HEAD, 1), zero).astype(BF16)
    y_ref[2 * half : 3 * half] = jnp.where(low, zero, pltpu.roll(xg, HEAD, 1)).astype(BF16)
    y_ref[3 * half : 4 * half] = jnp.where(low, zero, xg).astype(BF16)
    y = y_ref[...]
    spans = [(c, c + ck) for c in range(0, keys, ck)]

    def kv_chunk(a, b):
        return kvq_ref[a // 128 : b // 128, :128, :].reshape(b - a, width)

    top = None
    for a, b in spans:
        both = lax.dot_general(y, kv_chunk(a, b), (((1,), (1,)), ((), ())), preferred_element_type=F32)
        s_ref[:, a:b] = both
        for t in range(0, ck, 128):
            piece = both[:rows, t : t + 128]
            top = piece if top is None else jnp.maximum(top, piece)
    top = jnp.max(top, axis=1, keepdims=True)
    total = jnp.zeros((rows, 128), F32)
    delta = jnp.zeros((rows, 128), F32)
    for a, b in spans:
        weights = jnp.exp(s_ref[:rows, a:b] - top)
        s_ref[:rows, a:b] = weights
        fold = weights * s_ref[rows:, a:b]
        for t in range(0, ck, 128):
            total = total + weights[:, t : t + 128]
            delta = delta + fold[:, t : t + 128]
    inverse = 1.0 / jnp.sum(total, axis=1, keepdims=True)
    delta = jnp.sum(delta, axis=1, keepdims=True) * inverse
    out = jnp.zeros((2 * rows, width), F32)
    for a, b in spans:
        probs = s_ref[:rows, a:b] * inverse
        x_ref[rows:, a:b] = probs.astype(BF16)
        x_ref[:rows, a:b] = (probs * (s_ref[rows:, a:b] - delta)).astype(BF16)
        x = x_ref[:, a:b]
        out = out + jnp.dot(x, kv_chunk(a, b), preferred_element_type=F32)
        acc_ref[a:b, :] += lax.dot_general(x, y, (((0,), (0,)), ((), ())), preferred_element_type=F32)
    lows = lax.broadcasted_iota(jnp.int32, (rows, width), 1) < HEAD
    res = jnp.where(lows, out[:rows] * SCALE, out[rows:]).astype(BF16)
    for h in range(2):
        for a in range(here):
            at = h * half + a * 64
            dqo_ref[a, h * 64 : (h + 1) * 64, :] = res[at : at + 64]

    @pl.when(step == last)
    def _():
        dkv_ref[...] = acc_ref[...].reshape(sources, 128, width).astype(BF16)


def attention(kvq, here=2, ck=1024):
    sources = kvq.shape[0]
    keys, rows = sources * 128, here * 128
    return pl.pallas_call(
        functools.partial(attention_kernel, ck),
        grid=(sources // here,),
        in_specs=[
            pl.BlockSpec((sources, 256, 128), lambda i: (0, 0, 0), pipeline_mode=pl.Buffered(1)),
        ],
        out_specs=[
            pl.BlockSpec((here, 128, 128), lambda i: (i, 0, 0)),
            pl.BlockSpec((sources, 128, 128), lambda i: (0, 0, 0)),
        ],
        out_shape=[
            jax.ShapeDtypeStruct((sources, 128, 128), BF16),
            jax.ShapeDtypeStruct((sources, 128, 128), BF16),
        ],
        scratch_shapes=[
            pltpu.VMEM((2 * rows, keys), F32),
            pltpu.VMEM((2 * rows, keys), BF16),
            pltpu.VMEM((2 * rows, 128), BF16),
            pltpu.VMEM((keys, 128), F32),
        ],
        compiler_params=pltpu.CompilerParams(vmem_limit_bytes=VMEM),
        cost_estimate=pl.CostEstimate(flops=48 * keys * keys * HEAD, bytes_accessed=4 << 20, transcendentals=keys * keys),
    )(kvq)


def in_weight_kernel(lat_ref, chan_ref, gain_ref, shift_ref, dqo_ref, dkv_ref, out_ref, acc_ref, turned_ref):
    step, last = pl.program_id(0), pl.num_programs(0) - 1
    sources, _, channels = lat_ref.shape
    rows = sources * 128

    @pl.when(step == 0)
    def _():
        acc_ref[...] = jnp.zeros_like(acc_ref)

    lat = lat_ref[...].reshape(rows, channels).astype(F32)
    centred = (lat - chan_ref[0:1]) * chan_ref[1:2]
    normed = (centred * gain_ref[...] + shift_ref[...]).astype(BF16)
    grads = jnp.concatenate(
        [dqo_ref[...].reshape(rows, 128), dkv_ref[...].reshape(rows, 128)], axis=1
    )
    acc_ref[...] += lax.dot_general(grads, normed, (((0,), (0,)), ((), ())), preferred_element_type=F32)

    @pl.when(step == last)
    def _():
        turned_ref[...] = acc_ref[...].T
        low = lax.broadcasted_iota(jnp.int32, (5, 128), 1) < HEAD
        for d in range(channels // 10):
            at = d * 10
            out_ref[d, 0:10] = turned_ref[at : at + 10, 128:256]
            first, second = turned_ref[at : at + 5, 0:128], turned_ref[at + 5 : at + 10, 0:128]
            out_ref[d, 10:15] = jnp.where(low, first, pltpu.roll(second, HEAD, 1))
            out_ref[d, 15:16] = jnp.zeros((1, 128), F32)


def in_weight(lat, chan, gain, shift, dqo, dkv, here=4):
    sources, _, channels = lat.shape
    return pl.pallas_call(
        in_weight_kernel,
        grid=(sources // here,),
        in_specs=[
            pl.BlockSpec((here, 128, channels), lambda i: (i, 0, 0)),
            pl.BlockSpec((2, channels), lambda i: (0, 0)),
            pl.BlockSpec((1, channels), lambda i: (0, 0)),
            pl.BlockSpec((1, channels), lambda i: (0, 0)),
            pl.BlockSpec((here, 128, 128), lambda i: (i, 0, 0)),
            pl.BlockSpec((here, 128, 128), lambda i: (i, 0, 0)),
        ],
        out_specs=pl.BlockSpec((channels // 10, 16, 128), lambda i: (0, 0, 0)),
        out_shape=jax.ShapeDtypeStruct((channels // 10, 16, 128), F32),
        scratch_shapes=[pltpu.VMEM((256, channels), F32), pltpu.VMEM((channels, 256), F32)],
        compiler_params=pltpu.CompilerParams(vmem_limit_bytes=VMEM),
        cost_estimate=pl.CostEstimate(flops=2 * 4096 * 1280 * 256, bytes_accessed=14 << 20, transcendentals=0),
    )(lat, chan, gain, shift, dqo, dkv)


def paired(first, second, low, upper):
    if upper:
        return jnp.where(low, pltpu.roll(first.astype(F32), HEAD, 1), second.astype(F32)).astype(BF16)
    return jnp.where(low, first.astype(F32), pltpu.roll(second.astype(F32), HEAD, 1)).astype(BF16)


def mixed_kernel(own_ref, dqo_ref, lat_ref, w_ref, mixed_ref, att_ref):
    half = w_ref.shape[1]
    low = lax.broadcasted_iota(jnp.int32, (128, 128), 1) < HEAD
    for h in range(0, HEADS, 2):
        for i in range(2):
            att_ref[i, :, h * HEAD : (h + 2) * HEAD] = paired(dqo_ref[h, i], dqo_ref[h + 1, i], low, True)
    own = own_ref[0]
    for i in range(2):
        near = att_ref[i, :, pl.ds(pl.multiple_of(own * half, 128), half)]
        far = att_ref[i, :, pl.ds(pl.multiple_of((1 - own) * half, 128), half)]
        total = jnp.dot(near, w_ref[0], preferred_element_type=F32)
        total = total + jnp.dot(far, w_ref[1], preferred_element_type=F32)
        mixed_ref[i] = (lat_ref[i].astype(F32) + total).astype(BF16)


def mix(own, dqo, lat, halves):
    channels = lat.shape[2]

    def whole(*shape):
        return pl.BlockSpec(shape, lambda s, own: (0,) * len(shape))

    return pl.pallas_call(
        mixed_kernel,
        grid_spec=pltpu.PrefetchScalarGridSpec(
            num_scalar_prefetch=1,
            grid=(1,),
            in_specs=[whole(*dqo.shape), whole(*lat.shape), whole(*halves.shape)],
            out_specs=[whole(*lat.shape), whole(2, 128, HEADS * HEAD)],
        ),
        out_shape=[
            jax.ShapeDtypeStruct(lat.shape, BF16),
            jax.ShapeDtypeStruct((2, 128, HEADS * HEAD), BF16),
        ],
        compiler_params=pltpu.CompilerParams(vmem_limit_bytes=VMEM),
        cost_estimate=pl.CostEstimate(flops=2 * 256 * 1280 * 1024, bytes_accessed=6 << 20, transcendentals=0),
    )(own, dqo, lat, halves)


def out_weight_kernel(own_ref, att_ref, att_far_ref, cot_ref, cot_far_ref, out_ref):
    channels = cot_ref.shape[2]
    wide = att_ref.shape[2]
    att = jnp.concatenate([att_ref[...].reshape(256, wide), att_far_ref[...].reshape(256, wide)], axis=0)
    cot = jnp.concatenate([cot_ref[...].reshape(256, channels), cot_far_ref[...].reshape(256, channels)], axis=0)
    total = lax.dot_general(att, cot, (((0,), (0,)), ((), ())), preferred_element_type=F32)
    blocks = total.reshape(wide // 16, 2, 8, channels)
    own = own_ref[0]
    out_ref[...] = jnp.where(own == 0, blocks[:, 0], blocks[:, 1])


def out_weight(own, att, att_far, cot, cot_far):
    channels, wide = cot.shape[2], att.shape[2]
    tile = 256
    side = pl.BlockSpec((2, 128, tile), lambda s, own: (0, 0, s))
    full = pl.BlockSpec(cot.shape, lambda s, own: (0, 0, 0))
    return pl.pallas_call(
        out_weight_kernel,
        grid_spec=pltpu.PrefetchScalarGridSpec(
            num_scalar_prefetch=1,
            grid=(wide // tile,),
            in_specs=[side, side, full, full],
            out_specs=pl.BlockSpec((tile // 16, 8, channels), lambda s, own: (s, 0, 0)),
        ),
        out_shape=jax.ShapeDtypeStruct((wide // 16, 8, channels), F32),
        compiler_params=pltpu.CompilerParams(vmem_limit_bytes=VMEM),
        cost_estimate=pl.CostEstimate(flops=4 * 256 * 1280 * 1024, bytes_accessed=6 << 20, transcendentals=0),
    )(own, att, att_far, cot, cot_far)


def back_kernel(own_ref, dqo_ref, dkv_ref, mine_ref, other_ref, lat_ref, chan_ref, gain_ref, grad_ref, sums_ref, rows_ref):
    own = own_ref[0]
    inner, half = HEADS * HEAD, mine_ref.shape[0]
    low = lax.broadcasted_iota(jnp.int32, (128, 128), 1) < HEAD
    for h in range(0, HEADS, 2):
        for i in range(2):
            rows, at = slice(i * 128, (i + 1) * 128), h * HEAD
            dq, dk = (dqo_ref[h, i], dqo_ref[h + 1, i]), (dkv_ref[h, i], dkv_ref[h + 1, i])
            rows_ref[rows, at : at + 128] = paired(*dq, low, False)
            rows_ref[rows, inner + at : inner + at + 128] = paired(*dk, low, False)
            rows_ref[rows, 2 * inner + at : 2 * inner + at + 128] = paired(*dk, low, True)
    grads = rows_ref[...]
    for side, w_ref in ((own, mine_ref), (1 - own, other_ref)):
        part = lax.dot_general(grads, w_ref[...], (((1,), (1,)), ((), ())), preferred_element_type=F32)
        lanes = pl.ds(pl.multiple_of(side * half, 128), half)
        for i in range(2):
            grad_ref[i, :, lanes] = part[i * 128 : (i + 1) * 128]
    ones, twos = [], []
    for i in range(2):
        grad = grad_ref[i] * gain_ref[...]
        grad_ref[i] = grad
        centred = (lat_ref[i].astype(F32) - chan_ref[i : i + 1]) * chan_ref[2 + i : 3 + i]
        ones.append(jnp.sum(grad, axis=0, keepdims=True))
        twos.append(jnp.sum(grad * centred, axis=0, keepdims=True))
    sums_ref[...] = jnp.broadcast_to(by_group(four_rows(ones + twos), members(lat_ref.shape[2]))[None], sums_ref.shape)


def back(own, dqo, dkv, mine, other, lat, chan, gain, copies):
    def whole(shape):
        return pl.BlockSpec(shape, lambda s, own: (0,) * len(shape), pipeline_mode=pl.Buffered(1))

    operands = (dqo, dkv, mine, other, lat, chan, gain)
    return pl.pallas_call(
        back_kernel,
        grid_spec=pltpu.PrefetchScalarGridSpec(
            num_scalar_prefetch=1,
            grid=(1,),
            in_specs=[whole(a.shape) for a in operands],
            out_specs=[whole(lat.shape), whole((copies, 8, 128))],
            scratch_shapes=[pltpu.VMEM((256, 3 * HEADS * HEAD), BF16)],
        ),
        out_shape=[jax.ShapeDtypeStruct(lat.shape, F32), jax.ShapeDtypeStruct((copies, 8, 128), F32)],
        compiler_params=pltpu.CompilerParams(vmem_limit_bytes=VMEM),
        cost_estimate=pl.CostEstimate(flops=2 * 256 * 1280 * 3072, bytes_accessed=14 << 20, transcendentals=0),
    )(own, *operands)


def final_kernel(count, grad_ref, sums_ref, lat_ref, cot_ref, chan_ref, out_ref):
    table = members(lat_ref.shape[2])
    means = by_channel(jnp.sum(sums_ref[...], axis=0) / count, table)
    for i in range(2):
        inv = chan_ref[2 + i : 3 + i]
        centred = (lat_ref[i].astype(F32) - chan_ref[i : i + 1]) * inv
        grad = inv * (grad_ref[i] - means[i : i + 1] - centred * means[2 + i : 3 + i])
        out_ref[i] = (cot_ref[i].astype(F32) + grad).astype(BF16)


def final(grad, sums, lat, cot, chan, count):
    return pl.pallas_call(
        functools.partial(final_kernel, count),
        out_shape=jax.ShapeDtypeStruct(lat.shape, BF16),
        compiler_params=pltpu.CompilerParams(vmem_limit_bytes=VMEM),
        cost_estimate=pl.CostEstimate(flops=4 << 20, bytes_accessed=4 << 20, transcendentals=0),
    )(grad, sums, lat, cot, chan)


def swapped(value, axis):
    return lax.ppermute(value, axis, [(0, 1), (1, 0)])


def exchanged(value, axes):
    return lax.all_to_all(value, axes, 0, 0, tiled=True)


def shards(latent, cotangent, norm_gain, norm_shift, proj_qkv, proj_out):
    local_len, images, channels = latent.shape
    seq_count = lax.axis_size(SEQ)
    count = local_len * seq_count * (channels // GROUPS)
    own = lax.axis_index("own").reshape(1)
    gain, shift = norm_gain.reshape(1, channels), norm_shift.reshape(1, channels)

    other_out = swapped(proj_out, "own")
    other_qkv = swapped(proj_qkv, "own")
    lat = latent.transpose(1, 0, 2)
    sums = exchanged(stats(lat, seq_count), SEQ)
    cot = cotangent.transpose(1, 0, 2)
    image = lax.axis_index("xl")
    near = jnp.where(image == 0, lat[0], lat[1])
    far = swapped(jnp.where(image == 0, lat[1], lat[0]), "xl")
    pair_lat = jnp.where(image == 0, jnp.stack([near, far]), jnp.stack([far, near]))
    halves_out = jnp.stack([proj_out, other_out])
    cot_far = swapped(cot, "own")
    g = attended_grad(own, cot, halves_out)
    kvqg_send, chan = project(own, lat, sums, gain, shift, g, proj_qkv, other_qkv, count)
    kvqg = exchanged(kvqg_send.reshape(seq_count, 256, 128), SEQ)
    pair_lat, kvqg = lax.optimization_barrier((pair_lat, kvqg))
    image_lat = lax.all_gather(pair_lat, ("y", "z"), tiled=True)

    dqo, dkv = attention(kvqg)

    dqo_tok = exchanged(dqo, SEQ)
    chan_image = jnp.where(image == 0, chan[0:4:2], chan[1:4:2])
    in_part = in_weight(image_lat, chan_image, gain, shift, dqo, dkv)
    dqo_tok, dkv, in_part = lax.optimization_barrier((dqo_tok, dkv, in_part))
    dkv_tok = exchanged(dkv, SEQ)
    dqo_tok = dqo_tok.reshape(HEADS, images, 128, 128)
    mixed, att = mix(own, dqo_tok, lat, halves_out)
    out_part = out_weight(own, att, swapped(att, "own"), cot, cot_far)
    dkv_tok, out_part = lax.optimization_barrier((dkv_tok, out_part))
    out_blocks = exchanged(out_part, LINE)
    dkv_tok = dkv_tok.reshape(HEADS, images, 128, 128)
    grad, back_sums = back(own, dqo_tok, dkv_tok, proj_qkv, other_qkv, lat, chan, gain, seq_count)
    out_blocks, back_sums = lax.optimization_barrier((out_blocks, back_sums))
    back_sums, in_part = lax.optimization_barrier((exchanged(back_sums, SEQ), in_part))
    in_blocks = exchanged(in_part, ALL)
    grad_latent = final(grad, back_sums, lat, cot, chan, count)

    grad_out = jnp.sum(out_blocks, axis=0)
    summed = jnp.sum(in_blocks.reshape(HEADS, 8, 16, 128), axis=1)
    dq = summed[:, 10:15].reshape(HEADS, 5, 2, HEAD).transpose(2, 1, 0, 3).reshape(10, HEADS * HEAD)
    dk = summed[:, :10, :HEAD].transpose(1, 0, 2).reshape(10, HEADS * HEAD)
    dv = summed[:, :10, HEAD:].transpose(1, 0, 2).reshape(10, HEADS * HEAD)
    grad_qkv = jnp.concatenate([dq, dk, dv], axis=1)
    return (mixed.transpose(1, 0, 2), grad_latent.transpose(1, 0, 2), grad_qkv, grad_out)


def solution(mesh):
    fine = Mesh(mesh.devices.reshape(4, 4, 2, 2, 2), ALL)
    tokens = P(SEQ, ("rep", "own"), None)
    return jax.shard_map(
        shards,
        mesh=fine,
        in_specs=(tokens, tokens, P(), P(), P("own", None), P("own", None)),
        out_specs=(tokens, tokens, P(ALL, None), P(ALL, None)),
        check_vma=False,
    )
```

```python
import functools

import jax
import jax.numpy as jnp
from jax import lax
from jax.experimental import pallas as pl
from jax.experimental.pallas import tpu as pltpu
from jax.sharding import Mesh
from jax.sharding import PartitionSpec as P

HEADS = 16
HEAD = 64
GROUPS = 32
SCALE = HEAD ** (-0.5)
SEQ = ("y", "z", "xl")
LINE = ("y", "z", "xl", "rep")
ALL = ("y", "z", "xl", "rep", "own")
F32, BF16 = jnp.float32, jnp.bfloat16
VMEM = 60 << 20


def members(channels):
    channel = lax.broadcasted_iota(jnp.int32, (channels, 128), 0)
    group = lax.broadcasted_iota(jnp.int32, (channels, 128), 1)
    first = group * (channels // GROUPS)
    return ((channel >= first) & (channel < first + channels // GROUPS)).astype(F32)


def by_group(rows, table):
    return lax.dot_general(
        rows, table, (((1,), (0,)), ((), ())),
        precision=lax.Precision.HIGHEST, preferred_element_type=F32,
    )


def by_channel(rows, table):
    return lax.dot_general(
        rows, table, (((1,), (1,)), ((), ())),
        precision=lax.Precision.HIGHEST, preferred_element_type=F32,
    )


def four_rows(rows):
    width = rows[0].shape[1]
    return jnp.concatenate([*rows, jnp.zeros((4, width), F32)], axis=0)


def stats_kernel(lat_ref, out_ref):
    values = [lat_ref[i].astype(F32) for i in range(2)]
    rows = [jnp.sum(v, axis=0, keepdims=True) for v in values]
    rows += [jnp.sum(v * v, axis=0, keepdims=True) for v in values]
    out_ref[...] = jnp.broadcast_to(by_group(four_rows(rows), members(lat_ref.shape[2]))[None], out_ref.shape)


def stats(lat, copies):
    return pl.pallas_call(
        stats_kernel,
        out_shape=jax.ShapeDtypeStruct((copies, 8, 128), F32),
        compiler_params=pltpu.CompilerParams(vmem_limit_bytes=VMEM),
        cost_estimate=pl.CostEstimate(flops=1 << 20, bytes_accessed=lat.size * 2, transcendentals=0),
    )(lat)


def moments(sums, count):
    means = sums / count
    var = means[2:4] - means[0:2] * means[0:2]
    return jnp.concatenate([means[0:2], lax.rsqrt(var + 1e-06), jnp.zeros((4, 128), F32)], axis=0)


def project_kernel(count, own_ref, lat_ref, sums_ref, gain_ref, shift_ref, g_ref, *refs):
    mine, other = refs[0:3], refs[3:6]
    out_ref, chan_ref, normed_ref = refs[6:]
    own = own_ref[0]
    half = mine[0].shape[0]

    @pl.when(pl.program_id(0) == 0)
    def _():
        table = members(lat_ref.shape[2])
        chan = by_channel(moments(jnp.sum(sums_ref[...], axis=0), count), table)
        chan_ref[...] = chan
        for i in range(2):
            centred = (lat_ref[i].astype(F32) - chan[i : i + 1]) * chan[2 + i : 3 + i]
            normed_ref[i * 128 : (i + 1) * 128] = (centred * gain_ref[...] + shift_ref[...]).astype(BF16)

    out_ref[:, :, 192:256] = g_ref[...]
    near = normed_ref[:, pl.ds(pl.multiple_of(own * half, 128), half)]
    far = normed_ref[:, pl.ds(pl.multiple_of((1 - own) * half, 128), half)]
    query, key, value = [
        jnp.dot(near, a[...], preferred_element_type=F32) + jnp.dot(far, b[...], preferred_element_type=F32)
        for a, b in zip(mine, other)
    ]
    low = lax.broadcasted_iota(jnp.int32, (128, 128), 1) < HEAD
    for h in range(0, query.shape[1] // HEAD, 2):
        for i in range(2):
            rows, lanes = slice(i * 128, (i + 1) * 128), slice(h * HEAD, (h + 2) * HEAD)
            q, k, v = query[rows, lanes], key[rows, lanes], value[rows, lanes]
            k_roll, v_roll = pltpu.roll(k, HEAD, 1), pltpu.roll(v, HEAD, 1)
            out_ref[h, i, :128] = jnp.where(low, k, v_roll).astype(BF16)
            out_ref[h + 1, i, :128] = jnp.where(low, k_roll, v).astype(BF16)
            first, second = q[:64], q[64:]
            out_ref[h, i, 128:192] = jnp.where(low[:64], first, pltpu.roll(second, HEAD, 1)).astype(BF16)
            out_ref[h + 1, i, 128:192] = jnp.where(low[:64], pltpu.roll(first, HEAD, 1), second).astype(BF16)


def project(own, lat, sums, gain, shift, g, mine, other, count):
    channels = lat.shape[2]
    cols, half = HEADS * HEAD // 256, mine.shape[0]

    def weight(part):
        return pl.BlockSpec((half, 256), lambda s, own: (0, part * cols + s))

    def whole(*shape):
        return pl.BlockSpec(shape, lambda s, own: (0,) * len(shape))

    return pl.pallas_call(
        functools.partial(project_kernel, count),
        grid_spec=pltpu.PrefetchScalarGridSpec(
            num_scalar_prefetch=1,
            grid=(cols,),
            in_specs=[whole(*lat.shape), whole(*sums.shape), whole(1, channels), whole(1, channels)]
            + [pl.BlockSpec((4, 2, 64, 128), lambda s, own: (s, 0, 0, 0))]
            + [weight(p) for p in range(3)] * 2,
            out_specs=[pl.BlockSpec((4, 2, 256, 128), lambda s, own: (s, 0, 0, 0)), whole(8, channels)],
            scratch_shapes=[pltpu.VMEM((256, channels), BF16)],
        ),
        out_shape=[
            jax.ShapeDtypeStruct((HEADS, 2, 256, 128), BF16),
            jax.ShapeDtypeStruct((8, channels), F32),
        ],
        compiler_params=pltpu.CompilerParams(vmem_limit_bytes=VMEM),
        cost_estimate=pl.CostEstimate(flops=2 * 256 * 1280 * 3072, bytes_accessed=12 << 20, transcendentals=0),
    )(own, lat, sums, gain, shift, g, mine, mine, mine, other, other, other)


def attended_grad_kernel(own_ref, cot_ref, w_ref, out_ref):
    rows = cot_ref[...].reshape(256, cot_ref.shape[2])
    grad = lax.dot_general(rows, w_ref[...], (((1,), (1,)), ((), ())), preferred_element_type=F32)
    low = lax.broadcasted_iota(jnp.int32, (64, 128), 1) < HEAD
    for h in range(0, grad.shape[1] // HEAD, 2):
        for i in range(2):
            first = grad[i * 128 : i * 128 + 64, h * HEAD : (h + 2) * HEAD]
            second = grad[i * 128 + 64 : (i + 1) * 128, h * HEAD : (h + 2) * HEAD]
            out_ref[h, i] = jnp.where(low, first, pltpu.roll(second, HEAD, 1)).astype(BF16)
            out_ref[h + 1, i] = jnp.where(low, pltpu.roll(first, HEAD, 1), second).astype(BF16)


def attended_grad(own, cot, halves):
    channels = cot.shape[2]
    per = halves.shape[1] // 256

    return pl.pallas_call(
        attended_grad_kernel,
        grid_spec=pltpu.PrefetchScalarGridSpec(
            num_scalar_prefetch=1,
            grid=(2 * per,),
            in_specs=[
                pl.BlockSpec(cot.shape, lambda s, own: (0, 0, 0)),
                pl.BlockSpec((None, 256, channels), lambda s, own: (s // per, s % per, 0)),
            ],
            out_specs=pl.BlockSpec(
                (4, 2, 64, 128),
                lambda s, own: ((s // per + own[0] - 2 * own[0] * (s // per)) * per + s % per, 0, 0, 0),
            ),
        ),
        out_shape=jax.ShapeDtypeStruct((HEADS, 2, 64, 128), BF16),
        compiler_params=pltpu.CompilerParams(vmem_limit_bytes=VMEM),
        cost_estimate=pl.CostEstimate(flops=2 * 256 * 1280 * 1024, bytes_accessed=4 << 20, transcendentals=0),
    )(own, cot, halves)


def attention_kernel(ck, kvq_ref, dqo_ref, dkv_ref, s_ref, x_ref, y_ref, acc_ref):
    step, last = pl.program_id(0), pl.num_programs(0) - 1
    sources, _, width = kvq_ref.shape
    keys = sources * 128
    here = dqo_ref.shape[0]
    rows = here * 128
    half = rows // 2

    @pl.when(step == 0)
    def _():
        acc_ref[...] = jnp.zeros_like(acc_ref)

    low = lax.broadcasted_iota(jnp.int32, (half, width), 1) < HEAD
    xq = kvq_ref[pl.ds(step * here, here), 128:192, :].reshape(half, width).astype(F32) * SCALE
    xg = kvq_ref[pl.ds(step * here, here), 192:256, :].reshape(half, width).astype(F32)
    zero = jnp.zeros_like(xq)
    y_ref[0 * half : 1 * half] = jnp.where(low, xq, zero).astype(BF16)
    y_ref[1 * half : 2 * half] = jnp.where(low, pltpu.roll(xq, HEAD, 1), zero).astype(BF16)
    y_ref[2 * half : 3 * half] = jnp.where(low, zero, pltpu.roll(xg, HEAD, 1)).astype(BF16)
    y_ref[3 * half : 4 * half] = jnp.where(low, zero, xg).astype(BF16)
    y = y_ref[...]
    spans = [(c, c + ck) for c in range(0, keys, ck)]

    def kv_chunk(a, b):
        return kvq_ref[a // 128 : b // 128, :128, :].reshape(b - a, width)

    top = None
    for a, b in spans:
        both = lax.dot_general(y, kv_chunk(a, b), (((1,), (1,)), ((), ())), preferred_element_type=F32)
        s_ref[:, a:b] = both
        for t in range(0, ck, 128):
            piece = both[:rows, t : t + 128]
            top = piece if top is None else jnp.maximum(top, piece)
    top = jnp.max(top, axis=1, keepdims=True)
    total = jnp.zeros((rows, 128), F32)
    delta = jnp.zeros((rows, 128), F32)
    for a, b in spans:
        weights = jnp.exp(s_ref[:rows, a:b] - top)
        s_ref[:rows, a:b] = weights
        fold = weights * s_ref[rows:, a:b]
        for t in range(0, ck, 128):
            total = total + weights[:, t : t + 128]
            delta = delta + fold[:, t : t + 128]
    inverse = 1.0 / jnp.sum(total, axis=1, keepdims=True)
    delta = jnp.sum(delta, axis=1, keepdims=True) * inverse
    out = jnp.zeros((2 * rows, width), F32)
    for a, b in spans:
        probs = s_ref[:rows, a:b] * inverse
        x_ref[rows:, a:b] = probs.astype(BF16)
        x_ref[:rows, a:b] = (probs * (s_ref[rows:, a:b] - delta)).astype(BF16)
        x = x_ref[:, a:b]
        out = out + jnp.dot(x, kv_chunk(a, b), preferred_element_type=F32)
        acc_ref[a:b, :] += lax.dot_general(x, y, (((0,), (0,)), ((), ())), preferred_element_type=F32)
    lows = lax.broadcasted_iota(jnp.int32, (rows, width), 1) < HEAD
    res = jnp.where(lows, out[:rows] * SCALE, out[rows:]).astype(BF16)
    for h in range(2):
        for a in range(here):
            at = h * half + a * 64
            dqo_ref[a, h * 64 : (h + 1) * 64, :] = res[at : at + 64]

    @pl.when(step == last)
    def _():
        dkv_ref[...] = acc_ref[...].reshape(sources, 128, width).astype(BF16)


def attention(kvq, here=2, ck=1024):
    sources = kvq.shape[0]
    keys, rows = sources * 128, here * 128
    return pl.pallas_call(
        functools.partial(attention_kernel, ck),
        grid=(sources // here,),
        in_specs=[
            pl.BlockSpec((sources, 256, 128), lambda i: (0, 0, 0), pipeline_mode=pl.Buffered(1)),
        ],
        out_specs=[
            pl.BlockSpec((here, 128, 128), lambda i: (i, 0, 0)),
            pl.BlockSpec((sources, 128, 128), lambda i: (0, 0, 0)),
        ],
        out_shape=[
            jax.ShapeDtypeStruct((sources, 128, 128), BF16),
            jax.ShapeDtypeStruct((sources, 128, 128), BF16),
        ],
        scratch_shapes=[
            pltpu.VMEM((2 * rows, keys), F32),
            pltpu.VMEM((2 * rows, keys), BF16),
            pltpu.VMEM((2 * rows, 128), BF16),
            pltpu.VMEM((keys, 128), F32),
        ],
        compiler_params=pltpu.CompilerParams(vmem_limit_bytes=VMEM),
        cost_estimate=pl.CostEstimate(flops=48 * keys * keys * HEAD, bytes_accessed=4 << 20, transcendentals=keys * keys),
    )(kvq)


def in_weight_kernel(lat_ref, chan_ref, gain_ref, shift_ref, dqo_ref, dkv_ref, out_ref, acc_ref, turned_ref):
    step, last = pl.program_id(0), pl.num_programs(0) - 1
    sources, _, channels = lat_ref.shape
    rows = sources * 128

    @pl.when(step == 0)
    def _():
        acc_ref[...] = jnp.zeros_like(acc_ref)

    lat = lat_ref[...].reshape(rows, channels).astype(F32)
    centred = (lat - chan_ref[0:1]) * chan_ref[1:2]
    normed = (centred * gain_ref[...] + shift_ref[...]).astype(BF16)
    grads = jnp.concatenate(
        [dqo_ref[...].reshape(rows, 128), dkv_ref[...].reshape(rows, 128)], axis=1
    )
    acc_ref[...] += lax.dot_general(grads, normed, (((0,), (0,)), ((), ())), preferred_element_type=F32)

    @pl.when(step == last)
    def _():
        turned_ref[...] = acc_ref[...].T
        low = lax.broadcasted_iota(jnp.int32, (5, 128), 1) < HEAD
        for d in range(channels // 10):
            at = d * 10
            out_ref[d, 0:10] = turned_ref[at : at + 10, 128:256]
            first, second = turned_ref[at : at + 5, 0:128], turned_ref[at + 5 : at + 10, 0:128]
            out_ref[d, 10:15] = jnp.where(low, first, pltpu.roll(second, HEAD, 1))
            out_ref[d, 15:16] = jnp.zeros((1, 128), F32)


def in_weight(lat, chan, gain, shift, dqo, dkv, here=4):
    sources, _, channels = lat.shape
    return pl.pallas_call(
        in_weight_kernel,
        grid=(sources // here,),
        in_specs=[
            pl.BlockSpec((here, 128, channels), lambda i: (i, 0, 0)),
            pl.BlockSpec((2, channels), lambda i: (0, 0)),
            pl.BlockSpec((1, channels), lambda i: (0, 0)),
            pl.BlockSpec((1, channels), lambda i: (0, 0)),
            pl.BlockSpec((here, 128, 128), lambda i: (i, 0, 0)),
            pl.BlockSpec((here, 128, 128), lambda i: (i, 0, 0)),
        ],
        out_specs=pl.BlockSpec((channels // 10, 16, 128), lambda i: (0, 0, 0)),
        out_shape=jax.ShapeDtypeStruct((channels // 10, 16, 128), F32),
        scratch_shapes=[pltpu.VMEM((256, channels), F32), pltpu.VMEM((channels, 256), F32)],
        compiler_params=pltpu.CompilerParams(vmem_limit_bytes=VMEM),
        cost_estimate=pl.CostEstimate(flops=2 * 4096 * 1280 * 256, bytes_accessed=14 << 20, transcendentals=0),
    )(lat, chan, gain, shift, dqo, dkv)


def paired(first, second, low, upper):
    if upper:
        return jnp.where(low, pltpu.roll(first.astype(F32), HEAD, 1), second.astype(F32)).astype(BF16)
    return jnp.where(low, first.astype(F32), pltpu.roll(second.astype(F32), HEAD, 1)).astype(BF16)


def mixed_kernel(own_ref, dqo_ref, lat_ref, w_ref, mixed_ref, att_ref):
    half = w_ref.shape[1]
    low = lax.broadcasted_iota(jnp.int32, (128, 128), 1) < HEAD
    for h in range(0, HEADS, 2):
        for i in range(2):
            att_ref[i, :, h * HEAD : (h + 2) * HEAD] = paired(dqo_ref[h, i], dqo_ref[h + 1, i], low, True)
    own = own_ref[0]
    for i in range(2):
        near = att_ref[i, :, pl.ds(pl.multiple_of(own * half, 128), half)]
        far = att_ref[i, :, pl.ds(pl.multiple_of((1 - own) * half, 128), half)]
        total = jnp.dot(near, w_ref[0], preferred_element_type=F32)
        total = total + jnp.dot(far, w_ref[1], preferred_element_type=F32)
        mixed_ref[i] = (lat_ref[i].astype(F32) + total).astype(BF16)


def mix(own, dqo, lat, halves):
    channels = lat.shape[2]

    def whole(*shape):
        return pl.BlockSpec(shape, lambda s, own: (0,) * len(shape))

    return pl.pallas_call(
        mixed_kernel,
        grid_spec=pltpu.PrefetchScalarGridSpec(
            num_scalar_prefetch=1,
            grid=(1,),
            in_specs=[whole(*dqo.shape), whole(*lat.shape), whole(*halves.shape)],
            out_specs=[whole(*lat.shape), whole(2, 128, HEADS * HEAD)],
        ),
        out_shape=[
            jax.ShapeDtypeStruct(lat.shape, BF16),
            jax.ShapeDtypeStruct((2, 128, HEADS * HEAD), BF16),
        ],
        compiler_params=pltpu.CompilerParams(vmem_limit_bytes=VMEM),
        cost_estimate=pl.CostEstimate(flops=2 * 256 * 1280 * 1024, bytes_accessed=6 << 20, transcendentals=0),
    )(own, dqo, lat, halves)


def out_weight_kernel(own_ref, att_ref, att_far_ref, cot_ref, cot_far_ref, out_ref):
    channels = cot_ref.shape[2]
    wide = att_ref.shape[2]
    att = jnp.concatenate([att_ref[...].reshape(256, wide), att_far_ref[...].reshape(256, wide)], axis=0)
    cot = jnp.concatenate([cot_ref[...].reshape(256, channels), cot_far_ref[...].reshape(256, channels)], axis=0)
    total = lax.dot_general(att, cot, (((0,), (0,)), ((), ())), preferred_element_type=F32)
    blocks = total.reshape(wide // 16, 2, 8, channels)
    own = own_ref[0]
    out_ref[...] = jnp.where(own == 0, blocks[:, 0], blocks[:, 1])


def out_weight(own, att, att_far, cot, cot_far):
    channels, wide = cot.shape[2], att.shape[2]
    tile = 256
    side = pl.BlockSpec((2, 128, tile), lambda s, own: (0, 0, s))
    full = pl.BlockSpec(cot.shape, lambda s, own: (0, 0, 0))
    return pl.pallas_call(
        out_weight_kernel,
        grid_spec=pltpu.PrefetchScalarGridSpec(
            num_scalar_prefetch=1,
            grid=(wide // tile,),
            in_specs=[side, side, full, full],
            out_specs=pl.BlockSpec((tile // 16, 8, channels), lambda s, own: (s, 0, 0)),
        ),
        out_shape=jax.ShapeDtypeStruct((wide // 16, 8, channels), F32),
        compiler_params=pltpu.CompilerParams(vmem_limit_bytes=VMEM),
        cost_estimate=pl.CostEstimate(flops=4 * 256 * 1280 * 1024, bytes_accessed=6 << 20, transcendentals=0),
    )(own, att, att_far, cot, cot_far)


def place():
    return tuple(lax.axis_index(axis) for axis in ALL)


def shifted(here, k, sign):
    dy, dz, dx, dr = k // 16, (k // 4) % 4, (k // 2) % 2, k % 2
    y = (here[0] + (dy if sign > 0 else 4 - dy)) % 4
    z = (here[1] + (dz if sign > 0 else 4 - dz)) % 4
    x = (here[2] + dx) % 2
    r = (here[3] + dr) % 2
    return {"y": y, "z": z, "xl": x, "rep": r}, ((y * 4 + z) * 2 + x) * 2 + r


def tail_kernel(
    count, part_ref, dqo_ref, dkv_ref, mine_ref, other_ref, lat_ref, cot_ref, chan_ref, gain_ref,
    out_ref, weight_ref, rows_ref, grad_ref, near_ref, far_ref, got_ref,
    part_send, part_recv, sums_send, sums_recv,
):
    here = place()
    own = here[4]
    lines, seqs = part_ref.shape[0], far_ref.shape[0]
    block = ((here[0] * 4 + here[1]) * 2 + here[2]) * 2 + here[3]
    line = block // 2

    barrier = pltpu.get_barrier_semaphore()

    @pl.loop(1, lines)
    def _(k):
        pl.semaphore_signal(barrier, inc=1, device_id=shifted(here, k, 1)[0], device_id_type=pl.DeviceIdType.MESH)

    pl.semaphore_wait(barrier, lines - 1)

    def part_copy(k):
        target, there = shifted(here, k, 1)
        return pltpu.make_async_remote_copy(
            src_ref=part_ref.at[there], dst_ref=got_ref.at[block],
            send_sem=part_send.at[k], recv_sem=part_recv.at[k],
            device_id=target, device_id_type=pl.DeviceIdType.MESH,
        )

    def part_arrival(k):
        source, there = shifted(here, k, -1)
        return pltpu.make_async_remote_copy(
            src_ref=part_ref.at[there], dst_ref=got_ref.at[there],
            send_sem=part_send.at[k], recv_sem=part_recv.at[k],
            device_id=source, device_id_type=pl.DeviceIdType.MESH,
        )

    def sums_copy(k):
        target, _ = shifted(here, 2 * k, 1)
        return pltpu.make_async_remote_copy(
            src_ref=near_ref, dst_ref=far_ref.at[line],
            send_sem=sums_send.at[k], recv_sem=sums_recv.at[k],
            device_id=target, device_id_type=pl.DeviceIdType.MESH,
        )

    def sums_arrival(k):
        source, there = shifted(here, 2 * k, -1)
        return pltpu.make_async_remote_copy(
            src_ref=near_ref, dst_ref=far_ref.at[there // 2],
            send_sem=sums_send.at[k], recv_sem=sums_recv.at[k],
            device_id=source, device_id_type=pl.DeviceIdType.MESH,
        )

    @pl.loop(1, lines)
    def _(k):
        part_copy(k).start()

    inner, half = HEADS * HEAD, mine_ref.shape[0]
    low = lax.broadcasted_iota(jnp.int32, (128, 128), 1) < HEAD
    for h in range(0, HEADS, 2):
        for i in range(2):
            rows, at = slice(i * 128, (i + 1) * 128), h * HEAD
            dq, dk = (dqo_ref[h, i], dqo_ref[h + 1, i]), (dkv_ref[h, i], dkv_ref[h + 1, i])
            rows_ref[rows, at : at + 128] = paired(*dq, low, False)
            rows_ref[rows, inner + at : inner + at + 128] = paired(*dk, low, False)
            rows_ref[rows, 2 * inner + at : 2 * inner + at + 128] = paired(*dk, low, True)
    grads = rows_ref[...]
    for side, w_ref in ((own, mine_ref), (1 - own, other_ref)):
        part = lax.dot_general(grads, w_ref[...], (((1,), (1,)), ((), ())), preferred_element_type=F32)
        lanes = pl.ds(pl.multiple_of(side * half, 128), half)
        for i in range(2):
            grad_ref[i, :, lanes] = part[i * 128 : (i + 1) * 128]
    ones, twos = [], []
    for i in range(2):
        grad = grad_ref[i] * gain_ref[...]
        grad_ref[i] = grad
        centred = (lat_ref[i].astype(F32) - chan_ref[i : i + 1]) * chan_ref[2 + i : 3 + i]
        ones.append(jnp.sum(grad, axis=0, keepdims=True))
        twos.append(jnp.sum(grad * centred, axis=0, keepdims=True))
    table = members(lat_ref.shape[2])
    sums = by_group(four_rows(ones + twos), table)
    near_ref[...] = sums
    far_ref[line] = sums

    @pl.loop(1, seqs)
    def _(k):
        sums_copy(k).start()

    got_ref[block] = part_ref[block]

    @pl.loop(1, seqs)
    def _(k):
        sums_arrival(k).wait_recv()

    means = by_channel(jnp.sum(far_ref[...], axis=0) / count, table)
    for i in range(2):
        inv = chan_ref[2 + i : 3 + i]
        centred = (lat_ref[i].astype(F32) - chan_ref[i : i + 1]) * inv
        grad = inv * (grad_ref[i] - means[i : i + 1] - centred * means[2 + i : 3 + i])
        out_ref[i] = (cot_ref[i].astype(F32) + grad).astype(BF16)

    @pl.loop(1, lines)
    def _(k):
        part_arrival(k).wait_recv()

    weight_ref[...] = jnp.sum(got_ref[...], axis=0)

    @pl.loop(1, lines)
    def _(k):
        part_copy(k).wait_send()

    @pl.loop(1, seqs)
    def _(k):
        sums_copy(k).wait_send()


def tail(part, dqo, dkv, mine, other, lat, cot, chan, gain, count):
    lines, channels = part.shape[0], part.shape[2]
    dma = pltpu.SemaphoreType.DMA
    return pl.pallas_call(
        functools.partial(tail_kernel, count),
        out_shape=[jax.ShapeDtypeStruct(lat.shape, BF16), jax.ShapeDtypeStruct((8, channels), F32)],
        scratch_shapes=[
            pltpu.VMEM((256, 3 * HEADS * HEAD), BF16),
            pltpu.VMEM(lat.shape, F32),
            pltpu.VMEM((8, 128), F32),
            pltpu.VMEM((lines // 2, 8, 128), F32),
            pltpu.VMEM(part.shape, F32),
            dma((lines,)), dma((lines,)), dma((lines // 2,)), dma((lines // 2,)),
        ],
        compiler_params=pltpu.CompilerParams(vmem_limit_bytes=VMEM, collective_id=1, has_side_effects=True),
        cost_estimate=pl.CostEstimate(flops=2 << 34, bytes_accessed=16 << 20, transcendentals=0),
    )(part, dqo, dkv, mine, other, lat, cot, chan, gain)


def swapped(value, axis):
    return lax.ppermute(value, axis, [(0, 1), (1, 0)])


def exchanged(value, axes):
    return lax.all_to_all(value, axes, 0, 0, tiled=True)


def shards(latent, cotangent, norm_gain, norm_shift, proj_qkv, proj_out):
    local_len, images, channels = latent.shape
    seq_count = lax.axis_size(SEQ)
    count = local_len * seq_count * (channels // GROUPS)
    own = lax.axis_index("own").reshape(1)
    gain, shift = norm_gain.reshape(1, channels), norm_shift.reshape(1, channels)

    other_out = swapped(proj_out, "own")
    other_qkv = swapped(proj_qkv, "own")
    lat = latent.transpose(1, 0, 2)
    sums = exchanged(stats(lat, seq_count), SEQ)
    cot = cotangent.transpose(1, 0, 2)
    image = lax.axis_index("xl")
    near = jnp.where(image == 0, lat[0], lat[1])
    far = swapped(jnp.where(image == 0, lat[1], lat[0]), "xl")
    pair_lat = jnp.where(image == 0, jnp.stack([near, far]), jnp.stack([far, near]))
    halves_out = jnp.stack([proj_out, other_out])
    cot_far = swapped(cot, "own")
    g = attended_grad(own, cot, halves_out)
    kvqg_send, chan = project(own, lat, sums, gain, shift, g, proj_qkv, other_qkv, count)
    kvqg = exchanged(kvqg_send.reshape(seq_count, 256, 128), SEQ)
    pair_lat, kvqg = lax.optimization_barrier((pair_lat, kvqg))
    image_lat = lax.all_gather(pair_lat, ("y", "z"), tiled=True)

    dqo, dkv = attention(kvqg)

    dqo_tok = exchanged(dqo, SEQ)
    chan_image = jnp.where(image == 0, chan[0:4:2], chan[1:4:2])
    in_part = in_weight(image_lat, chan_image, gain, shift, dqo, dkv)
    dqo_tok, dkv, in_part = lax.optimization_barrier((dqo_tok, dkv, in_part))
    dkv_tok = exchanged(dkv, SEQ)
    dqo_tok = dqo_tok.reshape(HEADS, images, 128, 128)
    mixed, att = mix(own, dqo_tok, lat, halves_out)
    out_part = out_weight(own, att, swapped(att, "own"), cot, cot_far)
    dkv_tok, out_part, in_part = lax.optimization_barrier((dkv_tok, out_part, in_part))
    in_blocks = exchanged(in_part, ALL)
    dkv_tok = dkv_tok.reshape(HEADS, images, 128, 128)
    grad_latent, grad_out = tail(
        out_part, dqo_tok, dkv_tok, proj_qkv, other_qkv, lat, cot, chan, gain, count
    )

    summed = jnp.sum(in_blocks.reshape(HEADS, 8, 16, 128), axis=1)
    dq = summed[:, 10:15].reshape(HEADS, 5, 2, HEAD).transpose(2, 1, 0, 3).reshape(10, HEADS * HEAD)
    dk = summed[:, :10, :HEAD].transpose(1, 0, 2).reshape(10, HEADS * HEAD)
    dv = summed[:, :10, HEAD:].transpose(1, 0, 2).reshape(10, HEADS * HEAD)
    grad_qkv = jnp.concatenate([dq, dk, dv], axis=1)
    return (mixed.transpose(1, 0, 2), grad_latent.transpose(1, 0, 2), grad_qkv, grad_out)


def solution(mesh):
    fine = Mesh(mesh.devices.reshape(4, 4, 2, 2, 2), ALL)
    tokens = P(SEQ, ("rep", "own"), None)
    return jax.shard_map(
        shards,
        mesh=fine,
        in_specs=(tokens, tokens, P(), P(), P("own", None), P("own", None)),
        out_specs=(tokens, tokens, P(ALL, None), P(ALL, None)),
        check_vma=False,
    )
```

```python
import functools

import jax
import jax.numpy as jnp
from jax import lax
from jax.experimental import pallas as pl
from jax.experimental.pallas import tpu as pltpu
from jax.sharding import Mesh
from jax.sharding import PartitionSpec as P

HEADS = 16
HEAD = 64
GROUPS = 32
SCALE = HEAD ** (-0.5)
SEQ = ("y", "z", "xl")
LINE = ("y", "z", "xl", "rep")
ALL = ("y", "z", "xl", "rep", "own")
F32, BF16 = jnp.float32, jnp.bfloat16
VMEM = 60 << 20


def members(channels):
    channel = lax.broadcasted_iota(jnp.int32, (channels, 128), 0)
    group = lax.broadcasted_iota(jnp.int32, (channels, 128), 1)
    first = group * (channels // GROUPS)
    return ((channel >= first) & (channel < first + channels // GROUPS)).astype(F32)


def by_group(rows, table):
    return lax.dot_general(
        rows, table, (((1,), (0,)), ((), ())),
        precision=lax.Precision.HIGHEST, preferred_element_type=F32,
    )


def by_channel(rows, table):
    return lax.dot_general(
        rows, table, (((1,), (1,)), ((), ())),
        precision=lax.Precision.HIGHEST, preferred_element_type=F32,
    )


def four_rows(rows):
    width = rows[0].shape[1]
    return jnp.concatenate([*rows, jnp.zeros((4, width), F32)], axis=0)


def stats_kernel(lat_ref, out_ref):
    values = [lat_ref[i].astype(F32) for i in range(2)]
    rows = [jnp.sum(v, axis=0, keepdims=True) for v in values]
    rows += [jnp.sum(v * v, axis=0, keepdims=True) for v in values]
    out_ref[...] = jnp.broadcast_to(by_group(four_rows(rows), members(lat_ref.shape[2]))[None], out_ref.shape)


def stats(lat, copies):
    return pl.pallas_call(
        stats_kernel,
        out_shape=jax.ShapeDtypeStruct((copies, 8, 128), F32),
        compiler_params=pltpu.CompilerParams(vmem_limit_bytes=VMEM),
        cost_estimate=pl.CostEstimate(flops=1 << 20, bytes_accessed=lat.size * 2, transcendentals=0),
    )(lat)


def moments(sums, count):
    means = sums / count
    var = means[2:4] - means[0:2] * means[0:2]
    return jnp.concatenate([means[0:2], lax.rsqrt(var + 1e-06), jnp.zeros((4, 128), F32)], axis=0)


def project_kernel(
    count, lat_ref, sums_ref, gain_ref, shift_ref, g_ref, mine_ref, other_ref,
    chan_ref, out_ref, normed_ref, send_ref, send_sem, recv_sem, keep_sem,
):
    here = place()
    own = here[4]
    half = mine_ref.shape[0]
    inner = HEADS * HEAD
    line = (here[0] * 4 + here[1]) * 2 + here[2]
    seqs = out_ref.shape[0]

    def device(at):
        return {"y": at // 8, "z": (at // 2) % 4, "xl": at % 2}

    barrier = pltpu.get_barrier_semaphore()

    @pl.loop(1, seqs)
    def _(k):
        to = lax.rem(line + k, seqs)
        pl.semaphore_signal(barrier, inc=1, device_id=device(to), device_id_type=pl.DeviceIdType.MESH)

    table = members(lat_ref.shape[2])
    chan = by_channel(moments(jnp.sum(sums_ref[...], axis=0), count), table)
    chan_ref[...] = chan
    for i in range(2):
        centred = (lat_ref[i].astype(F32) - chan[i : i + 1]) * chan[2 + i : 3 + i]
        normed_ref[i * 128 : (i + 1) * 128] = (centred * gain_ref[...] + shift_ref[...]).astype(BF16)
    near = normed_ref[:, pl.ds(pl.multiple_of(own * half, 128), half)]
    far = normed_ref[:, pl.ds(pl.multiple_of((1 - own) * half, 128), half)]
    low = lax.broadcasted_iota(jnp.int32, (128, 128), 1) < HEAD

    def copy(row, column):
        at = row * 8 + column
        return pltpu.make_async_remote_copy(
            src_ref=send_ref.at[at], dst_ref=out_ref.at[line],
            send_sem=send_sem.at[at], recv_sem=recv_sem.at[line],
            device_id=device(at), device_id_type=pl.DeviceIdType.MESH,
        )

    def arrival(at):
        return pltpu.make_async_remote_copy(
            src_ref=send_ref.at[at], dst_ref=out_ref.at[at],
            send_sem=send_sem.at[at], recv_sem=recv_sem.at[at],
            device_id=device(at), device_id_type=pl.DeviceIdType.MESH,
        )

    def block_row(row):
        lanes = [pl.ds(pl.multiple_of(p * inner + row * 256, 256), 256) for p in range(3)]
        query, key, value = [
            jnp.dot(near, mine_ref[:, at], preferred_element_type=F32)
            + jnp.dot(far, other_ref[:, at], preferred_element_type=F32)
            for at in lanes
        ]
        for h in range(0, 4, 2):
            for i in range(2):
                rows, part = slice(i * 128, (i + 1) * 128), slice(h * HEAD, (h + 2) * HEAD)
                q, k, v = query[rows, part], key[rows, part], value[rows, part]
                k_roll, v_roll = pltpu.roll(k, HEAD, 1), pltpu.roll(v, HEAD, 1)
                first, second = q[:64], q[64:]
                one, two = row * 8 + h * 2 + i, row * 8 + (h + 1) * 2 + i
                send_ref[one, :128] = jnp.where(low, k, v_roll).astype(BF16)
                send_ref[two, :128] = jnp.where(low, k_roll, v).astype(BF16)
                send_ref[one, 128:192] = jnp.where(low[:64], first, pltpu.roll(second, HEAD, 1)).astype(BF16)
                send_ref[two, 128:192] = jnp.where(low[:64], pltpu.roll(first, HEAD, 1), second).astype(BF16)
                send_ref[one, 192:256] = g_ref[row * 4 + h, i]
                send_ref[two, 192:256] = g_ref[row * 4 + h + 1, i]

    pl.semaphore_wait(barrier, seqs - 1)
    for j in range(4):
        row = (here[0] + (j + 1)) % 4
        block_row(row)
        if j < 3:
            @pl.loop(0, 8)
            def _(k):
                copy(row, (here[1] * 2 + here[2] + k) % 8).start()
        else:
            @pl.loop(1, 8)
            def _(k):
                copy(row, (here[1] * 2 + here[2] + k) % 8).start()

    keep = pltpu.make_async_copy(send_ref.at[line], out_ref.at[line], keep_sem)
    keep.start()

    @pl.loop(1, seqs)
    def _(k):
        arrival(lax.rem(line + k, seqs)).wait()

    keep.wait()


def project(lat, sums, gain, shift, g, mine, other, count):
    channels = lat.shape[2]
    seqs = sums.shape[0]
    dma = pltpu.SemaphoreType.DMA
    whole = pl.BlockSpec(memory_space=pltpu.VMEM)
    return pl.pallas_call(
        functools.partial(project_kernel, count),
        in_specs=[whole] * 7,
        out_specs=[whole, pl.BlockSpec(memory_space=pl.ANY)],
        out_shape=[
            jax.ShapeDtypeStruct((8, channels), F32),
            jax.ShapeDtypeStruct((seqs, 256, 128), BF16),
        ],
        scratch_shapes=[
            pltpu.VMEM((256, channels), BF16),
            pltpu.VMEM((seqs, 256, 128), BF16),
            dma((seqs,)), dma((seqs,)), dma,
        ],
        compiler_params=pltpu.CompilerParams(vmem_limit_bytes=VMEM, collective_id=2, has_side_effects=True),
        cost_estimate=pl.CostEstimate(flops=2 << 34, bytes_accessed=12 << 20, transcendentals=0),
    )(lat, sums, gain, shift, g, mine, other)


def attended_grad_kernel(own_ref, cot_ref, w_ref, out_ref):
    rows = cot_ref[...].reshape(256, cot_ref.shape[2])
    grad = lax.dot_general(rows, w_ref[...], (((1,), (1,)), ((), ())), preferred_element_type=F32)
    low = lax.broadcasted_iota(jnp.int32, (64, 128), 1) < HEAD
    for h in range(0, grad.shape[1] // HEAD, 2):
        for i in range(2):
            first = grad[i * 128 : i * 128 + 64, h * HEAD : (h + 2) * HEAD]
            second = grad[i * 128 + 64 : (i + 1) * 128, h * HEAD : (h + 2) * HEAD]
            out_ref[h, i] = jnp.where(low, first, pltpu.roll(second, HEAD, 1)).astype(BF16)
            out_ref[h + 1, i] = jnp.where(low, pltpu.roll(first, HEAD, 1), second).astype(BF16)


def attended_grad(own, cot, halves):
    channels = cot.shape[2]
    per = halves.shape[1] // 256

    return pl.pallas_call(
        attended_grad_kernel,
        grid_spec=pltpu.PrefetchScalarGridSpec(
            num_scalar_prefetch=1,
            grid=(2 * per,),
            in_specs=[
                pl.BlockSpec(cot.shape, lambda s, own: (0, 0, 0)),
                pl.BlockSpec((None, 256, channels), lambda s, own: (s // per, s % per, 0)),
            ],
            out_specs=pl.BlockSpec(
                (4, 2, 64, 128),
                lambda s, own: ((s // per + own[0] - 2 * own[0] * (s // per)) * per + s % per, 0, 0, 0),
            ),
        ),
        out_shape=jax.ShapeDtypeStruct((HEADS, 2, 64, 128), BF16),
        compiler_params=pltpu.CompilerParams(vmem_limit_bytes=VMEM),
        cost_estimate=pl.CostEstimate(flops=2 * 256 * 1280 * 1024, bytes_accessed=4 << 20, transcendentals=0),
    )(own, cot, halves)


def attention_kernel(ck, kvq_ref, dqo_ref, dkv_ref, s_ref, x_ref, y_ref, acc_ref):
    step, last = pl.program_id(0), pl.num_programs(0) - 1
    sources, _, width = kvq_ref.shape
    keys = sources * 128
    here = dqo_ref.shape[0]
    rows = here * 128
    half = rows // 2

    @pl.when(step == 0)
    def _():
        acc_ref[...] = jnp.zeros_like(acc_ref)

    low = lax.broadcasted_iota(jnp.int32, (half, width), 1) < HEAD
    xq = kvq_ref[pl.ds(step * here, here), 128:192, :].reshape(half, width).astype(F32) * SCALE
    xg = kvq_ref[pl.ds(step * here, here), 192:256, :].reshape(half, width).astype(F32)
    zero = jnp.zeros_like(xq)
    y_ref[0 * half : 1 * half] = jnp.where(low, xq, zero).astype(BF16)
    y_ref[1 * half : 2 * half] = jnp.where(low, pltpu.roll(xq, HEAD, 1), zero).astype(BF16)
    y_ref[2 * half : 3 * half] = jnp.where(low, zero, pltpu.roll(xg, HEAD, 1)).astype(BF16)
    y_ref[3 * half : 4 * half] = jnp.where(low, zero, xg).astype(BF16)
    y = y_ref[...]
    spans = [(c, c + ck) for c in range(0, keys, ck)]

    def kv_chunk(a, b):
        return kvq_ref[a // 128 : b // 128, :128, :].reshape(b - a, width)

    top = None
    for a, b in spans:
        both = lax.dot_general(y, kv_chunk(a, b), (((1,), (1,)), ((), ())), preferred_element_type=F32)
        s_ref[:, a:b] = both
        for t in range(0, ck, 128):
            piece = both[:rows, t : t + 128]
            top = piece if top is None else jnp.maximum(top, piece)
    top = jnp.max(top, axis=1, keepdims=True)
    total = jnp.zeros((rows, 128), F32)
    delta = jnp.zeros((rows, 128), F32)
    for a, b in spans:
        weights = jnp.exp(s_ref[:rows, a:b] - top)
        s_ref[:rows, a:b] = weights
        fold = weights * s_ref[rows:, a:b]
        for t in range(0, ck, 128):
            total = total + weights[:, t : t + 128]
            delta = delta + fold[:, t : t + 128]
    inverse = 1.0 / jnp.sum(total, axis=1, keepdims=True)
    delta = jnp.sum(delta, axis=1, keepdims=True) * inverse
    out = jnp.zeros((2 * rows, width), F32)
    for a, b in spans:
        probs = s_ref[:rows, a:b] * inverse
        x_ref[rows:, a:b] = probs.astype(BF16)
        x_ref[:rows, a:b] = (probs * (s_ref[rows:, a:b] - delta)).astype(BF16)
        x = x_ref[:, a:b]
        out = out + jnp.dot(x, kv_chunk(a, b), preferred_element_type=F32)
        acc_ref[a:b, :] += lax.dot_general(x, y, (((0,), (0,)), ((), ())), preferred_element_type=F32)
    lows = lax.broadcasted_iota(jnp.int32, (rows, width), 1) < HEAD
    res = jnp.where(lows, out[:rows] * SCALE, out[rows:]).astype(BF16)
    for h in range(2):
        for a in range(here):
            at = h * half + a * 64
            dqo_ref[a, h * 64 : (h + 1) * 64, :] = res[at : at + 64]

    @pl.when(step == last)
    def _():
        dkv_ref[...] = acc_ref[...].reshape(sources, 128, width).astype(BF16)


def attention(kvq, here=2, ck=1024):
    sources = kvq.shape[0]
    keys, rows = sources * 128, here * 128
    return pl.pallas_call(
        functools.partial(attention_kernel, ck),
        grid=(sources // here,),
        in_specs=[
            pl.BlockSpec((sources, 256, 128), lambda i: (0, 0, 0), pipeline_mode=pl.Buffered(1)),
        ],
        out_specs=[
            pl.BlockSpec((here, 128, 128), lambda i: (i, 0, 0)),
            pl.BlockSpec((sources, 128, 128), lambda i: (0, 0, 0)),
        ],
        out_shape=[
            jax.ShapeDtypeStruct((sources, 128, 128), BF16),
            jax.ShapeDtypeStruct((sources, 128, 128), BF16),
        ],
        scratch_shapes=[
            pltpu.VMEM((2 * rows, keys), F32),
            pltpu.VMEM((2 * rows, keys), BF16),
            pltpu.VMEM((2 * rows, 128), BF16),
            pltpu.VMEM((keys, 128), F32),
        ],
        compiler_params=pltpu.CompilerParams(vmem_limit_bytes=VMEM),
        cost_estimate=pl.CostEstimate(flops=48 * keys * keys * HEAD, bytes_accessed=4 << 20, transcendentals=keys * keys),
    )(kvq)


def in_weight_kernel(lat_ref, chan_ref, gain_ref, shift_ref, dqo_ref, dkv_ref, out_ref, acc_ref, turned_ref, block_ref):
    step, last = pl.program_id(0), pl.num_programs(0) - 1
    sources, _, channels = lat_ref.shape
    rows = sources * 128

    @pl.when(step == 0)
    def _():
        acc_ref[...] = jnp.zeros_like(acc_ref)

    lat = lat_ref[...].reshape(rows, channels).astype(F32)
    centred = (lat - chan_ref[0:1]) * chan_ref[1:2]
    normed = (centred * gain_ref[...] + shift_ref[...]).astype(BF16)
    grads = jnp.concatenate(
        [dqo_ref[...].reshape(rows, 128), dkv_ref[...].reshape(rows, 128)], axis=1
    )
    acc_ref[...] += lax.dot_general(grads, normed, (((0,), (0,)), ((), ())), preferred_element_type=F32)

    @pl.when(step == last)
    def _():
        turned_ref[...] = acc_ref[...].T
        low = lax.broadcasted_iota(jnp.int32, (5, 128), 1) < HEAD
        for d in range(channels // 10):
            at = d * 10
            block_ref[0:10] = turned_ref[at : at + 10, 128:256]
            first, second = turned_ref[at : at + 5, 0:128], turned_ref[at + 5 : at + 10, 0:128]
            block_ref[10:15] = jnp.where(low, first, pltpu.roll(second, HEAD, 1))
            block_ref[15:16] = jnp.zeros((1, 128), F32)
            out_ref[d] = block_ref[...].astype(BF16)


def in_weight(lat, chan, gain, shift, dqo, dkv, here=4):
    sources, _, channels = lat.shape
    return pl.pallas_call(
        in_weight_kernel,
        grid=(sources // here,),
        in_specs=[
            pl.BlockSpec((here, 128, channels), lambda i: (i, 0, 0)),
            pl.BlockSpec((2, channels), lambda i: (0, 0)),
            pl.BlockSpec((1, channels), lambda i: (0, 0)),
            pl.BlockSpec((1, channels), lambda i: (0, 0)),
            pl.BlockSpec((here, 128, 128), lambda i: (i, 0, 0)),
            pl.BlockSpec((here, 128, 128), lambda i: (i, 0, 0)),
        ],
        out_specs=pl.BlockSpec((channels // 10, 16, 128), lambda i: (0, 0, 0)),
        out_shape=jax.ShapeDtypeStruct((channels // 10, 16, 128), BF16),
        scratch_shapes=[
            pltpu.VMEM((256, channels), F32), pltpu.VMEM((channels, 256), F32), pltpu.VMEM((16, 128), F32),
        ],
        compiler_params=pltpu.CompilerParams(vmem_limit_bytes=VMEM),
        cost_estimate=pl.CostEstimate(flops=2 * 4096 * 1280 * 256, bytes_accessed=14 << 20, transcendentals=0),
    )(lat, chan, gain, shift, dqo, dkv)


def paired(first, second, low, upper):
    if upper:
        return jnp.where(low, pltpu.roll(first.astype(F32), HEAD, 1), second.astype(F32)).astype(BF16)
    return jnp.where(low, first.astype(F32), pltpu.roll(second.astype(F32), HEAD, 1)).astype(BF16)


def mixed_kernel(own_ref, dqo_ref, lat_ref, w_ref, mixed_ref, att_ref):
    half = w_ref.shape[1]
    low = lax.broadcasted_iota(jnp.int32, (128, 128), 1) < HEAD
    for h in range(0, HEADS, 2):
        for i in range(2):
            att_ref[i, :, h * HEAD : (h + 2) * HEAD] = paired(dqo_ref[h, i], dqo_ref[h + 1, i], low, True)
    own = own_ref[0]
    for i in range(2):
        near = att_ref[i, :, pl.ds(pl.multiple_of(own * half, 128), half)]
        far = att_ref[i, :, pl.ds(pl.multiple_of((1 - own) * half, 128), half)]
        total = jnp.dot(near, w_ref[0], preferred_element_type=F32)
        total = total + jnp.dot(far, w_ref[1], preferred_element_type=F32)
        mixed_ref[i] = (lat_ref[i].astype(F32) + total).astype(BF16)


def mix(own, dqo, lat, halves):
    channels = lat.shape[2]

    def whole(*shape):
        return pl.BlockSpec(shape, lambda s, own: (0,) * len(shape))

    return pl.pallas_call(
        mixed_kernel,
        grid_spec=pltpu.PrefetchScalarGridSpec(
            num_scalar_prefetch=1,
            grid=(1,),
            in_specs=[whole(*dqo.shape), whole(*lat.shape), whole(*halves.shape)],
            out_specs=[whole(*lat.shape), whole(2, 128, HEADS * HEAD)],
        ),
        out_shape=[
            jax.ShapeDtypeStruct(lat.shape, BF16),
            jax.ShapeDtypeStruct((2, 128, HEADS * HEAD), BF16),
        ],
        compiler_params=pltpu.CompilerParams(vmem_limit_bytes=VMEM),
        cost_estimate=pl.CostEstimate(flops=2 * 256 * 1280 * 1024, bytes_accessed=6 << 20, transcendentals=0),
    )(own, dqo, lat, halves)


def out_weight_kernel(own_ref, att_ref, att_far_ref, cot_ref, cot_far_ref, out_ref):
    channels = cot_ref.shape[2]
    wide = att_ref.shape[2]
    att = jnp.concatenate([att_ref[...].reshape(256, wide), att_far_ref[...].reshape(256, wide)], axis=0)
    cot = jnp.concatenate([cot_ref[...].reshape(256, channels), cot_far_ref[...].reshape(256, channels)], axis=0)
    total = lax.dot_general(att, cot, (((0,), (0,)), ((), ())), preferred_element_type=F32)
    blocks = total.reshape(wide // 16, 2, 8, channels)
    own = own_ref[0]
    out_ref[...] = jnp.where(own == 0, blocks[:, 0], blocks[:, 1]).astype(BF16)


def out_weight(own, att, att_far, cot, cot_far):
    channels, wide = cot.shape[2], att.shape[2]
    tile = 256
    side = pl.BlockSpec((2, 128, tile), lambda s, own: (0, 0, s))
    full = pl.BlockSpec(cot.shape, lambda s, own: (0, 0, 0))
    return pl.pallas_call(
        out_weight_kernel,
        grid_spec=pltpu.PrefetchScalarGridSpec(
            num_scalar_prefetch=1,
            grid=(wide // tile,),
            in_specs=[side, side, full, full],
            out_specs=pl.BlockSpec((tile // 16, 8, channels), lambda s, own: (s, 0, 0)),
        ),
        out_shape=jax.ShapeDtypeStruct((wide // 16, 8, channels), BF16),
        compiler_params=pltpu.CompilerParams(vmem_limit_bytes=VMEM),
        cost_estimate=pl.CostEstimate(flops=4 * 256 * 1280 * 1024, bytes_accessed=6 << 20, transcendentals=0),
    )(own, att, att_far, cot, cot_far)


def place():
    return tuple(lax.axis_index(axis) for axis in ALL)


def shifted(here, k, sign):
    dy, dz, dx, dr = k // 16, (k // 4) % 4, (k // 2) % 2, k % 2
    y = (here[0] + (dy if sign > 0 else 4 - dy)) % 4
    z = (here[1] + (dz if sign > 0 else 4 - dz)) % 4
    x = (here[2] + dx) % 2
    r = (here[3] + dr) % 2
    return {"y": y, "z": z, "xl": x, "rep": r}, ((y * 4 + z) * 2 + x) * 2 + r


def tail_kernel(
    count, part_ref, dqo_ref, dkv_ref, mine_ref, other_ref, lat_ref, cot_ref, chan_ref, gain_ref,
    out_ref, weight_ref, rows_ref, grad_ref, near_ref, far_ref, got_ref,
    part_send, part_recv, sums_send, sums_recv,
):
    here = place()
    own = here[4]
    lines, seqs = part_ref.shape[0], far_ref.shape[0]
    block = ((here[0] * 4 + here[1]) * 2 + here[2]) * 2 + here[3]
    line = block // 2

    barrier = pltpu.get_barrier_semaphore()

    @pl.loop(1, lines)
    def _(k):
        pl.semaphore_signal(barrier, inc=1, device_id=shifted(here, k, 1)[0], device_id_type=pl.DeviceIdType.MESH)

    pl.semaphore_wait(barrier, lines - 1)

    def part_copy(k):
        target, there = shifted(here, k, 1)
        return pltpu.make_async_remote_copy(
            src_ref=part_ref.at[there], dst_ref=got_ref.at[block],
            send_sem=part_send.at[k], recv_sem=part_recv.at[k],
            device_id=target, device_id_type=pl.DeviceIdType.MESH,
        )

    def part_arrival(k):
        source, there = shifted(here, k, -1)
        return pltpu.make_async_remote_copy(
            src_ref=part_ref.at[there], dst_ref=got_ref.at[there],
            send_sem=part_send.at[k], recv_sem=part_recv.at[k],
            device_id=source, device_id_type=pl.DeviceIdType.MESH,
        )

    def sums_copy(k):
        target, _ = shifted(here, 2 * k, 1)
        return pltpu.make_async_remote_copy(
            src_ref=near_ref, dst_ref=far_ref.at[line],
            send_sem=sums_send.at[k], recv_sem=sums_recv.at[k],
            device_id=target, device_id_type=pl.DeviceIdType.MESH,
        )

    def sums_arrival(k):
        source, there = shifted(here, 2 * k, -1)
        return pltpu.make_async_remote_copy(
            src_ref=near_ref, dst_ref=far_ref.at[there // 2],
            send_sem=sums_send.at[k], recv_sem=sums_recv.at[k],
            device_id=source, device_id_type=pl.DeviceIdType.MESH,
        )

    @pl.loop(1, lines)
    def _(k):
        part_copy(k).start()

    inner, half = HEADS * HEAD, mine_ref.shape[0]
    low = lax.broadcasted_iota(jnp.int32, (128, 128), 1) < HEAD
    for h in range(0, HEADS, 2):
        for i in range(2):
            rows, at = slice(i * 128, (i + 1) * 128), h * HEAD
            dq, dk = (dqo_ref[h, i], dqo_ref[h + 1, i]), (dkv_ref[h, i], dkv_ref[h + 1, i])
            rows_ref[rows, at : at + 128] = paired(*dq, low, False)
            rows_ref[rows, inner + at : inner + at + 128] = paired(*dk, low, False)
            rows_ref[rows, 2 * inner + at : 2 * inner + at + 128] = paired(*dk, low, True)
    grads = rows_ref[...]
    for side, w_ref in ((own, mine_ref), (1 - own, other_ref)):
        part = lax.dot_general(grads, w_ref[...], (((1,), (1,)), ((), ())), preferred_element_type=F32)
        lanes = pl.ds(pl.multiple_of(side * half, 128), half)
        for i in range(2):
            grad_ref[i, :, lanes] = part[i * 128 : (i + 1) * 128]
    ones, twos = [], []
    for i in range(2):
        grad = grad_ref[i] * gain_ref[...]
        grad_ref[i] = grad
        centred = (lat_ref[i].astype(F32) - chan_ref[i : i + 1]) * chan_ref[2 + i : 3 + i]
        ones.append(jnp.sum(grad, axis=0, keepdims=True))
        twos.append(jnp.sum(grad * centred, axis=0, keepdims=True))
    table = members(lat_ref.shape[2])
    sums = by_group(four_rows(ones + twos), table)
    near_ref[...] = sums
    far_ref[line] = sums

    @pl.loop(1, seqs)
    def _(k):
        sums_copy(k).start()

    got_ref[block] = part_ref[block]

    @pl.loop(1, seqs)
    def _(k):
        sums_arrival(k).wait_recv()

    means = by_channel(jnp.sum(far_ref[...], axis=0) / count, table)
    for i in range(2):
        inv = chan_ref[2 + i : 3 + i]
        centred = (lat_ref[i].astype(F32) - chan_ref[i : i + 1]) * inv
        grad = inv * (grad_ref[i] - means[i : i + 1] - centred * means[2 + i : 3 + i])
        out_ref[i] = (cot_ref[i].astype(F32) + grad).astype(BF16)

    @pl.loop(1, lines)
    def _(k):
        part_arrival(k).wait_recv()

    total = got_ref[0:8].astype(F32)
    for k in range(8, lines, 8):
        total = total + got_ref[k : k + 8].astype(F32)
    weight_ref[...] = jnp.sum(total, axis=0)

    @pl.loop(1, lines)
    def _(k):
        part_copy(k).wait_send()

    @pl.loop(1, seqs)
    def _(k):
        sums_copy(k).wait_send()


def tail(part, dqo, dkv, mine, other, lat, cot, chan, gain, count):
    lines, channels = part.shape[0], part.shape[2]
    dma = pltpu.SemaphoreType.DMA
    return pl.pallas_call(
        functools.partial(tail_kernel, count),
        out_shape=[jax.ShapeDtypeStruct(lat.shape, BF16), jax.ShapeDtypeStruct((8, channels), F32)],
        scratch_shapes=[
            pltpu.VMEM((256, 3 * HEADS * HEAD), BF16),
            pltpu.VMEM(lat.shape, F32),
            pltpu.VMEM((8, 128), F32),
            pltpu.VMEM((lines // 2, 8, 128), F32),
            pltpu.VMEM(part.shape, BF16),
            dma((lines,)), dma((lines,)), dma((lines // 2,)), dma((lines // 2,)),
        ],
        compiler_params=pltpu.CompilerParams(vmem_limit_bytes=VMEM, collective_id=1, has_side_effects=True),
        cost_estimate=pl.CostEstimate(flops=2 << 34, bytes_accessed=16 << 20, transcendentals=0),
    )(part, dqo, dkv, mine, other, lat, cot, chan, gain)


def swapped(value, axis):
    return lax.ppermute(value, axis, [(0, 1), (1, 0)])


def exchanged(value, axes):
    return lax.all_to_all(value, axes, 0, 0, tiled=True)


def shards(latent, cotangent, norm_gain, norm_shift, proj_qkv, proj_out):
    local_len, images, channels = latent.shape
    seq_count = lax.axis_size(SEQ)
    count = local_len * seq_count * (channels // GROUPS)
    own = lax.axis_index("own").reshape(1)
    gain, shift = norm_gain.reshape(1, channels), norm_shift.reshape(1, channels)

    other_out = swapped(proj_out, "own")
    other_qkv = swapped(proj_qkv, "own")
    lat = latent.transpose(1, 0, 2)
    sums = exchanged(stats(lat, seq_count), SEQ)
    cot = cotangent.transpose(1, 0, 2)
    image = lax.axis_index("xl")
    near = jnp.where(image == 0, lat[0], lat[1])
    far = swapped(jnp.where(image == 0, lat[1], lat[0]), "xl")
    pair_lat = jnp.where(image == 0, jnp.stack([near, far]), jnp.stack([far, near]))
    halves_out = jnp.stack([proj_out, other_out])
    cot_far = swapped(cot, "own")
    g = attended_grad(own, cot, halves_out)
    pair_lat, sums = lax.optimization_barrier((pair_lat, sums))
    chan, kvqg = project(lat, sums, gain, shift, g, proj_qkv, other_qkv, count)
    pair_lat, kvqg = lax.optimization_barrier((pair_lat, kvqg))
    image_lat = lax.all_gather(pair_lat, ("y", "z"), tiled=True)

    dqo, dkv = attention(kvqg)

    dqo_tok = exchanged(dqo, SEQ)
    chan_image = jnp.where(image == 0, chan[0:4:2], chan[1:4:2])
    in_part = in_weight(image_lat, chan_image, gain, shift, dqo, dkv)
    dqo_tok, dkv, in_part = lax.optimization_barrier((dqo_tok, dkv, in_part))
    dkv_tok = exchanged(dkv, SEQ)
    dqo_tok = dqo_tok.reshape(HEADS, images, 128, 128)
    mixed, att = mix(own, dqo_tok, lat, halves_out)
    out_part = out_weight(own, att, swapped(att, "own"), cot, cot_far)
    dkv_tok, out_part, in_part = lax.optimization_barrier((dkv_tok, out_part, in_part))
    in_blocks = exchanged(in_part, ALL)
    dkv_tok = dkv_tok.reshape(HEADS, images, 128, 128)
    grad_latent, grad_out = tail(
        out_part, dqo_tok, dkv_tok, proj_qkv, other_qkv, lat, cot, chan, gain, count
    )

    summed = jnp.sum(in_blocks.reshape(HEADS, 8, 16, 128).astype(F32), axis=1)
    dq = summed[:, 10:15].reshape(HEADS, 5, 2, HEAD).transpose(2, 1, 0, 3).reshape(10, HEADS * HEAD)
    dk = summed[:, :10, :HEAD].transpose(1, 0, 2).reshape(10, HEADS * HEAD)
    dv = summed[:, :10, HEAD:].transpose(1, 0, 2).reshape(10, HEADS * HEAD)
    grad_qkv = jnp.concatenate([dq, dk, dv], axis=1)
    return (mixed.transpose(1, 0, 2), grad_latent.transpose(1, 0, 2), grad_qkv, grad_out)


def solution(mesh):
    fine = Mesh(mesh.devices.reshape(4, 4, 2, 2, 2), ALL)
    tokens = P(SEQ, ("rep", "own"), None)
    return jax.shard_map(
        shards,
        mesh=fine,
        in_specs=(tokens, tokens, P(), P(), P("own", None), P("own", None)),
        out_specs=(tokens, tokens, P(ALL, None), P(ALL, None)),
        check_vma=False,
    )
```

```python
import functools

import jax
import jax.numpy as jnp
from jax import lax
from jax.experimental import pallas as pl
from jax.experimental.pallas import tpu as pltpu
from jax.sharding import Mesh
from jax.sharding import PartitionSpec as P

HEADS = 16
HEAD = 64
GROUPS = 32
SCALE = HEAD ** (-0.5)
SEQ = ("y", "z", "xl")
LINE = ("y", "z", "xl", "rep")
ALL = ("y", "z", "xl", "rep", "own")
F32, BF16 = jnp.float32, jnp.bfloat16
VMEM = 60 << 20


def place():
    return tuple(lax.axis_index(axis) for axis in ALL)


def members(channels):
    channel = lax.broadcasted_iota(jnp.int32, (channels, 128), 0)
    group = lax.broadcasted_iota(jnp.int32, (channels, 128), 1)
    first = group * (channels // GROUPS)
    return ((channel >= first) & (channel < first + channels // GROUPS)).astype(F32)


def by_group(rows, table):
    return lax.dot_general(
        rows, table, (((1,), (0,)), ((), ())),
        precision=lax.Precision.HIGHEST, preferred_element_type=F32,
    )


def by_channel(rows, table):
    return lax.dot_general(
        rows, table, (((1,), (1,)), ((), ())),
        precision=lax.Precision.HIGHEST, preferred_element_type=F32,
    )


def four_rows(rows):
    width = rows[0].shape[1]
    return jnp.concatenate([*rows, jnp.zeros((4, width), F32)], axis=0)


def stats_kernel(lat_ref, out_ref):
    values = [lat_ref[i].astype(F32) for i in range(2)]
    rows = [jnp.sum(v, axis=0, keepdims=True) for v in values]
    rows += [jnp.sum(v * v, axis=0, keepdims=True) for v in values]
    out_ref[...] = jnp.broadcast_to(by_group(four_rows(rows), members(lat_ref.shape[2]))[None], out_ref.shape)


def stats(lat, copies):
    return pl.pallas_call(
        stats_kernel,
        out_shape=jax.ShapeDtypeStruct((copies, 8, 128), F32),
        compiler_params=pltpu.CompilerParams(vmem_limit_bytes=VMEM),
        cost_estimate=pl.CostEstimate(flops=1 << 20, bytes_accessed=lat.size * 2, transcendentals=0),
    )(lat)


def moments(sums, count):
    means = sums / count
    var = means[2:4] - means[0:2] * means[0:2]
    return jnp.concatenate([means[0:2], lax.rsqrt(var + 1e-06), jnp.zeros((4, 128), F32)], axis=0)


def project_kernel(
    count, lat_ref, sums_ref, gain_ref, shift_ref, g_ref, mine_ref, other_ref,
    chan_ref, out_ref, normed_ref, send_ref, send_sem, recv_sem, keep_sem,
):
    here = place()
    own = here[4]
    half = mine_ref.shape[0]
    inner = HEADS * HEAD
    line = (here[0] * 4 + here[1]) * 2 + here[2]
    seqs = out_ref.shape[0]

    def device(at):
        return {"y": at // 8, "z": (at // 2) % 4, "xl": at % 2}

    barrier = pltpu.get_barrier_semaphore()

    @pl.loop(1, seqs)
    def _(k):
        to = lax.rem(line + k, seqs)
        pl.semaphore_signal(barrier, inc=1, device_id=device(to), device_id_type=pl.DeviceIdType.MESH)

    table = members(lat_ref.shape[2])
    chan = by_channel(moments(jnp.sum(sums_ref[...], axis=0), count), table)
    chan_ref[...] = chan
    for i in range(2):
        centred = (lat_ref[i].astype(F32) - chan[i : i + 1]) * chan[2 + i : 3 + i]
        normed_ref[i * 128 : (i + 1) * 128] = (centred * gain_ref[...] + shift_ref[...]).astype(BF16)
    near = normed_ref[:, pl.ds(pl.multiple_of(own * half, 128), half)]
    far = normed_ref[:, pl.ds(pl.multiple_of((1 - own) * half, 128), half)]
    low = lax.broadcasted_iota(jnp.int32, (128, 128), 1) < HEAD

    def copy(row, column):
        at = row * 8 + column
        return pltpu.make_async_remote_copy(
            src_ref=send_ref.at[at], dst_ref=out_ref.at[line],
            send_sem=send_sem.at[at], recv_sem=recv_sem.at[line],
            device_id=device(at), device_id_type=pl.DeviceIdType.MESH,
        )

    def arrival(at):
        return pltpu.make_async_remote_copy(
            src_ref=send_ref.at[at], dst_ref=out_ref.at[at],
            send_sem=send_sem.at[at], recv_sem=recv_sem.at[at],
            device_id=device(at), device_id_type=pl.DeviceIdType.MESH,
        )

    def block_row(row):
        lanes = [pl.ds(pl.multiple_of(p * inner + row * 256, 256), 256) for p in range(3)]
        query, key, value = [
            jnp.dot(near, mine_ref[:, at], preferred_element_type=F32)
            + jnp.dot(far, other_ref[:, at], preferred_element_type=F32)
            for at in lanes
        ]
        for h in range(0, 4, 2):
            for i in range(2):
                rows, part = slice(i * 128, (i + 1) * 128), slice(h * HEAD, (h + 2) * HEAD)
                q, k, v = query[rows, part], key[rows, part], value[rows, part]
                k_roll, v_roll = pltpu.roll(k, HEAD, 1), pltpu.roll(v, HEAD, 1)
                first, second = q[:64], q[64:]
                one, two = row * 8 + h * 2 + i, row * 8 + (h + 1) * 2 + i
                send_ref[one, :128] = jnp.where(low, k, v_roll).astype(BF16)
                send_ref[two, :128] = jnp.where(low, k_roll, v).astype(BF16)
                send_ref[one, 128:192] = jnp.where(low[:64], first, pltpu.roll(second, HEAD, 1)).astype(BF16)
                send_ref[two, 128:192] = jnp.where(low[:64], pltpu.roll(first, HEAD, 1), second).astype(BF16)
                send_ref[one, 192:256] = g_ref[row * 4 + h, i]
                send_ref[two, 192:256] = g_ref[row * 4 + h + 1, i]

    pl.semaphore_wait(barrier, seqs - 1)
    for j in range(4):
        row = (here[0] + (j + 1)) % 4
        block_row(row)
        if j < 3:
            @pl.loop(0, 8)
            def _(k):
                copy(row, (here[1] * 2 + here[2] + k) % 8).start()
        else:
            @pl.loop(1, 8)
            def _(k):
                copy(row, (here[1] * 2 + here[2] + k) % 8).start()

    keep = pltpu.make_async_copy(send_ref.at[line], out_ref.at[line], keep_sem)
    keep.start()

    @pl.loop(1, seqs)
    def _(k):
        arrival(lax.rem(line + k, seqs)).wait()

    keep.wait()


def project(lat, sums, gain, shift, g, mine, other, count):
    channels = lat.shape[2]
    seqs = sums.shape[0]
    dma = pltpu.SemaphoreType.DMA
    whole = pl.BlockSpec(memory_space=pltpu.VMEM)
    return pl.pallas_call(
        functools.partial(project_kernel, count),
        in_specs=[whole] * 7,
        out_specs=[whole, pl.BlockSpec(memory_space=pl.ANY)],
        out_shape=[
            jax.ShapeDtypeStruct((8, channels), F32),
            jax.ShapeDtypeStruct((seqs, 256, 128), BF16),
        ],
        scratch_shapes=[
            pltpu.VMEM((256, channels), BF16),
            pltpu.VMEM((seqs, 256, 128), BF16),
            dma((seqs,)), dma((seqs,)), dma,
        ],
        compiler_params=pltpu.CompilerParams(vmem_limit_bytes=VMEM, collective_id=2, has_side_effects=True),
        cost_estimate=pl.CostEstimate(flops=2 << 34, bytes_accessed=12 << 20, transcendentals=0),
    )(lat, sums, gain, shift, g, mine, other)


def attended_grad_kernel(own_ref, cot_ref, w_ref, out_ref):
    rows = cot_ref[...].reshape(256, cot_ref.shape[2])
    grad = lax.dot_general(rows, w_ref[...], (((1,), (1,)), ((), ())), preferred_element_type=F32)
    low = lax.broadcasted_iota(jnp.int32, (64, 128), 1) < HEAD
    for h in range(0, grad.shape[1] // HEAD, 2):
        for i in range(2):
            first = grad[i * 128 : i * 128 + 64, h * HEAD : (h + 2) * HEAD]
            second = grad[i * 128 + 64 : (i + 1) * 128, h * HEAD : (h + 2) * HEAD]
            out_ref[h, i] = jnp.where(low, first, pltpu.roll(second, HEAD, 1)).astype(BF16)
            out_ref[h + 1, i] = jnp.where(low, pltpu.roll(first, HEAD, 1), second).astype(BF16)


def attended_grad(own, cot, halves):
    channels = cot.shape[2]
    per = halves.shape[1] // 256

    return pl.pallas_call(
        attended_grad_kernel,
        grid_spec=pltpu.PrefetchScalarGridSpec(
            num_scalar_prefetch=1,
            grid=(2 * per,),
            in_specs=[
                pl.BlockSpec(cot.shape, lambda s, own: (0, 0, 0)),
                pl.BlockSpec((None, 256, channels), lambda s, own: (s // per, s % per, 0)),
            ],
            out_specs=pl.BlockSpec(
                (4, 2, 64, 128),
                lambda s, own: ((s // per + own[0] - 2 * own[0] * (s // per)) * per + s % per, 0, 0, 0),
            ),
        ),
        out_shape=jax.ShapeDtypeStruct((HEADS, 2, 64, 128), BF16),
        compiler_params=pltpu.CompilerParams(vmem_limit_bytes=VMEM),
        cost_estimate=pl.CostEstimate(flops=2 * 256 * 1280 * 1024, bytes_accessed=4 << 20, transcendentals=0),
    )(own, cot, halves)


def attention_kernel(
    ck, kvq_ref, dqo_ref, dkv_ref, tok_ref, s_ref, x_ref, y_ref, acc_ref, send_ref, send_sem, recv_sem, keep_sem
):
    here_at = place()
    line = (here_at[0] * 4 + here_at[1]) * 2 + here_at[2]

    def device(at):
        return {"y": at // 8, "z": (at // 2) % 4, "xl": at % 2}

    def copy(at):
        return pltpu.make_async_remote_copy(
            src_ref=send_ref.at[at], dst_ref=tok_ref.at[line],
            send_sem=send_sem.at[at], recv_sem=recv_sem.at[line],
            device_id=device(at), device_id_type=pl.DeviceIdType.MESH,
        )

    def arrival(at):
        return pltpu.make_async_remote_copy(
            src_ref=send_ref.at[at], dst_ref=tok_ref.at[at],
            send_sem=send_sem.at[at], recv_sem=recv_sem.at[at],
            device_id=device(at), device_id_type=pl.DeviceIdType.MESH,
        )

    def keep():
        return pltpu.make_async_copy(send_ref.at[line], tok_ref.at[line], keep_sem)

    step, last = pl.program_id(0), pl.num_programs(0) - 1
    sources, _, width = kvq_ref.shape
    keys = sources * 128
    here = dqo_ref.shape[0]
    base = lax.rem(line // here * here + (step + 1) * here, sources)
    rows = here * 128
    half = rows // 2

    @pl.when(step == 0)
    def _():
        acc_ref[...] = jnp.zeros_like(acc_ref)
        barrier = pltpu.get_barrier_semaphore()

        @pl.loop(1, sources)
        def _(k):
            to = lax.rem(line + k, sources)
            pl.semaphore_signal(barrier, inc=1, device_id=device(to), device_id_type=pl.DeviceIdType.MESH)

        pl.semaphore_wait(barrier, sources - 1)

    low = lax.broadcasted_iota(jnp.int32, (half, width), 1) < HEAD
    xq = kvq_ref[pl.ds(base, here), 128:192, :].reshape(half, width).astype(F32) * SCALE
    xg = kvq_ref[pl.ds(base, here), 192:256, :].reshape(half, width).astype(F32)
    zero = jnp.zeros_like(xq)
    y_ref[0 * half : 1 * half] = jnp.where(low, xq, zero).astype(BF16)
    y_ref[1 * half : 2 * half] = jnp.where(low, pltpu.roll(xq, HEAD, 1), zero).astype(BF16)
    y_ref[2 * half : 3 * half] = jnp.where(low, zero, pltpu.roll(xg, HEAD, 1)).astype(BF16)
    y_ref[3 * half : 4 * half] = jnp.where(low, zero, xg).astype(BF16)
    y = y_ref[...]
    spans = [(c, c + ck) for c in range(0, keys, ck)]

    def kv_chunk(a, b):
        return kvq_ref[a // 128 : b // 128, :128, :].reshape(b - a, width)

    top = None
    for a, b in spans:
        both = lax.dot_general(y, kv_chunk(a, b), (((1,), (1,)), ((), ())), preferred_element_type=F32)
        s_ref[:, a:b] = both
        for t in range(0, ck, 128):
            piece = both[:rows, t : t + 128]
            top = piece if top is None else jnp.maximum(top, piece)
    top = jnp.max(top, axis=1, keepdims=True)
    total = jnp.zeros((rows, 128), F32)
    delta = jnp.zeros((rows, 128), F32)
    for a, b in spans:
        weights = jnp.exp(s_ref[:rows, a:b] - top)
        s_ref[:rows, a:b] = weights
        fold = weights * s_ref[rows:, a:b]
        for t in range(0, ck, 128):
            total = total + weights[:, t : t + 128]
            delta = delta + fold[:, t : t + 128]
    inverse = 1.0 / jnp.sum(total, axis=1, keepdims=True)
    delta = jnp.sum(delta, axis=1, keepdims=True) * inverse
    out = jnp.zeros((2 * rows, width), F32)
    for a, b in spans:
        probs = s_ref[:rows, a:b] * inverse
        x_ref[rows:, a:b] = probs.astype(BF16)
        x_ref[:rows, a:b] = (probs * (s_ref[rows:, a:b] - delta)).astype(BF16)
        x = x_ref[:, a:b]
        out = out + jnp.dot(x, kv_chunk(a, b), preferred_element_type=F32)
        acc_ref[a:b, :] += lax.dot_general(x, y, (((0,), (0,)), ((), ())), preferred_element_type=F32)
    lows = lax.broadcasted_iota(jnp.int32, (rows, width), 1) < HEAD
    res = jnp.where(lows, out[:rows] * SCALE, out[rows:]).astype(BF16)
    for h in range(2):
        for a in range(here):
            at = h * half + a * 64
            dqo_ref[a, h * 64 : (h + 1) * 64, :] = res[at : at + 64]
            send_ref[base + a, h * 64 : (h + 1) * 64, :] = res[at : at + 64]

    for a in range(here):
        @pl.when(base + a != line)
        def _():
            copy(base + a).start()

        @pl.when(base + a == line)
        def _():
            keep().start()

    @pl.when(step == last)
    def _():
        dkv_ref[...] = acc_ref[...].reshape(sources, 128, width).astype(BF16)

        @pl.loop(1, sources)
        def _(k):
            arrival(lax.rem(line + k, sources)).wait()

        keep().wait()


def attention(kvq, here=2, ck=1024):
    sources = kvq.shape[0]
    keys, rows = sources * 128, here * 128
    dma = pltpu.SemaphoreType.DMA

    def block(i):
        here_at = place()
        line = (here_at[0] * 4 + here_at[1]) * 2 + here_at[2]
        return lax.rem(line // here + i + 1, sources // here), 0, 0

    return pl.pallas_call(
        functools.partial(attention_kernel, ck),
        grid=(sources // here,),
        in_specs=[
            pl.BlockSpec((sources, 256, 128), lambda i: (0, 0, 0), pipeline_mode=pl.Buffered(1)),
        ],
        out_specs=[
            pl.BlockSpec((here, 128, 128), block),
            pl.BlockSpec((sources, 128, 128), lambda i: (0, 0, 0)),
            pl.BlockSpec(memory_space=pl.ANY),
        ],
        out_shape=[
            jax.ShapeDtypeStruct((sources, 128, 128), BF16),
            jax.ShapeDtypeStruct((sources, 128, 128), BF16),
            jax.ShapeDtypeStruct((sources, 128, 128), BF16),
        ],
        scratch_shapes=[
            pltpu.VMEM((2 * rows, keys), F32),
            pltpu.VMEM((2 * rows, keys), BF16),
            pltpu.VMEM((2 * rows, 128), BF16),
            pltpu.VMEM((keys, 128), F32),
            pltpu.VMEM((sources, 128, 128), BF16),
            dma((sources,)), dma((sources,)), dma,
        ],
        compiler_params=pltpu.CompilerParams(vmem_limit_bytes=VMEM, collective_id=3, has_side_effects=True),
        cost_estimate=pl.CostEstimate(flops=48 * keys * keys * HEAD, bytes_accessed=4 << 20, transcendentals=keys * keys),
    )(kvq)


def in_weight_kernel(lat_ref, chan_ref, gain_ref, shift_ref, dqo_ref, dkv_ref, out_ref, acc_ref, turned_ref, block_ref):
    step, last = pl.program_id(0), pl.num_programs(0) - 1
    sources, _, channels = lat_ref.shape
    rows = sources * 128

    @pl.when(step == 0)
    def _():
        acc_ref[...] = jnp.zeros_like(acc_ref)

    lat = lat_ref[...].reshape(rows, channels).astype(F32)
    centred = (lat - chan_ref[0:1]) * chan_ref[1:2]
    normed = (centred * gain_ref[...] + shift_ref[...]).astype(BF16)
    grads = jnp.concatenate(
        [dqo_ref[...].reshape(rows, 128), dkv_ref[...].reshape(rows, 128)], axis=1
    )
    acc_ref[...] += lax.dot_general(grads, normed, (((0,), (0,)), ((), ())), preferred_element_type=F32)

    @pl.when(step == last)
    def _():
        turned_ref[...] = acc_ref[...].T
        low = lax.broadcasted_iota(jnp.int32, (5, 128), 1) < HEAD
        for d in range(channels // 10):
            at = d * 10
            block_ref[0:10] = turned_ref[at : at + 10, 128:256]
            first, second = turned_ref[at : at + 5, 0:128], turned_ref[at + 5 : at + 10, 0:128]
            block_ref[10:15] = jnp.where(low, first, pltpu.roll(second, HEAD, 1))
            block_ref[15:16] = jnp.zeros((1, 128), F32)
            out_ref[d] = block_ref[...].astype(BF16)


def in_weight(lat, chan, gain, shift, dqo, dkv, here=4):
    sources, _, channels = lat.shape
    return pl.pallas_call(
        in_weight_kernel,
        grid=(sources // here,),
        in_specs=[
            pl.BlockSpec((here, 128, channels), lambda i: (i, 0, 0)),
            pl.BlockSpec((2, channels), lambda i: (0, 0)),
            pl.BlockSpec((1, channels), lambda i: (0, 0)),
            pl.BlockSpec((1, channels), lambda i: (0, 0)),
            pl.BlockSpec((here, 128, 128), lambda i: (i, 0, 0)),
            pl.BlockSpec((here, 128, 128), lambda i: (i, 0, 0)),
        ],
        out_specs=pl.BlockSpec((channels // 10, 16, 128), lambda i: (0, 0, 0)),
        out_shape=jax.ShapeDtypeStruct((channels // 10, 16, 128), BF16),
        scratch_shapes=[
            pltpu.VMEM((256, channels), F32), pltpu.VMEM((channels, 256), F32), pltpu.VMEM((16, 128), F32),
        ],
        compiler_params=pltpu.CompilerParams(vmem_limit_bytes=VMEM),
        cost_estimate=pl.CostEstimate(flops=2 * 4096 * 1280 * 256, bytes_accessed=14 << 20, transcendentals=0),
    )(lat, chan, gain, shift, dqo, dkv)


def paired(first, second, low, upper):
    if upper:
        return jnp.where(low, pltpu.roll(first.astype(F32), HEAD, 1), second.astype(F32)).astype(BF16)
    return jnp.where(low, first.astype(F32), pltpu.roll(second.astype(F32), HEAD, 1)).astype(BF16)


def mixed_kernel(own_ref, dqo_ref, lat_ref, w_ref, mixed_ref, att_ref):
    half = w_ref.shape[1]
    low = lax.broadcasted_iota(jnp.int32, (128, 128), 1) < HEAD
    for h in range(0, HEADS, 2):
        for i in range(2):
            att_ref[i, :, h * HEAD : (h + 2) * HEAD] = paired(dqo_ref[h, i], dqo_ref[h + 1, i], low, True)
    own = own_ref[0]
    for i in range(2):
        near = att_ref[i, :, pl.ds(pl.multiple_of(own * half, 128), half)]
        far = att_ref[i, :, pl.ds(pl.multiple_of((1 - own) * half, 128), half)]
        total = jnp.dot(near, w_ref[0], preferred_element_type=F32)
        total = total + jnp.dot(far, w_ref[1], preferred_element_type=F32)
        mixed_ref[i] = (lat_ref[i].astype(F32) + total).astype(BF16)


def mix(own, dqo, lat, halves):
    channels = lat.shape[2]

    def whole(*shape):
        return pl.BlockSpec(shape, lambda s, own: (0,) * len(shape))

    return pl.pallas_call(
        mixed_kernel,
        grid_spec=pltpu.PrefetchScalarGridSpec(
            num_scalar_prefetch=1,
            grid=(1,),
            in_specs=[whole(*dqo.shape), whole(*lat.shape), whole(*halves.shape)],
            out_specs=[whole(*lat.shape), whole(2, 128, HEADS * HEAD)],
        ),
        out_shape=[
            jax.ShapeDtypeStruct(lat.shape, BF16),
            jax.ShapeDtypeStruct((2, 128, HEADS * HEAD), BF16),
        ],
        compiler_params=pltpu.CompilerParams(vmem_limit_bytes=VMEM),
        cost_estimate=pl.CostEstimate(flops=2 * 256 * 1280 * 1024, bytes_accessed=6 << 20, transcendentals=0),
    )(own, dqo, lat, halves)


def out_weight_kernel(own_ref, att_ref, att_far_ref, cot_ref, cot_far_ref, out_ref):
    channels = cot_ref.shape[2]
    wide = att_ref.shape[2]
    att = jnp.concatenate([att_ref[...].reshape(256, wide), att_far_ref[...].reshape(256, wide)], axis=0)
    cot = jnp.concatenate([cot_ref[...].reshape(256, channels), cot_far_ref[...].reshape(256, channels)], axis=0)
    total = lax.dot_general(att, cot, (((0,), (0,)), ((), ())), preferred_element_type=F32)
    blocks = total.reshape(wide // 16, 2, 8, channels)
    own = own_ref[0]
    out_ref[...] = jnp.where(own == 0, blocks[:, 0], blocks[:, 1]).astype(BF16)


def out_weight(own, att, att_far, cot, cot_far):
    channels, wide = cot.shape[2], att.shape[2]
    tile = 256
    side = pl.BlockSpec((2, 128, tile), lambda s, own: (0, 0, s))
    full = pl.BlockSpec(cot.shape, lambda s, own: (0, 0, 0))
    return pl.pallas_call(
        out_weight_kernel,
        grid_spec=pltpu.PrefetchScalarGridSpec(
            num_scalar_prefetch=1,
            grid=(wide // tile,),
            in_specs=[side, side, full, full],
            out_specs=pl.BlockSpec((tile // 16, 8, channels), lambda s, own: (s, 0, 0)),
        ),
        out_shape=jax.ShapeDtypeStruct((wide // 16, 8, channels), BF16),
        compiler_params=pltpu.CompilerParams(vmem_limit_bytes=VMEM),
        cost_estimate=pl.CostEstimate(flops=4 * 256 * 1280 * 1024, bytes_accessed=6 << 20, transcendentals=0),
    )(own, att, att_far, cot, cot_far)


def shifted(here, k, sign):
    dy, dz, dx, dr = k // 16, (k // 4) % 4, (k // 2) % 2, k % 2
    y = (here[0] + (dy if sign > 0 else 4 - dy)) % 4
    z = (here[1] + (dz if sign > 0 else 4 - dz)) % 4
    x = (here[2] + dx) % 2
    r = (here[3] + dr) % 2
    return {"y": y, "z": z, "xl": x, "rep": r}, ((y * 4 + z) * 2 + x) * 2 + r


def tail_kernel(
    count, part_ref, dqo_ref, dkv_ref, mine_ref, other_ref, lat_ref, cot_ref, chan_ref, gain_ref,
    out_ref, weight_ref, rows_ref, grad_ref, near_ref, far_ref, got_ref,
    part_send, part_recv, sums_send, sums_recv,
):
    here = place()
    own = here[4]
    lines, seqs = part_ref.shape[0], far_ref.shape[0]
    block = ((here[0] * 4 + here[1]) * 2 + here[2]) * 2 + here[3]
    line = block // 2

    barrier = pltpu.get_barrier_semaphore()

    @pl.loop(1, lines)
    def _(k):
        pl.semaphore_signal(barrier, inc=1, device_id=shifted(here, k, 1)[0], device_id_type=pl.DeviceIdType.MESH)

    pl.semaphore_wait(barrier, lines - 1)

    def part_copy(k):
        target, there = shifted(here, k, 1)
        return pltpu.make_async_remote_copy(
            src_ref=part_ref.at[there], dst_ref=got_ref.at[block],
            send_sem=part_send.at[k], recv_sem=part_recv.at[k],
            device_id=target, device_id_type=pl.DeviceIdType.MESH,
        )

    def part_arrival(k):
        source, there = shifted(here, k, -1)
        return pltpu.make_async_remote_copy(
            src_ref=part_ref.at[there], dst_ref=got_ref.at[there],
            send_sem=part_send.at[k], recv_sem=part_recv.at[k],
            device_id=source, device_id_type=pl.DeviceIdType.MESH,
        )

    def sums_copy(k):
        target, _ = shifted(here, 2 * k, 1)
        return pltpu.make_async_remote_copy(
            src_ref=near_ref, dst_ref=far_ref.at[line],
            send_sem=sums_send.at[k], recv_sem=sums_recv.at[k],
            device_id=target, device_id_type=pl.DeviceIdType.MESH,
        )

    def sums_arrival(k):
        source, there = shifted(here, 2 * k, -1)
        return pltpu.make_async_remote_copy(
            src_ref=near_ref, dst_ref=far_ref.at[there // 2],
            send_sem=sums_send.at[k], recv_sem=sums_recv.at[k],
            device_id=source, device_id_type=pl.DeviceIdType.MESH,
        )

    @pl.loop(1, lines)
    def _(k):
        part_copy(k).start()

    inner, half = HEADS * HEAD, mine_ref.shape[0]
    low = lax.broadcasted_iota(jnp.int32, (128, 128), 1) < HEAD
    for h in range(0, HEADS, 2):
        for i in range(2):
            rows, at = slice(i * 128, (i + 1) * 128), h * HEAD
            dq, dk = (dqo_ref[h, i], dqo_ref[h + 1, i]), (dkv_ref[h, i], dkv_ref[h + 1, i])
            rows_ref[rows, at : at + 128] = paired(*dq, low, False)
            rows_ref[rows, inner + at : inner + at + 128] = paired(*dk, low, False)
            rows_ref[rows, 2 * inner + at : 2 * inner + at + 128] = paired(*dk, low, True)
    grads = rows_ref[...]
    for side, w_ref in ((own, mine_ref), (1 - own, other_ref)):
        part = lax.dot_general(grads, w_ref[...], (((1,), (1,)), ((), ())), preferred_element_type=F32)
        lanes = pl.ds(pl.multiple_of(side * half, 128), half)
        for i in range(2):
            grad_ref[i, :, lanes] = part[i * 128 : (i + 1) * 128]
    ones, twos = [], []
    for i in range(2):
        grad = grad_ref[i] * gain_ref[...]
        grad_ref[i] = grad
        centred = (lat_ref[i].astype(F32) - chan_ref[i : i + 1]) * chan_ref[2 + i : 3 + i]
        ones.append(jnp.sum(grad, axis=0, keepdims=True))
        twos.append(jnp.sum(grad * centred, axis=0, keepdims=True))
    table = members(lat_ref.shape[2])
    sums = by_group(four_rows(ones + twos), table)
    near_ref[...] = sums
    far_ref[line] = sums

    @pl.loop(1, seqs)
    def _(k):
        sums_copy(k).start()

    got_ref[block] = part_ref[block]

    @pl.loop(1, seqs)
    def _(k):
        sums_arrival(k).wait_recv()

    means = by_channel(jnp.sum(far_ref[...], axis=0) / count, table)
    for i in range(2):
        inv = chan_ref[2 + i : 3 + i]
        centred = (lat_ref[i].astype(F32) - chan_ref[i : i + 1]) * inv
        grad = inv * (grad_ref[i] - means[i : i + 1] - centred * means[2 + i : 3 + i])
        out_ref[i] = (cot_ref[i].astype(F32) + grad).astype(BF16)

    @pl.loop(1, lines)
    def _(k):
        part_arrival(k).wait_recv()

    total = got_ref[0:8].astype(F32)
    for k in range(8, lines, 8):
        total = total + got_ref[k : k + 8].astype(F32)
    weight_ref[...] = jnp.sum(total, axis=0)

    @pl.loop(1, lines)
    def _(k):
        part_copy(k).wait_send()

    @pl.loop(1, seqs)
    def _(k):
        sums_copy(k).wait_send()


def tail(part, dqo, dkv, mine, other, lat, cot, chan, gain, count):
    lines, channels = part.shape[0], part.shape[2]
    dma = pltpu.SemaphoreType.DMA
    return pl.pallas_call(
        functools.partial(tail_kernel, count),
        out_shape=[jax.ShapeDtypeStruct(lat.shape, BF16), jax.ShapeDtypeStruct((8, channels), F32)],
        scratch_shapes=[
            pltpu.VMEM((256, 3 * HEADS * HEAD), BF16),
            pltpu.VMEM(lat.shape, F32),
            pltpu.VMEM((8, 128), F32),
            pltpu.VMEM((lines // 2, 8, 128), F32),
            pltpu.VMEM(part.shape, BF16),
            dma((lines,)), dma((lines,)), dma((lines // 2,)), dma((lines // 2,)),
        ],
        compiler_params=pltpu.CompilerParams(vmem_limit_bytes=VMEM, collective_id=1, has_side_effects=True),
        cost_estimate=pl.CostEstimate(flops=2 << 34, bytes_accessed=16 << 20, transcendentals=0),
    )(part, dqo, dkv, mine, other, lat, cot, chan, gain)


def swapped(value, axis):
    return lax.ppermute(value, axis, [(0, 1), (1, 0)])


def exchanged(value, axes):
    return lax.all_to_all(value, axes, 0, 0, tiled=True)


def shards(latent, cotangent, norm_gain, norm_shift, proj_qkv, proj_out):
    local_len, images, channels = latent.shape
    seq_count = lax.axis_size(SEQ)
    count = local_len * seq_count * (channels // GROUPS)
    own = lax.axis_index("own").reshape(1)
    gain, shift = norm_gain.reshape(1, channels), norm_shift.reshape(1, channels)

    other_out = swapped(proj_out, "own")
    other_qkv = swapped(proj_qkv, "own")
    lat = latent.transpose(1, 0, 2)
    sums = exchanged(stats(lat, seq_count), SEQ)
    cot = cotangent.transpose(1, 0, 2)
    image = lax.axis_index("xl")
    near = jnp.where(image == 0, lat[0], lat[1])
    far = swapped(jnp.where(image == 0, lat[1], lat[0]), "xl")
    pair_lat = jnp.where(image == 0, jnp.stack([near, far]), jnp.stack([far, near]))
    halves_out = jnp.stack([proj_out, other_out])
    cot_far = swapped(cot, "own")
    g = attended_grad(own, cot, halves_out)
    pair_lat, sums = lax.optimization_barrier((pair_lat, sums))
    chan, kvqg = project(lat, sums, gain, shift, g, proj_qkv, other_qkv, count)
    pair_lat, kvqg = lax.optimization_barrier((pair_lat, kvqg))
    image_lat = lax.all_gather(pair_lat, ("y", "z"), tiled=True)

    dqo, dkv, dqo_tok = attention(kvqg)

    dkv_tok = exchanged(dkv, SEQ)
    chan_image = jnp.where(image == 0, chan[0:4:2], chan[1:4:2])
    in_part = in_weight(image_lat, chan_image, gain, shift, dqo, dkv)
    dqo_tok, in_part = lax.optimization_barrier((dqo_tok, in_part))
    dqo_tok = dqo_tok.reshape(HEADS, images, 128, 128)
    mixed, att = mix(own, dqo_tok, lat, halves_out)
    out_part = out_weight(own, att, swapped(att, "own"), cot, cot_far)
    dkv_tok, out_part, in_part = lax.optimization_barrier((dkv_tok, out_part, in_part))
    in_blocks = exchanged(in_part, ALL)
    dkv_tok = dkv_tok.reshape(HEADS, images, 128, 128)
    grad_latent, grad_out = tail(
        out_part, dqo_tok, dkv_tok, proj_qkv, other_qkv, lat, cot, chan, gain, count
    )

    summed = jnp.sum(in_blocks.reshape(HEADS, 8, 16, 128).astype(F32), axis=1)
    dq = summed[:, 10:15].reshape(HEADS, 5, 2, HEAD).transpose(2, 1, 0, 3).reshape(10, HEADS * HEAD)
    dk = summed[:, :10, :HEAD].transpose(1, 0, 2).reshape(10, HEADS * HEAD)
    dv = summed[:, :10, HEAD:].transpose(1, 0, 2).reshape(10, HEADS * HEAD)
    grad_qkv = jnp.concatenate([dq, dk, dv], axis=1)
    return (mixed.transpose(1, 0, 2), grad_latent.transpose(1, 0, 2), grad_qkv, grad_out)


def solution(mesh):
    fine = Mesh(mesh.devices.reshape(4, 4, 2, 2, 2), ALL)
    tokens = P(SEQ, ("rep", "own"), None)
    return jax.shard_map(
        shards,
        mesh=fine,
        in_specs=(tokens, tokens, P(), P(), P("own", None), P("own", None)),
        out_specs=(tokens, tokens, P(ALL, None), P(ALL, None)),
        check_vma=False,
    )
```

```python
import functools

import jax
import jax.numpy as jnp
from jax import lax
from jax.experimental import pallas as pl
from jax.experimental.pallas import tpu as pltpu
from jax.sharding import Mesh
from jax.sharding import PartitionSpec as P

HEADS = 16
HEAD = 64
GROUPS = 32
SCALE = HEAD ** (-0.5)
SEQ = ("y", "z", "xl")
ALL = ("y", "z", "xl", "rep", "own")
F32, BF16 = jnp.float32, jnp.bfloat16
VMEM = 60 << 20


def place():
    return tuple(lax.axis_index(axis) for axis in ALL)


def members(channels):
    channel = lax.broadcasted_iota(jnp.int32, (channels, 128), 0)
    group = lax.broadcasted_iota(jnp.int32, (channels, 128), 1)
    first = group * (channels // GROUPS)
    return ((channel >= first) & (channel < first + channels // GROUPS)).astype(F32)


def by_group(rows, table):
    return lax.dot_general(
        rows, table, (((1,), (0,)), ((), ())),
        precision=lax.Precision.HIGHEST, preferred_element_type=F32,
    )


def by_channel(rows, table):
    return lax.dot_general(
        rows, table, (((1,), (1,)), ((), ())),
        precision=lax.Precision.HIGHEST, preferred_element_type=F32,
    )


def four_rows(rows):
    width = rows[0].shape[1]
    return jnp.concatenate([*rows, jnp.zeros((4, width), F32)], axis=0)


def stats_kernel(lat_ref, out_ref):
    values = [lat_ref[i].astype(F32) for i in range(2)]
    rows = [jnp.sum(v, axis=0, keepdims=True) for v in values]
    rows += [jnp.sum(v * v, axis=0, keepdims=True) for v in values]
    out_ref[...] = jnp.broadcast_to(by_group(four_rows(rows), members(lat_ref.shape[2]))[None], out_ref.shape)


def stats(lat, copies):
    return pl.pallas_call(
        stats_kernel,
        out_shape=jax.ShapeDtypeStruct((copies, 8, 128), F32),
        compiler_params=pltpu.CompilerParams(vmem_limit_bytes=VMEM),
        cost_estimate=pl.CostEstimate(flops=1 << 20, bytes_accessed=lat.size * 2, transcendentals=0),
    )(lat)


def moments(sums, count):
    means = sums / count
    var = means[2:4] - means[0:2] * means[0:2]
    return jnp.concatenate([means[0:2], lax.rsqrt(var + 1e-06), jnp.zeros((4, 128), F32)], axis=0)


def project_kernel(
    count, lat_ref, sums_ref, gain_ref, shift_ref, g_ref, mine_ref, other_ref,
    chan_ref, out_ref, normed_ref, send_ref, send_sem, recv_sem, keep_sem,
):
    here = place()
    own = here[4]
    half = mine_ref.shape[0]
    inner = HEADS * HEAD
    line = (here[0] * 4 + here[1]) * 2 + here[2]
    seqs = out_ref.shape[0]

    def device(at):
        return {"y": at // 8, "z": (at // 2) % 4, "xl": at % 2}

    barrier = pltpu.get_barrier_semaphore()

    @pl.loop(1, seqs)
    def _(k):
        to = lax.rem(line + k, seqs)
        pl.semaphore_signal(barrier, inc=1, device_id=device(to), device_id_type=pl.DeviceIdType.MESH)

    table = members(lat_ref.shape[2])
    chan = by_channel(moments(jnp.sum(sums_ref[...], axis=0), count), table)
    chan_ref[...] = chan
    for i in range(2):
        centred = (lat_ref[i].astype(F32) - chan[i : i + 1]) * chan[2 + i : 3 + i]
        normed_ref[i * 128 : (i + 1) * 128] = (centred * gain_ref[...] + shift_ref[...]).astype(BF16)
    near = normed_ref[:, pl.ds(pl.multiple_of(own * half, 128), half)]
    far = normed_ref[:, pl.ds(pl.multiple_of((1 - own) * half, 128), half)]
    low = lax.broadcasted_iota(jnp.int32, (128, 128), 1) < HEAD

    def copy(row, column):
        at = row * 8 + column
        return pltpu.make_async_remote_copy(
            src_ref=send_ref.at[at], dst_ref=out_ref.at[line],
            send_sem=send_sem.at[at], recv_sem=recv_sem.at[line],
            device_id=device(at), device_id_type=pl.DeviceIdType.MESH,
        )

    def arrival(at):
        return pltpu.make_async_remote_copy(
            src_ref=send_ref.at[at], dst_ref=out_ref.at[at],
            send_sem=send_sem.at[at], recv_sem=recv_sem.at[at],
            device_id=device(at), device_id_type=pl.DeviceIdType.MESH,
        )

    def block_row(row):
        lanes = [pl.ds(pl.multiple_of(p * inner + row * 256, 256), 256) for p in range(3)]
        query, key, value = [
            jnp.dot(near, mine_ref[:, at], preferred_element_type=F32)
            + jnp.dot(far, other_ref[:, at], preferred_element_type=F32)
            for at in lanes
        ]
        for h in range(0, 4, 2):
            for i in range(2):
                rows, part = slice(i * 128, (i + 1) * 128), slice(h * HEAD, (h + 2) * HEAD)
                q, k, v = query[rows, part], key[rows, part], value[rows, part]
                k_roll, v_roll = pltpu.roll(k, HEAD, 1), pltpu.roll(v, HEAD, 1)
                first, second = q[:64], q[64:]
                one, two = row * 8 + h * 2 + i, row * 8 + (h + 1) * 2 + i
                send_ref[one, :128] = jnp.where(low, k, v_roll).astype(BF16)
                send_ref[two, :128] = jnp.where(low, k_roll, v).astype(BF16)
                send_ref[one, 128:192] = jnp.where(low[:64], first, pltpu.roll(second, HEAD, 1)).astype(BF16)
                send_ref[two, 128:192] = jnp.where(low[:64], pltpu.roll(first, HEAD, 1), second).astype(BF16)
                send_ref[one, 192:256] = g_ref[row * 4 + h, i]
                send_ref[two, 192:256] = g_ref[row * 4 + h + 1, i]

    pl.semaphore_wait(barrier, seqs - 1)
    for j in range(4):
        row = (here[0] + (j + 1)) % 4
        block_row(row)
        if j < 3:
            @pl.loop(0, 8)
            def _(k):
                copy(row, (here[1] * 2 + here[2] + k) % 8).start()
        else:
            @pl.loop(1, 8)
            def _(k):
                copy(row, (here[1] * 2 + here[2] + k) % 8).start()

    keep = pltpu.make_async_copy(send_ref.at[line], out_ref.at[line], keep_sem)
    keep.start()

    @pl.loop(1, seqs)
    def _(k):
        arrival(lax.rem(line + k, seqs)).wait()

    keep.wait()


def project(lat, sums, gain, shift, g, mine, other, count):
    channels = lat.shape[2]
    seqs = sums.shape[0]
    dma = pltpu.SemaphoreType.DMA
    whole = pl.BlockSpec(memory_space=pltpu.VMEM)
    return pl.pallas_call(
        functools.partial(project_kernel, count),
        in_specs=[whole] * 7,
        out_specs=[whole, pl.BlockSpec(memory_space=pl.ANY)],
        out_shape=[
            jax.ShapeDtypeStruct((8, channels), F32),
            jax.ShapeDtypeStruct((seqs, 256, 128), BF16),
        ],
        scratch_shapes=[
            pltpu.VMEM((256, channels), BF16),
            pltpu.VMEM((seqs, 256, 128), BF16),
            dma((seqs,)), dma((seqs,)), dma,
        ],
        compiler_params=pltpu.CompilerParams(vmem_limit_bytes=VMEM, collective_id=2, has_side_effects=True),
        cost_estimate=pl.CostEstimate(flops=2 << 34, bytes_accessed=12 << 20, transcendentals=0),
    )(lat, sums, gain, shift, g, mine, other)


def attended_grad_kernel(own_ref, cot_ref, w_ref, out_ref):
    rows = cot_ref[...].reshape(256, cot_ref.shape[2])
    grad = lax.dot_general(rows, w_ref[...], (((1,), (1,)), ((), ())), preferred_element_type=F32)
    low = lax.broadcasted_iota(jnp.int32, (64, 128), 1) < HEAD
    for h in range(0, grad.shape[1] // HEAD, 2):
        for i in range(2):
            first = grad[i * 128 : i * 128 + 64, h * HEAD : (h + 2) * HEAD]
            second = grad[i * 128 + 64 : (i + 1) * 128, h * HEAD : (h + 2) * HEAD]
            out_ref[h, i] = jnp.where(low, first, pltpu.roll(second, HEAD, 1)).astype(BF16)
            out_ref[h + 1, i] = jnp.where(low, pltpu.roll(first, HEAD, 1), second).astype(BF16)


def attended_grad(own, cot, halves):
    channels = cot.shape[2]
    per = halves.shape[1] // 256

    return pl.pallas_call(
        attended_grad_kernel,
        grid_spec=pltpu.PrefetchScalarGridSpec(
            num_scalar_prefetch=1,
            grid=(2 * per,),
            in_specs=[
                pl.BlockSpec(cot.shape, lambda s, own: (0, 0, 0)),
                pl.BlockSpec((None, 256, channels), lambda s, own: (s // per, s % per, 0)),
            ],
            out_specs=pl.BlockSpec(
                (4, 2, 64, 128),
                lambda s, own: ((s // per + own[0] - 2 * own[0] * (s // per)) * per + s % per, 0, 0, 0),
            ),
        ),
        out_shape=jax.ShapeDtypeStruct((HEADS, 2, 64, 128), BF16),
        compiler_params=pltpu.CompilerParams(vmem_limit_bytes=VMEM),
        cost_estimate=pl.CostEstimate(flops=2 * 256 * 1280 * 1024, bytes_accessed=4 << 20, transcendentals=0),
    )(own, cot, halves)


def attention_kernel(
    ck, kvq_ref, dqo_ref, dkv_ref, tok_ref, s_ref, x_ref, y_ref, acc_ref, send_ref, send_sem, recv_sem, keep_sem
):
    here_at = place()
    line = (here_at[0] * 4 + here_at[1]) * 2 + here_at[2]

    def device(at):
        return {"y": at // 8, "z": (at // 2) % 4, "xl": at % 2}

    def copy(at):
        return pltpu.make_async_remote_copy(
            src_ref=send_ref.at[at], dst_ref=tok_ref.at[line],
            send_sem=send_sem.at[at], recv_sem=recv_sem.at[line],
            device_id=device(at), device_id_type=pl.DeviceIdType.MESH,
        )

    def arrival(at):
        return pltpu.make_async_remote_copy(
            src_ref=send_ref.at[at], dst_ref=tok_ref.at[at],
            send_sem=send_sem.at[at], recv_sem=recv_sem.at[at],
            device_id=device(at), device_id_type=pl.DeviceIdType.MESH,
        )

    def keep():
        return pltpu.make_async_copy(send_ref.at[line], tok_ref.at[line], keep_sem)

    step, last = pl.program_id(0), pl.num_programs(0) - 1
    sources, _, width = kvq_ref.shape
    keys = sources * 128
    here = dqo_ref.shape[0]
    base = lax.rem(line // here * here + (step + 1) * here, sources)
    rows = here * 128
    half = rows // 2

    @pl.when(step == 0)
    def _():
        acc_ref[...] = jnp.zeros_like(acc_ref)
        barrier = pltpu.get_barrier_semaphore()

        @pl.loop(1, sources)
        def _(k):
            to = lax.rem(line + k, sources)
            pl.semaphore_signal(barrier, inc=1, device_id=device(to), device_id_type=pl.DeviceIdType.MESH)

        pl.semaphore_wait(barrier, sources - 1)

    low = lax.broadcasted_iota(jnp.int32, (half, width), 1) < HEAD
    xq = kvq_ref[pl.ds(base, here), 128:192, :].reshape(half, width).astype(F32) * SCALE
    xg = kvq_ref[pl.ds(base, here), 192:256, :].reshape(half, width).astype(F32)
    zero = jnp.zeros_like(xq)
    y_ref[0 * half : 1 * half] = jnp.where(low, xq, zero).astype(BF16)
    y_ref[1 * half : 2 * half] = jnp.where(low, pltpu.roll(xq, HEAD, 1), zero).astype(BF16)
    y_ref[2 * half : 3 * half] = jnp.where(low, zero, pltpu.roll(xg, HEAD, 1)).astype(BF16)
    y_ref[3 * half : 4 * half] = jnp.where(low, zero, xg).astype(BF16)
    y = y_ref[...]
    spans = [(c, c + ck) for c in range(0, keys, ck)]

    def kv_chunk(a, b):
        return kvq_ref[a // 128 : b // 128, :128, :].reshape(b - a, width)

    top = None
    for a, b in spans:
        both = lax.dot_general(y, kv_chunk(a, b), (((1,), (1,)), ((), ())), preferred_element_type=F32)
        s_ref[:, a:b] = both
        for t in range(0, ck, 128):
            piece = both[:rows, t : t + 128]
            top = piece if top is None else jnp.maximum(top, piece)
    top = jnp.max(top, axis=1, keepdims=True)
    total = jnp.zeros((rows, 128), F32)
    delta = jnp.zeros((rows, 128), F32)
    for a, b in spans:
        weights = jnp.exp(s_ref[:rows, a:b] - top)
        s_ref[:rows, a:b] = weights
        fold = weights * s_ref[rows:, a:b]
        for t in range(0, ck, 128):
            total = total + weights[:, t : t + 128]
            delta = delta + fold[:, t : t + 128]
    inverse = 1.0 / jnp.sum(total, axis=1, keepdims=True)
    delta = jnp.sum(delta, axis=1, keepdims=True) * inverse
    out = jnp.zeros((2 * rows, width), F32)
    for a, b in spans:
        probs = s_ref[:rows, a:b] * inverse
        x_ref[rows:, a:b] = probs.astype(BF16)
        x_ref[:rows, a:b] = (probs * (s_ref[rows:, a:b] - delta)).astype(BF16)
        x = x_ref[:, a:b]
        out = out + jnp.dot(x, kv_chunk(a, b), preferred_element_type=F32)
        acc_ref[a:b, :] += lax.dot_general(x, y, (((0,), (0,)), ((), ())), preferred_element_type=F32)
    lows = lax.broadcasted_iota(jnp.int32, (rows, width), 1) < HEAD
    res = jnp.where(lows, out[:rows] * SCALE, out[rows:]).astype(BF16)
    for h in range(2):
        for a in range(here):
            at = h * half + a * 64
            dqo_ref[a, h * 64 : (h + 1) * 64, :] = res[at : at + 64]
            send_ref[base + a, h * 64 : (h + 1) * 64, :] = res[at : at + 64]

    for a in range(here):
        @pl.when(base + a != line)
        def _():
            copy(base + a).start()

        @pl.when(base + a == line)
        def _():
            keep().start()

    @pl.when(step == last)
    def _():
        dkv_ref[...] = acc_ref[...].reshape(sources, 128, width).astype(BF16)

        @pl.loop(1, sources)
        def _(k):
            arrival(lax.rem(line + k, sources)).wait()

        keep().wait()


def attention(kvq, here=2, ck=1024):
    sources = kvq.shape[0]
    keys, rows = sources * 128, here * 128
    dma = pltpu.SemaphoreType.DMA

    def block(i):
        here_at = place()
        line = (here_at[0] * 4 + here_at[1]) * 2 + here_at[2]
        return lax.rem(line // here + i + 1, sources // here), 0, 0

    return pl.pallas_call(
        functools.partial(attention_kernel, ck),
        grid=(sources // here,),
        in_specs=[
            pl.BlockSpec((sources, 256, 128), lambda i: (0, 0, 0), pipeline_mode=pl.Buffered(1)),
        ],
        out_specs=[
            pl.BlockSpec((here, 128, 128), block),
            pl.BlockSpec((sources, 128, 128), lambda i: (0, 0, 0)),
            pl.BlockSpec(memory_space=pl.ANY),
        ],
        out_shape=[
            jax.ShapeDtypeStruct((sources, 128, 128), BF16),
            jax.ShapeDtypeStruct((sources, 128, 128), BF16),
            jax.ShapeDtypeStruct((sources, 128, 128), BF16),
        ],
        scratch_shapes=[
            pltpu.VMEM((2 * rows, keys), F32),
            pltpu.VMEM((2 * rows, keys), BF16),
            pltpu.VMEM((2 * rows, 128), BF16),
            pltpu.VMEM((keys, 128), F32),
            pltpu.VMEM((sources, 128, 128), BF16),
            dma((sources,)), dma((sources,)), dma,
        ],
        compiler_params=pltpu.CompilerParams(vmem_limit_bytes=VMEM, collective_id=3, has_side_effects=True),
        cost_estimate=pl.CostEstimate(flops=48 * keys * keys * HEAD, bytes_accessed=4 << 20, transcendentals=keys * keys),
    )(kvq)


def in_weight_kernel(lat_ref, chan_ref, gain_ref, shift_ref, dqo_ref, dkv_ref, out_ref, acc_ref, turned_ref, block_ref):
    step, last = pl.program_id(0), pl.num_programs(0) - 1
    sources, _, channels = lat_ref.shape
    rows = sources * 128

    @pl.when(step == 0)
    def _():
        acc_ref[...] = jnp.zeros_like(acc_ref)

    lat = lat_ref[...].reshape(rows, channels).astype(F32)
    centred = (lat - chan_ref[0:1]) * chan_ref[1:2]
    normed = (centred * gain_ref[...] + shift_ref[...]).astype(BF16)
    grads = jnp.concatenate(
        [dqo_ref[...].reshape(rows, 128), dkv_ref[...].reshape(rows, 128)], axis=1
    )
    acc_ref[...] += lax.dot_general(grads, normed, (((0,), (0,)), ((), ())), preferred_element_type=F32)

    @pl.when(step == last)
    def _():
        turned_ref[...] = acc_ref[...].T
        low = lax.broadcasted_iota(jnp.int32, (5, 128), 1) < HEAD
        for d in range(channels // 10):
            at = d * 10
            block_ref[0:10] = turned_ref[at : at + 10, 128:256]
            first, second = turned_ref[at : at + 5, 0:128], turned_ref[at + 5 : at + 10, 0:128]
            block_ref[10:15] = jnp.where(low, first, pltpu.roll(second, HEAD, 1))
            block_ref[15:16] = jnp.zeros((1, 128), F32)
            out_ref[d] = block_ref[...].astype(BF16)


def in_weight(lat, chan, gain, shift, dqo, dkv, here=4):
    sources, _, channels = lat.shape
    return pl.pallas_call(
        in_weight_kernel,
        grid=(sources // here,),
        in_specs=[
            pl.BlockSpec((here, 128, channels), lambda i: (i, 0, 0)),
            pl.BlockSpec((2, channels), lambda i: (0, 0)),
            pl.BlockSpec((1, channels), lambda i: (0, 0)),
            pl.BlockSpec((1, channels), lambda i: (0, 0)),
            pl.BlockSpec((here, 128, 128), lambda i: (i, 0, 0)),
            pl.BlockSpec((here, 128, 128), lambda i: (i, 0, 0)),
        ],
        out_specs=pl.BlockSpec((channels // 10, 16, 128), lambda i: (0, 0, 0)),
        out_shape=jax.ShapeDtypeStruct((channels // 10, 16, 128), BF16),
        scratch_shapes=[
            pltpu.VMEM((256, channels), F32), pltpu.VMEM((channels, 256), F32), pltpu.VMEM((16, 128), F32),
        ],
        compiler_params=pltpu.CompilerParams(vmem_limit_bytes=VMEM),
        cost_estimate=pl.CostEstimate(flops=2 * 4096 * 1280 * 256, bytes_accessed=14 << 20, transcendentals=0),
    )(lat, chan, gain, shift, dqo, dkv)


def paired(first, second, low, upper):
    if upper:
        return jnp.where(low, pltpu.roll(first.astype(F32), HEAD, 1), second.astype(F32)).astype(BF16)
    return jnp.where(low, first.astype(F32), pltpu.roll(second.astype(F32), HEAD, 1)).astype(BF16)


def shifted(here, k, sign):
    dy, dz, dx = k // 8, (k // 2) % 4, k % 2
    y = (here[0] + (dy if sign > 0 else 4 - dy)) % 4
    z = (here[1] + (dz if sign > 0 else 4 - dz)) % 4
    x = (here[2] + dx) % 2
    return {"y": y, "z": z, "xl": x}, (y * 4 + z) * 2 + x


def tail_kernel(
    count, dqo_ref, dkv_ref, mine_ref, other_ref, halves_ref, lat_ref, cot_ref, cot_far_ref, chan_ref, gain_ref,
    out_ref, weight_ref, mixed_ref, rows_ref, grad_ref, near_ref, far_ref, got_ref, part_ref, att_ref, att_far_ref,
    give_ref, take_ref, part_send, part_recv, sums_send, sums_recv, att_send, att_recv, give_send, give_recv,
):
    here = place()
    own = here[4]
    seqs = far_ref.shape[0]
    line = (here[0] * 4 + here[1]) * 2 + here[2]
    mesh_id = pl.DeviceIdType.MESH

    barrier = pltpu.get_barrier_semaphore()

    @pl.loop(1, seqs)
    def _(k):
        pl.semaphore_signal(barrier, inc=1, device_id=shifted(here, k, 1)[0], device_id_type=mesh_id)

    pl.semaphore_signal(barrier, inc=1, device_id={"own": 1 - own}, device_id_type=mesh_id)
    pl.semaphore_signal(barrier, inc=1, device_id={"rep": 1 - here[3]}, device_id_type=mesh_id)
    pl.semaphore_wait(barrier, seqs + 1)

    def pair(at):
        return pl.ds(at * 2, 2)

    def part_copy(k):
        target, there = shifted(here, k, 1)
        return pltpu.make_async_remote_copy(
            src_ref=part_ref.at[pair(there)], dst_ref=got_ref.at[pair(line)],
            send_sem=part_send.at[k], recv_sem=part_recv.at[k],
            device_id=target, device_id_type=mesh_id,
        )

    def part_arrival(k):
        source, there = shifted(here, k, -1)
        return pltpu.make_async_remote_copy(
            src_ref=part_ref.at[pair(there)], dst_ref=got_ref.at[pair(there)],
            send_sem=part_send.at[k], recv_sem=part_recv.at[k],
            device_id=source, device_id_type=mesh_id,
        )

    def sums_copy(k):
        target, _ = shifted(here, k, 1)
        return pltpu.make_async_remote_copy(
            src_ref=near_ref, dst_ref=far_ref.at[line],
            send_sem=sums_send.at[k], recv_sem=sums_recv.at[k],
            device_id=target, device_id_type=mesh_id,
        )

    def sums_arrival(k):
        source, there = shifted(here, k, -1)
        return pltpu.make_async_remote_copy(
            src_ref=near_ref, dst_ref=far_ref.at[there],
            send_sem=sums_send.at[k], recv_sem=sums_recv.at[k],
            device_id=source, device_id_type=mesh_id,
        )

    inner, half = HEADS * HEAD, mine_ref.shape[0]
    low = lax.broadcasted_iota(jnp.int32, (128, 128), 1) < HEAD
    for h in range(0, HEADS, 2):
        for i in range(2):
            att_ref[i * 128 : (i + 1) * 128, h * HEAD : (h + 2) * HEAD] = paired(dqo_ref[h, i], dqo_ref[h + 1, i], low, True)
    swap = pltpu.make_async_remote_copy(
        src_ref=att_ref, dst_ref=att_far_ref, send_sem=att_send, recv_sem=att_recv,
        device_id={"own": 1 - own}, device_id_type=pl.DeviceIdType.MESH,
    )
    swap.start()
    wide = halves_ref.shape[1]
    near = att_ref[:, pl.ds(pl.multiple_of(own * wide, 128), wide)]
    far = att_ref[:, pl.ds(pl.multiple_of((1 - own) * wide, 128), wide)]
    total = jnp.dot(near, halves_ref[0], preferred_element_type=F32)
    total = total + jnp.dot(far, halves_ref[1], preferred_element_type=F32)
    for i in range(2):
        mixed_ref[i] = (lat_ref[i].astype(F32) + total[i * 128 : (i + 1) * 128]).astype(BF16)
    swap.wait()
    channels = cot_ref.shape[2]
    cot, cot_far = cot_ref[...].reshape(256, channels), cot_far_ref[...].reshape(256, channels)
    for j in range(4):
        row = (here[0] + (j + 1)) % 4
        at = pl.ds(pl.multiple_of(row * 256, 256), 256)
        total = lax.dot_general(att_ref[:, at], cot, (((0,), (0,)), ((), ())), preferred_element_type=F32)
        total = total + lax.dot_general(
            att_far_ref[:, at], cot_far, (((0,), (0,)), ((), ())), preferred_element_type=F32
        )
        blocks = total.reshape(16, 2, 8, channels)
        part_ref[pl.ds(row * 16, 16)] = jnp.where(own == 0, blocks[:, 0], blocks[:, 1]).astype(BF16)

        @pl.loop(0 if j < 3 else 1, 8)
        def _(k):
            part_copy(((j + 1) % 4) * 8 + k).start()

    for h in range(0, HEADS, 2):
        for i in range(2):
            rows, at = slice(i * 128, (i + 1) * 128), h * HEAD
            dq, dk = (dqo_ref[h, i], dqo_ref[h + 1, i]), (dkv_ref[h, i], dkv_ref[h + 1, i])
            rows_ref[rows, at : at + 128] = paired(*dq, low, False)
            rows_ref[rows, inner + at : inner + at + 128] = paired(*dk, low, False)
            rows_ref[rows, 2 * inner + at : 2 * inner + at + 128] = paired(*dk, low, True)
    grads = rows_ref[...]
    for side, w_ref in ((own, mine_ref), (1 - own, other_ref)):
        part = lax.dot_general(grads, w_ref[...], (((1,), (1,)), ((), ())), preferred_element_type=F32)
        lanes = pl.ds(pl.multiple_of(side * half, 128), half)
        for i in range(2):
            grad_ref[i, :, lanes] = part[i * 128 : (i + 1) * 128]
    ones, twos = [], []
    for i in range(2):
        grad = grad_ref[i] * gain_ref[...]
        grad_ref[i] = grad
        centred = (lat_ref[i].astype(F32) - chan_ref[i : i + 1]) * chan_ref[2 + i : 3 + i]
        ones.append(jnp.sum(grad, axis=0, keepdims=True))
        twos.append(jnp.sum(grad * centred, axis=0, keepdims=True))
    table = members(lat_ref.shape[2])
    sums = by_group(four_rows(ones + twos), table)
    near_ref[...] = sums
    far_ref[line] = sums

    @pl.loop(1, seqs)
    def _(k):
        sums_copy(k).start()

    got_ref[pair(line)] = part_ref[pair(line)]

    @pl.loop(1, seqs)
    def _(k):
        sums_arrival(k).wait_recv()

    means = by_channel(jnp.sum(far_ref[...], axis=0) / count, table)
    for i in range(2):
        inv = chan_ref[2 + i : 3 + i]
        centred = (lat_ref[i].astype(F32) - chan_ref[i : i + 1]) * inv
        grad = inv * (grad_ref[i] - means[i : i + 1] - centred * means[2 + i : 3 + i])
        out_ref[i] = (cot_ref[i].astype(F32) + grad).astype(BF16)

    @pl.loop(1, seqs)
    def _(k):
        part_arrival(k).wait_recv()

    total = got_ref[0:8].astype(F32)
    for k in range(8, 2 * seqs, 8):
        total = total + got_ref[k : k + 8].astype(F32)
    pairs = jnp.sum(total.reshape(4, 2, 8, channels), axis=0)
    upper = here[3] == 1
    give_ref[...] = jnp.where(upper, pairs[0], pairs[1])
    give = pltpu.make_async_remote_copy(
        src_ref=give_ref, dst_ref=take_ref, send_sem=give_send, recv_sem=give_recv,
        device_id={"rep": 1 - here[3]}, device_id_type=mesh_id,
    )
    give.start()
    give.wait()
    weight_ref[...] = jnp.where(upper, pairs[1], pairs[0]) + take_ref[...]

    @pl.loop(1, seqs)
    def _(k):
        part_copy(k).wait_send()

    @pl.loop(1, seqs)
    def _(k):
        sums_copy(k).wait_send()


def tail(dqo, dkv, mine, other, halves, lat, cot, cot_far, chan, gain, count):
    channels, wide = lat.shape[2], HEADS * HEAD
    seqs = wide // 32
    dma = pltpu.SemaphoreType.DMA
    return pl.pallas_call(
        functools.partial(tail_kernel, count),
        out_shape=[
            jax.ShapeDtypeStruct(lat.shape, BF16),
            jax.ShapeDtypeStruct((8, channels), F32),
            jax.ShapeDtypeStruct(lat.shape, BF16),
        ],
        scratch_shapes=[
            pltpu.VMEM((256, 3 * HEADS * HEAD), BF16),
            pltpu.VMEM(lat.shape, F32),
            pltpu.VMEM((8, 128), F32),
            pltpu.VMEM((seqs, 8, 128), F32),
            pltpu.VMEM((2 * seqs, 8, channels), BF16),
            pltpu.VMEM((2 * seqs, 8, channels), BF16),
            pltpu.VMEM((256, wide), BF16),
            pltpu.VMEM((256, wide), BF16),
            pltpu.VMEM((8, channels), F32),
            pltpu.VMEM((8, channels), F32),
            dma((seqs,)), dma((seqs,)), dma((seqs,)), dma((seqs,)), dma, dma, dma, dma,
        ],
        compiler_params=pltpu.CompilerParams(vmem_limit_bytes=VMEM, collective_id=1, has_side_effects=True),
        cost_estimate=pl.CostEstimate(flops=2 << 34, bytes_accessed=16 << 20, transcendentals=0),
    )(dqo, dkv, mine, other, halves, lat, cot, cot_far, chan, gain)


def swapped(value, axis):
    return lax.ppermute(value, axis, [(0, 1), (1, 0)])


def exchanged(value, axes):
    return lax.all_to_all(value, axes, 0, 0, tiled=True)


def shards(latent, cotangent, norm_gain, norm_shift, proj_qkv, proj_out):
    local_len, images, channels = latent.shape
    seq_count = lax.axis_size(SEQ)
    count = local_len * seq_count * (channels // GROUPS)
    own = lax.axis_index("own").reshape(1)
    gain, shift = norm_gain.reshape(1, channels), norm_shift.reshape(1, channels)

    other_out = swapped(proj_out, "own")
    other_qkv = swapped(proj_qkv, "own")
    lat = latent.transpose(1, 0, 2)
    sums = exchanged(stats(lat, seq_count), SEQ)
    cot = cotangent.transpose(1, 0, 2)
    image = lax.axis_index("xl")
    near = jnp.where(image == 0, lat[0], lat[1])
    far = swapped(jnp.where(image == 0, lat[1], lat[0]), "xl")
    pair_lat = jnp.where(image == 0, jnp.stack([near, far]), jnp.stack([far, near]))
    halves_out = jnp.stack([proj_out, other_out])
    cot_far = swapped(cot, "own")
    g = attended_grad(own, cot, halves_out)
    pair_lat, g = lax.optimization_barrier((pair_lat, g))
    chan, kvqg = project(lat, sums, gain, shift, g, proj_qkv, other_qkv, count)
    pair_lat, kvqg = lax.optimization_barrier((pair_lat, kvqg))
    image_lat = lax.all_gather(pair_lat, ("y", "z"), tiled=True)

    dqo, dkv, dqo_tok = attention(kvqg)

    dkv_tok = exchanged(dkv, SEQ)
    chan_image = jnp.where(image == 0, chan[0:4:2], chan[1:4:2])
    in_part = in_weight(image_lat, chan_image, gain, shift, dqo, dkv)
    dqo_tok, in_part = lax.optimization_barrier((dqo_tok, in_part))
    dqo_tok = dqo_tok.reshape(HEADS, images, 128, 128)
    dkv_tok, in_part = lax.optimization_barrier((dkv_tok, in_part))
    in_blocks = exchanged(in_part, ALL)
    dkv_tok = dkv_tok.reshape(HEADS, images, 128, 128)
    grad_latent, grad_out, mixed = tail(
        dqo_tok, dkv_tok, proj_qkv, other_qkv, halves_out, lat, cot, cot_far, chan, gain, count
    )

    summed = jnp.sum(in_blocks.reshape(HEADS, 8, 16, 128).astype(F32), axis=1)
    dq = summed[:, 10:15].reshape(HEADS, 5, 2, HEAD).transpose(2, 1, 0, 3).reshape(10, HEADS * HEAD)
    dk = summed[:, :10, :HEAD].transpose(1, 0, 2).reshape(10, HEADS * HEAD)
    dv = summed[:, :10, HEAD:].transpose(1, 0, 2).reshape(10, HEADS * HEAD)
    grad_qkv = jnp.concatenate([dq, dk, dv], axis=1)
    return (mixed.transpose(1, 0, 2), grad_latent.transpose(1, 0, 2), grad_qkv, grad_out)


def solution(mesh):
    fine = Mesh(mesh.devices.reshape(4, 4, 2, 2, 2), ALL)
    tokens = P(SEQ, ("rep", "own"), None)
    return jax.shard_map(
        shards,
        mesh=fine,
        in_specs=(tokens, tokens, P(), P(), P("own", None), P("own", None)),
        out_specs=(tokens, tokens, P(ALL, None), P(ALL, None)),
        check_vma=False,
    )
```

```python
import functools

import jax
import jax.numpy as jnp
from jax import lax
from jax.experimental import pallas as pl
from jax.experimental.pallas import tpu as pltpu
from jax.sharding import Mesh
from jax.sharding import PartitionSpec as P

HEADS = 16
HEAD = 64
GROUPS = 32
SCALE = HEAD ** (-0.5)
SEQ = ("y", "z", "xl")
ALL = ("y", "z", "xl", "rep", "own")
F32, BF16 = jnp.float32, jnp.bfloat16
VMEM = 60 << 20


def place():
    return tuple(lax.axis_index(axis) for axis in ALL)


def members(channels):
    channel = lax.broadcasted_iota(jnp.int32, (channels, 128), 0)
    group = lax.broadcasted_iota(jnp.int32, (channels, 128), 1)
    first = group * (channels // GROUPS)
    return ((channel >= first) & (channel < first + channels // GROUPS)).astype(F32)


def by_group(rows, table):
    return lax.dot_general(
        rows, table, (((1,), (0,)), ((), ())),
        precision=lax.Precision.HIGHEST, preferred_element_type=F32,
    )


def by_channel(rows, table):
    return lax.dot_general(
        rows, table, (((1,), (1,)), ((), ())),
        precision=lax.Precision.HIGHEST, preferred_element_type=F32,
    )


def four_rows(rows):
    width = rows[0].shape[1]
    return jnp.concatenate([*rows, jnp.zeros((4, width), F32)], axis=0)


def moments(sums, count):
    means = sums / count
    var = means[2:4] - means[0:2] * means[0:2]
    return jnp.concatenate([means[0:2], lax.rsqrt(var + 1e-06), jnp.zeros((4, 128), F32)], axis=0)


def project_kernel(
    count, lat_ref, sums_ref, gain_ref, shift_ref, g_ref, mine_ref, other_ref,
    chan_ref, out_ref, normed_ref, send_ref, send_sem, recv_sem, keep_sem,
):
    here = place()
    own = here[4]
    half = mine_ref.shape[0]
    inner = HEADS * HEAD
    line = (here[0] * 4 + here[1]) * 2 + here[2]
    seqs = out_ref.shape[0]

    def device(at):
        return {"y": at // 8, "z": (at // 2) % 4, "xl": at % 2}

    barrier = pltpu.get_barrier_semaphore()

    @pl.loop(1, seqs)
    def _(k):
        to = lax.rem(line + k, seqs)
        pl.semaphore_signal(barrier, inc=1, device_id=device(to), device_id_type=pl.DeviceIdType.MESH)

    table = members(lat_ref.shape[2])
    chan = by_channel(moments(sums_ref[...], count), table)
    chan_ref[...] = chan
    for i in range(2):
        centred = (lat_ref[i].astype(F32) - chan[i : i + 1]) * chan[2 + i : 3 + i]
        normed_ref[i * 128 : (i + 1) * 128] = (centred * gain_ref[...] + shift_ref[...]).astype(BF16)
    near = normed_ref[:, pl.ds(pl.multiple_of(own * half, 128), half)]
    far = normed_ref[:, pl.ds(pl.multiple_of((1 - own) * half, 128), half)]
    low = lax.broadcasted_iota(jnp.int32, (128, 128), 1) < HEAD

    def copy(row, column):
        at = row * 8 + column
        return pltpu.make_async_remote_copy(
            src_ref=send_ref.at[at], dst_ref=out_ref.at[line],
            send_sem=send_sem.at[at], recv_sem=recv_sem.at[line],
            device_id=device(at), device_id_type=pl.DeviceIdType.MESH,
        )

    def arrival(at):
        return pltpu.make_async_remote_copy(
            src_ref=send_ref.at[at], dst_ref=out_ref.at[at],
            send_sem=send_sem.at[at], recv_sem=recv_sem.at[at],
            device_id=device(at), device_id_type=pl.DeviceIdType.MESH,
        )

    def block_row(row):
        lanes = [pl.ds(pl.multiple_of(p * inner + row * 256, 256), 256) for p in range(3)]
        query, key, value = [
            jnp.dot(near, mine_ref[:, at], preferred_element_type=F32)
            + jnp.dot(far, other_ref[:, at], preferred_element_type=F32)
            for at in lanes
        ]
        for h in range(0, 4, 2):
            for i in range(2):
                rows, part = slice(i * 128, (i + 1) * 128), slice(h * HEAD, (h + 2) * HEAD)
                q, k, v = query[rows, part], key[rows, part], value[rows, part]
                k_roll, v_roll = pltpu.roll(k, HEAD, 1), pltpu.roll(v, HEAD, 1)
                first, second = q[:64], q[64:]
                one, two = row * 8 + h * 2 + i, row * 8 + (h + 1) * 2 + i
                send_ref[one, :128] = jnp.where(low, k, v_roll).astype(BF16)
                send_ref[two, :128] = jnp.where(low, k_roll, v).astype(BF16)
                send_ref[one, 128:192] = jnp.where(low[:64], first, pltpu.roll(second, HEAD, 1)).astype(BF16)
                send_ref[two, 128:192] = jnp.where(low[:64], pltpu.roll(first, HEAD, 1), second).astype(BF16)
                send_ref[one, 192:256] = g_ref[row * 4 + h, i]
                send_ref[two, 192:256] = g_ref[row * 4 + h + 1, i]

    for j in range(4):
        row = (here[0] + (j + 1)) % 4
        block_row(row)
        if j == 0:
            pl.semaphore_wait(barrier, seqs - 1)
        if j < 3:
            @pl.loop(0, 8)
            def _(k):
                copy(row, (here[1] * 2 + here[2] + k) % 8).start()
        else:
            @pl.loop(1, 8)
            def _(k):
                copy(row, (here[1] * 2 + here[2] + k) % 8).start()

    keep = pltpu.make_async_copy(send_ref.at[line], out_ref.at[line], keep_sem)
    keep.start()

    @pl.loop(1, seqs)
    def _(k):
        arrival(lax.rem(line + k, seqs)).wait()

    keep.wait()


def project(lat, sums, gain, shift, g, mine, other, count):
    channels = lat.shape[2]
    seqs = g.shape[0] * 2
    dma = pltpu.SemaphoreType.DMA
    whole = pl.BlockSpec(memory_space=pltpu.VMEM)
    return pl.pallas_call(
        functools.partial(project_kernel, count),
        in_specs=[whole] * 7,
        out_specs=[whole, pl.BlockSpec(memory_space=pl.ANY)],
        out_shape=[
            jax.ShapeDtypeStruct((8, channels), F32),
            jax.ShapeDtypeStruct((seqs, 256, 128), BF16),
        ],
        scratch_shapes=[
            pltpu.VMEM((256, channels), BF16),
            pltpu.VMEM((seqs, 256, 128), BF16),
            dma((seqs,)), dma((seqs,)), dma,
        ],
        compiler_params=pltpu.CompilerParams(vmem_limit_bytes=VMEM, collective_id=2, has_side_effects=True),
        cost_estimate=pl.CostEstimate(flops=2 << 34, bytes_accessed=12 << 20, transcendentals=0),
    )(lat, sums, gain, shift, g, mine, other)


def first_kernel(
    lat_ref, cot_ref, mine_ref, other_ref, sums_ref, g_ref, near_ref, far_ref, sums_send, sums_recv
):
    here = place()
    own = here[4]
    seqs, channels = far_ref.shape[0], lat_ref.shape[2]
    line = (here[0] * 4 + here[1]) * 2 + here[2]
    mesh_id = pl.DeviceIdType.MESH
    barrier = pltpu.get_barrier_semaphore()

    @pl.loop(1, seqs)
    def _(k):
        pl.semaphore_signal(barrier, inc=1, device_id=shifted(here, k, 1)[0], device_id_type=mesh_id)

    values = [lat_ref[i].astype(F32) for i in range(2)]
    rows = [jnp.sum(v, axis=0, keepdims=True) for v in values]
    rows += [jnp.sum(v * v, axis=0, keepdims=True) for v in values]
    sums = by_group(four_rows(rows), members(channels))
    near_ref[...] = sums
    far_ref[line] = sums

    def sums_copy(k):
        target, _ = shifted(here, k, 1)
        return pltpu.make_async_remote_copy(
            src_ref=near_ref, dst_ref=far_ref.at[line],
            send_sem=sums_send.at[k], recv_sem=sums_recv.at[k],
            device_id=target, device_id_type=mesh_id,
        )

    def sums_arrival(k):
        source, there = shifted(here, k, -1)
        return pltpu.make_async_remote_copy(
            src_ref=near_ref, dst_ref=far_ref.at[there],
            send_sem=sums_send.at[k], recv_sem=sums_recv.at[k],
            device_id=source, device_id_type=mesh_id,
        )

    pl.semaphore_wait(barrier, seqs - 1)

    @pl.loop(1, seqs)
    def _(k):
        sums_copy(k).start()

    cot = cot_ref[...].reshape(256, channels)
    low = lax.broadcasted_iota(jnp.int32, (64, 128), 1) < HEAD
    half = mine_ref.shape[0] // HEAD
    for side, w_ref in ((own, mine_ref), (1 - own, other_ref)):
        grad = lax.dot_general(cot, w_ref[...], (((1,), (1,)), ((), ())), preferred_element_type=F32)
        for h in range(0, half, 2):
            for i in range(2):
                upper = grad[i * 128 : i * 128 + 64, h * HEAD : (h + 2) * HEAD]
                lower = grad[i * 128 + 64 : (i + 1) * 128, h * HEAD : (h + 2) * HEAD]
                g_ref[side * half + h, i] = jnp.where(low, upper, pltpu.roll(lower, HEAD, 1)).astype(BF16)
                g_ref[side * half + h + 1, i] = jnp.where(low, pltpu.roll(upper, HEAD, 1), lower).astype(BF16)

    @pl.loop(1, seqs)
    def _(k):
        sums_arrival(k).wait()

    sums_ref[...] = jnp.sum(far_ref[...], axis=0)


def first(lat, cot, mine, other):
    dma = pltpu.SemaphoreType.DMA
    return pl.pallas_call(
        first_kernel,
        out_shape=[
            jax.ShapeDtypeStruct((8, 128), F32),
            jax.ShapeDtypeStruct((HEADS, 2, 64, 128), BF16),
        ],
        scratch_shapes=[
            pltpu.VMEM((8, 128), F32),
            pltpu.VMEM((2 * HEADS, 8, 128), F32),
            dma((2 * HEADS,)), dma((2 * HEADS,)),
        ],
        compiler_params=pltpu.CompilerParams(vmem_limit_bytes=VMEM, collective_id=4, has_side_effects=True),
        cost_estimate=pl.CostEstimate(flops=2 << 32, bytes_accessed=6 << 20, transcendentals=0),
    )(lat, cot, mine, other)


def attention_kernel(
    ck, kvq_ref, dqo_ref, dkv_ref, tok_ref, s_ref, x_ref, y_ref, acc_ref, send_ref, send_sem, recv_sem, keep_sem
):
    here_at = place()
    line = (here_at[0] * 4 + here_at[1]) * 2 + here_at[2]

    def device(at):
        return {"y": at // 8, "z": (at // 2) % 4, "xl": at % 2}

    def copy(at):
        return pltpu.make_async_remote_copy(
            src_ref=send_ref.at[at], dst_ref=tok_ref.at[line],
            send_sem=send_sem.at[at], recv_sem=recv_sem.at[line],
            device_id=device(at), device_id_type=pl.DeviceIdType.MESH,
        )

    def arrival(at):
        return pltpu.make_async_remote_copy(
            src_ref=send_ref.at[at], dst_ref=tok_ref.at[at],
            send_sem=send_sem.at[at], recv_sem=recv_sem.at[at],
            device_id=device(at), device_id_type=pl.DeviceIdType.MESH,
        )

    def keep():
        return pltpu.make_async_copy(send_ref.at[line], tok_ref.at[line], keep_sem)

    step, last = pl.program_id(0), pl.num_programs(0) - 1
    sources, _, width = kvq_ref.shape
    keys = sources * 128
    here = dqo_ref.shape[0]
    base = lax.rem(line // here * here + (step + 1) * here, sources)
    rows = here * 128
    half = rows // 2

    @pl.when(step == 0)
    def _():
        acc_ref[...] = jnp.zeros_like(acc_ref)
        barrier = pltpu.get_barrier_semaphore()

        @pl.loop(1, sources)
        def _(k):
            to = lax.rem(line + k, sources)
            pl.semaphore_signal(barrier, inc=1, device_id=device(to), device_id_type=pl.DeviceIdType.MESH)

    low = lax.broadcasted_iota(jnp.int32, (half, width), 1) < HEAD
    xq = kvq_ref[pl.ds(base, here), 128:192, :].reshape(half, width).astype(F32) * SCALE
    xg = kvq_ref[pl.ds(base, here), 192:256, :].reshape(half, width).astype(F32)
    zero = jnp.zeros_like(xq)
    y_ref[0 * half : 1 * half] = jnp.where(low, xq, zero).astype(BF16)
    y_ref[1 * half : 2 * half] = jnp.where(low, pltpu.roll(xq, HEAD, 1), zero).astype(BF16)
    y_ref[2 * half : 3 * half] = jnp.where(low, zero, pltpu.roll(xg, HEAD, 1)).astype(BF16)
    y_ref[3 * half : 4 * half] = jnp.where(low, zero, xg).astype(BF16)
    y = y_ref[...]
    spans = [(c, c + ck) for c in range(0, keys, ck)]

    def kv_chunk(a, b):
        return kvq_ref[a // 128 : b // 128, :128, :].reshape(b - a, width)

    top = None
    for a, b in spans:
        both = lax.dot_general(y, kv_chunk(a, b), (((1,), (1,)), ((), ())), preferred_element_type=F32)
        s_ref[:, a:b] = both
        for t in range(0, ck, 128):
            piece = both[:rows, t : t + 128]
            top = piece if top is None else jnp.maximum(top, piece)
    top = jnp.max(top, axis=1, keepdims=True)
    total = jnp.zeros((rows, 128), F32)
    delta = jnp.zeros((rows, 128), F32)
    for a, b in spans:
        weights = jnp.exp(s_ref[:rows, a:b] - top)
        s_ref[:rows, a:b] = weights
        fold = weights * s_ref[rows:, a:b]
        for t in range(0, ck, 128):
            total = total + weights[:, t : t + 128]
            delta = delta + fold[:, t : t + 128]
    inverse = 1.0 / jnp.sum(total, axis=1, keepdims=True)
    delta = jnp.sum(delta, axis=1, keepdims=True) * inverse
    out = jnp.zeros((2 * rows, width), F32)
    for a, b in spans:
        probs = s_ref[:rows, a:b] * inverse
        x_ref[rows:, a:b] = probs.astype(BF16)
        x_ref[:rows, a:b] = (probs * (s_ref[rows:, a:b] - delta)).astype(BF16)
        x = x_ref[:, a:b]
        out = out + jnp.dot(x, kv_chunk(a, b), preferred_element_type=F32)
        acc_ref[a:b, :] += lax.dot_general(x, y, (((0,), (0,)), ((), ())), preferred_element_type=F32)
    lows = lax.broadcasted_iota(jnp.int32, (rows, width), 1) < HEAD
    res = jnp.where(lows, out[:rows] * SCALE, out[rows:]).astype(BF16)
    for h in range(2):
        for a in range(here):
            at = h * half + a * 64
            dqo_ref[a, h * 64 : (h + 1) * 64, :] = res[at : at + 64]
            send_ref[base + a, h * 64 : (h + 1) * 64, :] = res[at : at + 64]

    @pl.when(step == 0)
    def _():
        pl.semaphore_wait(pltpu.get_barrier_semaphore(), sources - 1)

    for a in range(here):
        @pl.when(base + a != line)
        def _():
            copy(base + a).start()

        @pl.when(base + a == line)
        def _():
            keep().start()

    @pl.when(step == last)
    def _():
        dkv_ref[...] = acc_ref[...].reshape(sources, 128, width).astype(BF16)

        @pl.loop(1, sources)
        def _(k):
            arrival(lax.rem(line + k, sources)).wait()

        keep().wait()


def attention(kvq, here=2, ck=1024):
    sources = kvq.shape[0]
    keys, rows = sources * 128, here * 128
    dma = pltpu.SemaphoreType.DMA

    def block(i):
        here_at = place()
        line = (here_at[0] * 4 + here_at[1]) * 2 + here_at[2]
        return lax.rem(line // here + i + 1, sources // here), 0, 0

    return pl.pallas_call(
        functools.partial(attention_kernel, ck),
        grid=(sources // here,),
        in_specs=[
            pl.BlockSpec((sources, 256, 128), lambda i: (0, 0, 0), pipeline_mode=pl.Buffered(1)),
        ],
        out_specs=[
            pl.BlockSpec((here, 128, 128), block),
            pl.BlockSpec((sources, 128, 128), lambda i: (0, 0, 0)),
            pl.BlockSpec(memory_space=pl.ANY),
        ],
        out_shape=[
            jax.ShapeDtypeStruct((sources, 128, 128), BF16),
            jax.ShapeDtypeStruct((sources, 128, 128), BF16),
            jax.ShapeDtypeStruct((sources, 128, 128), BF16),
        ],
        scratch_shapes=[
            pltpu.VMEM((2 * rows, keys), F32),
            pltpu.VMEM((2 * rows, keys), BF16),
            pltpu.VMEM((2 * rows, 128), BF16),
            pltpu.VMEM((keys, 128), F32),
            pltpu.VMEM((sources, 128, 128), BF16),
            dma((sources,)), dma((sources,)), dma,
        ],
        compiler_params=pltpu.CompilerParams(vmem_limit_bytes=VMEM, collective_id=3, has_side_effects=True),
        cost_estimate=pl.CostEstimate(flops=48 * keys * keys * HEAD, bytes_accessed=4 << 20, transcendentals=keys * keys),
    )(kvq)


def in_weight_kernel(lat_ref, chan_ref, gain_ref, shift_ref, dqo_ref, dkv_ref, out_ref, acc_ref, turned_ref, block_ref):
    step, last = pl.program_id(0), pl.num_programs(0) - 1
    sources, _, channels = lat_ref.shape
    rows = sources * 128

    @pl.when(step == 0)
    def _():
        acc_ref[...] = jnp.zeros_like(acc_ref)

    lat = lat_ref[...].reshape(rows, channels).astype(F32)
    centred = (lat - chan_ref[0:1]) * chan_ref[1:2]
    normed = (centred * gain_ref[...] + shift_ref[...]).astype(BF16)
    grads = jnp.concatenate(
        [dqo_ref[...].reshape(rows, 128), dkv_ref[...].reshape(rows, 128)], axis=1
    )
    acc_ref[...] += lax.dot_general(grads, normed, (((0,), (0,)), ((), ())), preferred_element_type=F32)

    @pl.when(step == last)
    def _():
        turned_ref[...] = acc_ref[...].T
        low = lax.broadcasted_iota(jnp.int32, (5, 128), 1) < HEAD
        for d in range(channels // 10):
            at = d * 10
            block_ref[0:10] = turned_ref[at : at + 10, 128:256]
            first, second = turned_ref[at : at + 5, 0:128], turned_ref[at + 5 : at + 10, 0:128]
            block_ref[10:15] = jnp.where(low, first, pltpu.roll(second, HEAD, 1))
            block_ref[15:16] = jnp.zeros((1, 128), F32)
            out_ref[d] = block_ref[...].astype(BF16)


def in_weight(lat, chan, gain, shift, dqo, dkv, here=4):
    sources, _, channels = lat.shape
    return pl.pallas_call(
        in_weight_kernel,
        grid=(sources // here,),
        in_specs=[
            pl.BlockSpec((here, 128, channels), lambda i: (i, 0, 0)),
            pl.BlockSpec((2, channels), lambda i: (0, 0)),
            pl.BlockSpec((1, channels), lambda i: (0, 0)),
            pl.BlockSpec((1, channels), lambda i: (0, 0)),
            pl.BlockSpec((here, 128, 128), lambda i: (i, 0, 0)),
            pl.BlockSpec((here, 128, 128), lambda i: (i, 0, 0)),
        ],
        out_specs=pl.BlockSpec((channels // 10, 16, 128), lambda i: (0, 0, 0)),
        out_shape=jax.ShapeDtypeStruct((channels // 10, 16, 128), BF16),
        scratch_shapes=[
            pltpu.VMEM((256, channels), F32), pltpu.VMEM((channels, 256), F32), pltpu.VMEM((16, 128), F32),
        ],
        compiler_params=pltpu.CompilerParams(vmem_limit_bytes=VMEM),
        cost_estimate=pl.CostEstimate(flops=2 * 4096 * 1280 * 256, bytes_accessed=14 << 20, transcendentals=0),
    )(lat, chan, gain, shift, dqo, dkv)


def paired(first, second, low, upper):
    if upper:
        return jnp.where(low, pltpu.roll(first.astype(F32), HEAD, 1), second.astype(F32)).astype(BF16)
    return jnp.where(low, first.astype(F32), pltpu.roll(second.astype(F32), HEAD, 1)).astype(BF16)


def shifted(here, k, sign):
    dy, dz, dx = k // 8, (k // 2) % 4, k % 2
    y = (here[0] + (dy if sign > 0 else 4 - dy)) % 4
    z = (here[1] + (dz if sign > 0 else 4 - dz)) % 4
    x = (here[2] + dx) % 2
    return {"y": y, "z": z, "xl": x}, (y * 4 + z) * 2 + x


def tail_kernel(
    count, dqo_ref, dkv_ref, mine_ref, other_ref, halves_ref, lat_ref, cot_ref, cot_far_ref, chan_ref, gain_ref,
    out_ref, weight_ref, mixed_ref, rows_ref, grad_ref, near_ref, far_ref, got_ref, part_ref, att_ref, att_far_ref,
    give_ref, take_ref, part_send, part_recv, sums_send, sums_recv, att_send, att_recv, give_send, give_recv,
):
    here = place()
    own = here[4]
    seqs = far_ref.shape[0]
    line = (here[0] * 4 + here[1]) * 2 + here[2]
    mesh_id = pl.DeviceIdType.MESH

    barrier = pltpu.get_barrier_semaphore()

    @pl.loop(1, seqs)
    def _(k):
        pl.semaphore_signal(barrier, inc=1, device_id=shifted(here, k, 1)[0], device_id_type=mesh_id)

    pl.semaphore_signal(barrier, inc=1, device_id={"own": 1 - own}, device_id_type=mesh_id)
    pl.semaphore_signal(barrier, inc=1, device_id={"rep": 1 - here[3]}, device_id_type=mesh_id)
    pl.semaphore_wait(barrier, seqs + 1)

    def pair(at):
        return pl.ds(at * 2, 2)

    def part_copy(k):
        target, there = shifted(here, k, 1)
        return pltpu.make_async_remote_copy(
            src_ref=part_ref.at[pair(there)], dst_ref=got_ref.at[pair(line)],
            send_sem=part_send.at[k], recv_sem=part_recv.at[k],
            device_id=target, device_id_type=mesh_id,
        )

    def part_arrival(k):
        source, there = shifted(here, k, -1)
        return pltpu.make_async_remote_copy(
            src_ref=part_ref.at[pair(there)], dst_ref=got_ref.at[pair(there)],
            send_sem=part_send.at[k], recv_sem=part_recv.at[k],
            device_id=source, device_id_type=mesh_id,
        )

    def sums_copy(k):
        target, _ = shifted(here, k, 1)
        return pltpu.make_async_remote_copy(
            src_ref=near_ref, dst_ref=far_ref.at[line],
            send_sem=sums_send.at[k], recv_sem=sums_recv.at[k],
            device_id=target, device_id_type=mesh_id,
        )

    def sums_arrival(k):
        source, there = shifted(here, k, -1)
        return pltpu.make_async_remote_copy(
            src_ref=near_ref, dst_ref=far_ref.at[there],
            send_sem=sums_send.at[k], recv_sem=sums_recv.at[k],
            device_id=source, device_id_type=mesh_id,
        )

    inner, half = HEADS * HEAD, mine_ref.shape[0]
    low = lax.broadcasted_iota(jnp.int32, (128, 128), 1) < HEAD
    for h in range(0, HEADS, 2):
        for i in range(2):
            att_ref[i * 128 : (i + 1) * 128, h * HEAD : (h + 2) * HEAD] = paired(dqo_ref[h, i], dqo_ref[h + 1, i], low, True)
    swap = pltpu.make_async_remote_copy(
        src_ref=att_ref, dst_ref=att_far_ref, send_sem=att_send, recv_sem=att_recv,
        device_id={"own": 1 - own}, device_id_type=pl.DeviceIdType.MESH,
    )
    swap.start()
    wide = halves_ref.shape[1]
    near = att_ref[:, pl.ds(pl.multiple_of(own * wide, 128), wide)]
    far = att_ref[:, pl.ds(pl.multiple_of((1 - own) * wide, 128), wide)]
    total = jnp.dot(near, halves_ref[0], preferred_element_type=F32)
    total = total + jnp.dot(far, halves_ref[1], preferred_element_type=F32)
    for i in range(2):
        mixed_ref[i] = (lat_ref[i].astype(F32) + total[i * 128 : (i + 1) * 128]).astype(BF16)
    swap.wait()
    channels = cot_ref.shape[2]
    cot, cot_far = cot_ref[...].reshape(256, channels), cot_far_ref[...].reshape(256, channels)
    for j in range(4):
        row = (here[0] + (j + 1)) % 4
        at = pl.ds(pl.multiple_of(row * 256, 256), 256)
        total = lax.dot_general(att_ref[:, at], cot, (((0,), (0,)), ((), ())), preferred_element_type=F32)
        total = total + lax.dot_general(
            att_far_ref[:, at], cot_far, (((0,), (0,)), ((), ())), preferred_element_type=F32
        )
        blocks = total.reshape(16, 2, 8, channels)
        part_ref[pl.ds(row * 16, 16)] = jnp.where(own == 0, blocks[:, 0], blocks[:, 1]).astype(BF16)

        @pl.loop(0 if j < 3 else 1, 8)
        def _(k):
            part_copy(((j + 1) % 4) * 8 + k).start()

    for h in range(0, HEADS, 2):
        for i in range(2):
            rows, at = slice(i * 128, (i + 1) * 128), h * HEAD
            dq, dk = (dqo_ref[h, i], dqo_ref[h + 1, i]), (dkv_ref[h, i], dkv_ref[h + 1, i])
            rows_ref[rows, at : at + 128] = paired(*dq, low, False)
            rows_ref[rows, inner + at : inner + at + 128] = paired(*dk, low, False)
            rows_ref[rows, 2 * inner + at : 2 * inner + at + 128] = paired(*dk, low, True)
    grads = rows_ref[...]
    for side, w_ref in ((own, mine_ref), (1 - own, other_ref)):
        part = lax.dot_general(grads, w_ref[...], (((1,), (1,)), ((), ())), preferred_element_type=F32)
        lanes = pl.ds(pl.multiple_of(side * half, 128), half)
        for i in range(2):
            grad_ref[i, :, lanes] = part[i * 128 : (i + 1) * 128]
    ones, twos = [], []
    for i in range(2):
        grad = grad_ref[i] * gain_ref[...]
        grad_ref[i] = grad
        centred = (lat_ref[i].astype(F32) - chan_ref[i : i + 1]) * chan_ref[2 + i : 3 + i]
        ones.append(jnp.sum(grad, axis=0, keepdims=True))
        twos.append(jnp.sum(grad * centred, axis=0, keepdims=True))
    table = members(lat_ref.shape[2])
    sums = by_group(four_rows(ones + twos), table)
    near_ref[...] = sums
    far_ref[line] = sums

    @pl.loop(1, seqs)
    def _(k):
        sums_copy(k).start()

    got_ref[pair(line)] = part_ref[pair(line)]

    @pl.loop(1, seqs)
    def _(k):
        sums_arrival(k).wait_recv()

    means = by_channel(jnp.sum(far_ref[...], axis=0) / count, table)
    for i in range(2):
        inv = chan_ref[2 + i : 3 + i]
        centred = (lat_ref[i].astype(F32) - chan_ref[i : i + 1]) * inv
        grad = inv * (grad_ref[i] - means[i : i + 1] - centred * means[2 + i : 3 + i])
        out_ref[i] = (cot_ref[i].astype(F32) + grad).astype(BF16)

    @pl.loop(1, seqs)
    def _(k):
        part_arrival(k).wait_recv()

    total = got_ref[0:8].astype(F32)
    for k in range(8, 2 * seqs, 8):
        total = total + got_ref[k : k + 8].astype(F32)
    pairs = jnp.sum(total.reshape(4, 2, 8, channels), axis=0)
    upper = here[3] == 1
    give_ref[...] = jnp.where(upper, pairs[0], pairs[1])
    give = pltpu.make_async_remote_copy(
        src_ref=give_ref, dst_ref=take_ref, send_sem=give_send, recv_sem=give_recv,
        device_id={"rep": 1 - here[3]}, device_id_type=mesh_id,
    )
    give.start()
    give.wait()
    weight_ref[...] = jnp.where(upper, pairs[1], pairs[0]) + take_ref[...]

    @pl.loop(1, seqs)
    def _(k):
        part_copy(k).wait_send()

    @pl.loop(1, seqs)
    def _(k):
        sums_copy(k).wait_send()


def tail(dqo, dkv, mine, other, halves, lat, cot, cot_far, chan, gain, count):
    channels, wide = lat.shape[2], HEADS * HEAD
    seqs = wide // 32
    dma = pltpu.SemaphoreType.DMA
    return pl.pallas_call(
        functools.partial(tail_kernel, count),
        out_shape=[
            jax.ShapeDtypeStruct(lat.shape, BF16),
            jax.ShapeDtypeStruct((8, channels), F32),
            jax.ShapeDtypeStruct(lat.shape, BF16),
        ],
        scratch_shapes=[
            pltpu.VMEM((256, 3 * HEADS * HEAD), BF16),
            pltpu.VMEM(lat.shape, F32),
            pltpu.VMEM((8, 128), F32),
            pltpu.VMEM((seqs, 8, 128), F32),
            pltpu.VMEM((2 * seqs, 8, channels), BF16),
            pltpu.VMEM((2 * seqs, 8, channels), BF16),
            pltpu.VMEM((256, wide), BF16),
            pltpu.VMEM((256, wide), BF16),
            pltpu.VMEM((8, channels), F32),
            pltpu.VMEM((8, channels), F32),
            dma((seqs,)), dma((seqs,)), dma((seqs,)), dma((seqs,)), dma, dma, dma, dma,
        ],
        compiler_params=pltpu.CompilerParams(vmem_limit_bytes=VMEM, collective_id=1, has_side_effects=True),
        cost_estimate=pl.CostEstimate(flops=2 << 34, bytes_accessed=16 << 20, transcendentals=0),
    )(dqo, dkv, mine, other, halves, lat, cot, cot_far, chan, gain)


def swapped(value, axis):
    return lax.ppermute(value, axis, [(0, 1), (1, 0)])


def exchanged(value, axes):
    return lax.all_to_all(value, axes, 0, 0, tiled=True)


def shards(latent, cotangent, norm_gain, norm_shift, proj_qkv, proj_out):
    local_len, images, channels = latent.shape
    seq_count = lax.axis_size(SEQ)
    count = local_len * seq_count * (channels // GROUPS)
    gain, shift = norm_gain.reshape(1, channels), norm_shift.reshape(1, channels)

    other_out = swapped(proj_out, "own")
    other_qkv = swapped(proj_qkv, "own")
    lat = latent.transpose(1, 0, 2)
    cot = cotangent.transpose(1, 0, 2)
    image = lax.axis_index("xl")
    near = jnp.where(image == 0, lat[0], lat[1])
    far = swapped(jnp.where(image == 0, lat[1], lat[0]), "xl")
    halves_out = jnp.stack([proj_out, other_out])
    cot_far = swapped(cot, "own")
    sums, g = first(lat, cot, proj_out, other_out)
    far, sums = lax.optimization_barrier((far, sums))
    pair_lat = jnp.where(image == 0, jnp.stack([near, far]), jnp.stack([far, near]))
    pair_lat, g = lax.optimization_barrier((pair_lat, g))
    chan, kvqg = project(lat, sums, gain, shift, g, proj_qkv, other_qkv, count)
    pair_lat, kvqg = lax.optimization_barrier((pair_lat, kvqg))
    image_lat = lax.all_gather(pair_lat, ("y", "z"), tiled=True)

    dqo, dkv, dqo_tok = attention(kvqg)

    dkv_tok = exchanged(dkv, SEQ)
    chan_image = jnp.where(image == 0, chan[0:4:2], chan[1:4:2])
    in_part = in_weight(image_lat, chan_image, gain, shift, dqo, dkv)
    dqo_tok, in_part = lax.optimization_barrier((dqo_tok, in_part))
    dqo_tok = dqo_tok.reshape(HEADS, images, 128, 128)
    dkv_tok, in_part = lax.optimization_barrier((dkv_tok, in_part))
    in_blocks = exchanged(in_part, ALL)
    dkv_tok = dkv_tok.reshape(HEADS, images, 128, 128)
    grad_latent, grad_out, mixed = tail(
        dqo_tok, dkv_tok, proj_qkv, other_qkv, halves_out, lat, cot, cot_far, chan, gain, count
    )

    summed = jnp.sum(in_blocks.reshape(HEADS, 8, 16, 128).astype(F32), axis=1)
    dq = summed[:, 10:15].reshape(HEADS, 5, 2, HEAD).transpose(2, 1, 0, 3).reshape(10, HEADS * HEAD)
    dk = summed[:, :10, :HEAD].transpose(1, 0, 2).reshape(10, HEADS * HEAD)
    dv = summed[:, :10, HEAD:].transpose(1, 0, 2).reshape(10, HEADS * HEAD)
    grad_qkv = jnp.concatenate([dq, dk, dv], axis=1)
    return (mixed.transpose(1, 0, 2), grad_latent.transpose(1, 0, 2), grad_qkv, grad_out)


def solution(mesh):
    fine = Mesh(mesh.devices.reshape(4, 4, 2, 2, 2), ALL)
    tokens = P(SEQ, ("rep", "own"), None)
    return jax.shard_map(
        shards,
        mesh=fine,
        in_specs=(tokens, tokens, P(), P(), P("own", None), P("own", None)),
        out_specs=(tokens, tokens, P(ALL, None), P(ALL, None)),
        check_vma=False,
    )
```

```python
import functools

import jax
import jax.numpy as jnp
from jax import lax
from jax.experimental import pallas as pl
from jax.experimental.pallas import tpu as pltpu
from jax.sharding import Mesh
from jax.sharding import PartitionSpec as P

HEADS = 16
HEAD = 64
GROUPS = 32
SCALE = HEAD ** (-0.5)
SEQ = ("y", "z", "xl")
ALL = ("y", "z", "xl", "rep", "own")
F32, BF16 = jnp.float32, jnp.bfloat16
VMEM = 60 << 20


def place():
    return tuple(lax.axis_index(axis) for axis in ALL)


def members(channels):
    channel = lax.broadcasted_iota(jnp.int32, (channels, 128), 0)
    group = lax.broadcasted_iota(jnp.int32, (channels, 128), 1)
    first = group * (channels // GROUPS)
    return ((channel >= first) & (channel < first + channels // GROUPS)).astype(F32)


def by_group(rows, table):
    return lax.dot_general(
        rows, table, (((1,), (0,)), ((), ())),
        precision=lax.Precision.HIGHEST, preferred_element_type=F32,
    )


def by_channel(rows, table):
    return lax.dot_general(
        rows, table, (((1,), (1,)), ((), ())),
        precision=lax.Precision.HIGHEST, preferred_element_type=F32,
    )


def four_rows(rows):
    width = rows[0].shape[1]
    return jnp.concatenate([*rows, jnp.zeros((4, width), F32)], axis=0)


def moments(sums, count):
    means = sums / count
    var = means[2:4] - means[0:2] * means[0:2]
    return jnp.concatenate([means[0:2], lax.rsqrt(var + 1e-06), jnp.zeros((4, 128), F32)], axis=0)


def project_kernel(
    count, lat_ref, sums_ref, gain_ref, shift_ref, g_ref, mine_ref, other_ref,
    chan_ref, out_ref, normed_ref, send_ref, send_sem, recv_sem, keep_sem,
):
    here = place()
    own = here[4]
    half = mine_ref.shape[0]
    inner = HEADS * HEAD
    line = (here[0] * 4 + here[1]) * 2 + here[2]
    seqs = out_ref.shape[0]

    def device(at):
        return {"y": at // 8, "z": (at // 2) % 4, "xl": at % 2}

    barrier = pltpu.get_barrier_semaphore()

    @pl.loop(1, seqs)
    def _(k):
        to = lax.rem(line + k, seqs)
        pl.semaphore_signal(barrier, inc=1, device_id=device(to), device_id_type=pl.DeviceIdType.MESH)

    table = members(lat_ref.shape[2])
    chan = by_channel(moments(sums_ref[...], count), table)
    chan_ref[...] = chan
    for i in range(2):
        centred = (lat_ref[i].astype(F32) - chan[i : i + 1]) * chan[2 + i : 3 + i]
        normed_ref[i * 128 : (i + 1) * 128] = (centred * gain_ref[...] + shift_ref[...]).astype(BF16)
    near = normed_ref[:, pl.ds(pl.multiple_of(own * half, 128), half)]
    far = normed_ref[:, pl.ds(pl.multiple_of((1 - own) * half, 128), half)]
    low = lax.broadcasted_iota(jnp.int32, (128, 128), 1) < HEAD

    def copy(row, column):
        at = row * 8 + column
        return pltpu.make_async_remote_copy(
            src_ref=send_ref.at[at], dst_ref=out_ref.at[line],
            send_sem=send_sem.at[at], recv_sem=recv_sem.at[line],
            device_id=device(at), device_id_type=pl.DeviceIdType.MESH,
        )

    def arrival(at):
        return pltpu.make_async_remote_copy(
            src_ref=send_ref.at[at], dst_ref=out_ref.at[at],
            send_sem=send_sem.at[at], recv_sem=recv_sem.at[at],
            device_id=device(at), device_id_type=pl.DeviceIdType.MESH,
        )

    def block_row(row):
        lanes = [pl.ds(pl.multiple_of(p * inner + row * 256, 256), 256) for p in range(3)]
        query, key, value = [
            jnp.dot(near, mine_ref[:, at], preferred_element_type=F32)
            + jnp.dot(far, other_ref[:, at], preferred_element_type=F32)
            for at in lanes
        ]
        for h in range(0, 4, 2):
            for i in range(2):
                rows, part = slice(i * 128, (i + 1) * 128), slice(h * HEAD, (h + 2) * HEAD)
                q, k, v = query[rows, part], key[rows, part], value[rows, part]
                k_roll, v_roll = pltpu.roll(k, HEAD, 1), pltpu.roll(v, HEAD, 1)
                first, second = q[:64], q[64:]
                one, two = row * 8 + h * 2 + i, row * 8 + (h + 1) * 2 + i
                send_ref[one, :128] = jnp.where(low, k, v_roll).astype(BF16)
                send_ref[two, :128] = jnp.where(low, k_roll, v).astype(BF16)
                send_ref[one, 128:192] = jnp.where(low[:64], first, pltpu.roll(second, HEAD, 1)).astype(BF16)
                send_ref[two, 128:192] = jnp.where(low[:64], pltpu.roll(first, HEAD, 1), second).astype(BF16)
                send_ref[one, 192:256] = g_ref[row * 4 + h, i]
                send_ref[two, 192:256] = g_ref[row * 4 + h + 1, i]

    for j in range(4):
        row = (here[0] + (j + 1)) % 4
        block_row(row)
        if j == 0:
            pl.semaphore_wait(barrier, seqs - 1)
        if j < 3:
            @pl.loop(0, 8)
            def _(k):
                copy(row, (here[1] * 2 + here[2] + k) % 8).start()
        else:
            @pl.loop(1, 8)
            def _(k):
                copy(row, (here[1] * 2 + here[2] + k) % 8).start()

    keep = pltpu.make_async_copy(send_ref.at[line], out_ref.at[line], keep_sem)
    keep.start()

    @pl.loop(1, seqs)
    def _(k):
        arrival(lax.rem(line + k, seqs)).wait()

    keep.wait()


def project(lat, sums, gain, shift, g, mine, other, count):
    channels = lat.shape[2]
    seqs = g.shape[0] * 2
    dma = pltpu.SemaphoreType.DMA
    whole = pl.BlockSpec(memory_space=pltpu.VMEM)
    return pl.pallas_call(
        functools.partial(project_kernel, count),
        in_specs=[whole] * 7,
        out_specs=[whole, pl.BlockSpec(memory_space=pl.ANY)],
        out_shape=[
            jax.ShapeDtypeStruct((8, channels), F32),
            jax.ShapeDtypeStruct((seqs, 256, 128), BF16),
        ],
        scratch_shapes=[
            pltpu.VMEM((256, channels), BF16),
            pltpu.VMEM((seqs, 256, 128), BF16),
            dma((seqs,)), dma((seqs,)), dma,
        ],
        compiler_params=pltpu.CompilerParams(vmem_limit_bytes=VMEM, collective_id=2, has_side_effects=True),
        cost_estimate=pl.CostEstimate(flops=2 << 34, bytes_accessed=12 << 20, transcendentals=0),
    )(lat, sums, gain, shift, g, mine, other)


def first_kernel(
    lat_ref, cot_ref, mine_ref, other_ref, sums_ref, g_ref, near_ref, far_ref, sums_send, sums_recv
):
    here = place()
    own = here[4]
    seqs, channels = far_ref.shape[0], lat_ref.shape[2]
    line = (here[0] * 4 + here[1]) * 2 + here[2]
    mesh_id = pl.DeviceIdType.MESH
    barrier = pltpu.get_barrier_semaphore()

    @pl.loop(1, seqs)
    def _(k):
        pl.semaphore_signal(barrier, inc=1, device_id=shifted(here, k, 1)[0], device_id_type=mesh_id)

    values = [lat_ref[i].astype(F32) for i in range(2)]
    rows = [jnp.sum(v, axis=0, keepdims=True) for v in values]
    rows += [jnp.sum(v * v, axis=0, keepdims=True) for v in values]
    sums = by_group(four_rows(rows), members(channels))
    near_ref[...] = sums
    far_ref[line] = sums

    def sums_copy(k):
        target, _ = shifted(here, k, 1)
        return pltpu.make_async_remote_copy(
            src_ref=near_ref, dst_ref=far_ref.at[line],
            send_sem=sums_send.at[k], recv_sem=sums_recv.at[k],
            device_id=target, device_id_type=mesh_id,
        )

    def sums_arrival(k):
        source, there = shifted(here, k, -1)
        return pltpu.make_async_remote_copy(
            src_ref=near_ref, dst_ref=far_ref.at[there],
            send_sem=sums_send.at[k], recv_sem=sums_recv.at[k],
            device_id=source, device_id_type=mesh_id,
        )

    pl.semaphore_wait(barrier, seqs - 1)

    @pl.loop(1, seqs)
    def _(k):
        sums_copy(k).start()

    cot = cot_ref[...].reshape(256, channels)
    low = lax.broadcasted_iota(jnp.int32, (64, 128), 1) < HEAD
    half = mine_ref.shape[0] // HEAD
    for side, w_ref in ((own, mine_ref), (1 - own, other_ref)):
        grad = lax.dot_general(cot, w_ref[...], (((1,), (1,)), ((), ())), preferred_element_type=F32)
        for h in range(0, half, 2):
            for i in range(2):
                upper = grad[i * 128 : i * 128 + 64, h * HEAD : (h + 2) * HEAD]
                lower = grad[i * 128 + 64 : (i + 1) * 128, h * HEAD : (h + 2) * HEAD]
                g_ref[side * half + h, i] = jnp.where(low, upper, pltpu.roll(lower, HEAD, 1)).astype(BF16)
                g_ref[side * half + h + 1, i] = jnp.where(low, pltpu.roll(upper, HEAD, 1), lower).astype(BF16)

    @pl.loop(1, seqs)
    def _(k):
        sums_arrival(k).wait()

    sums_ref[...] = jnp.sum(far_ref[...], axis=0)


def first(lat, cot, mine, other):
    dma = pltpu.SemaphoreType.DMA
    return pl.pallas_call(
        first_kernel,
        out_shape=[
            jax.ShapeDtypeStruct((8, 128), F32),
            jax.ShapeDtypeStruct((HEADS, 2, 64, 128), BF16),
        ],
        scratch_shapes=[
            pltpu.VMEM((8, 128), F32),
            pltpu.VMEM((2 * HEADS, 8, 128), F32),
            dma((2 * HEADS,)), dma((2 * HEADS,)),
        ],
        compiler_params=pltpu.CompilerParams(vmem_limit_bytes=VMEM, collective_id=4, has_side_effects=True),
        cost_estimate=pl.CostEstimate(flops=2 << 32, bytes_accessed=6 << 20, transcendentals=0),
    )(lat, cot, mine, other)


def attention_kernel(
    ck, kvq_ref, dqo_ref, dkv_ref, tok_ref, s_ref, x_ref, y_ref, acc_ref, send_ref, send_sem, recv_sem, keep_sem
):
    here_at = place()
    line = (here_at[0] * 4 + here_at[1]) * 2 + here_at[2]

    def device(at):
        return {"y": at // 8, "z": (at // 2) % 4, "xl": at % 2}

    def copy(at):
        return pltpu.make_async_remote_copy(
            src_ref=send_ref.at[at], dst_ref=tok_ref.at[line],
            send_sem=send_sem.at[at], recv_sem=recv_sem.at[line],
            device_id=device(at), device_id_type=pl.DeviceIdType.MESH,
        )

    def arrival(at):
        return pltpu.make_async_remote_copy(
            src_ref=send_ref.at[at], dst_ref=tok_ref.at[at],
            send_sem=send_sem.at[at], recv_sem=recv_sem.at[at],
            device_id=device(at), device_id_type=pl.DeviceIdType.MESH,
        )

    def keep():
        return pltpu.make_async_copy(send_ref.at[line], tok_ref.at[line], keep_sem)

    step, last = pl.program_id(0), pl.num_programs(0) - 1
    sources, _, width = kvq_ref.shape
    keys = sources * 128
    here = dqo_ref.shape[0]
    base = lax.rem(line // here * here + (step + 1) * here, sources)
    rows = here * 128
    half = rows // 2

    @pl.when(step == 0)
    def _():
        acc_ref[...] = jnp.zeros_like(acc_ref)
        barrier = pltpu.get_barrier_semaphore()

        @pl.loop(1, sources)
        def _(k):
            to = lax.rem(line + k, sources)
            pl.semaphore_signal(barrier, inc=1, device_id=device(to), device_id_type=pl.DeviceIdType.MESH)

    low = lax.broadcasted_iota(jnp.int32, (half, width), 1) < HEAD
    xq = kvq_ref[pl.ds(base, here), 128:192, :].reshape(half, width).astype(F32) * SCALE
    xg = kvq_ref[pl.ds(base, here), 192:256, :].reshape(half, width).astype(F32)
    zero = jnp.zeros_like(xq)
    y_ref[0 * half : 1 * half] = jnp.where(low, xq, zero).astype(BF16)
    y_ref[1 * half : 2 * half] = jnp.where(low, pltpu.roll(xq, HEAD, 1), zero).astype(BF16)
    y_ref[2 * half : 3 * half] = jnp.where(low, zero, pltpu.roll(xg, HEAD, 1)).astype(BF16)
    y_ref[3 * half : 4 * half] = jnp.where(low, zero, xg).astype(BF16)
    y = y_ref[...]
    spans = [(c, c + ck) for c in range(0, keys, ck)]

    def kv_chunk(a, b):
        return kvq_ref[a // 128 : b // 128, :128, :].reshape(b - a, width)

    top = None
    for a, b in spans:
        both = lax.dot_general(y, kv_chunk(a, b), (((1,), (1,)), ((), ())), preferred_element_type=F32)
        s_ref[:, a:b] = both
        for t in range(0, ck, 128):
            piece = both[:rows, t : t + 128]
            top = piece if top is None else jnp.maximum(top, piece)
    top = jnp.max(top, axis=1, keepdims=True)
    total = jnp.zeros((rows, 128), F32)
    delta = jnp.zeros((rows, 128), F32)
    for a, b in spans:
        weights = jnp.exp(s_ref[:rows, a:b] - top)
        s_ref[:rows, a:b] = weights
        fold = weights * s_ref[rows:, a:b]
        for t in range(0, ck, 128):
            total = total + weights[:, t : t + 128]
            delta = delta + fold[:, t : t + 128]
    inverse = 1.0 / jnp.sum(total, axis=1, keepdims=True)
    delta = jnp.sum(delta, axis=1, keepdims=True) * inverse
    out = jnp.zeros((2 * rows, width), F32)
    for a, b in spans:
        probs = s_ref[:rows, a:b] * inverse
        x_ref[rows:, a:b] = probs.astype(BF16)
        x_ref[:rows, a:b] = (probs * (s_ref[rows:, a:b] - delta)).astype(BF16)
        x = x_ref[:, a:b]
        out = out + jnp.dot(x, kv_chunk(a, b), preferred_element_type=F32)
        acc_ref[a:b, :] += lax.dot_general(x, y, (((0,), (0,)), ((), ())), preferred_element_type=F32)
    lows = lax.broadcasted_iota(jnp.int32, (rows, width), 1) < HEAD
    res = jnp.where(lows, out[:rows] * SCALE, out[rows:]).astype(BF16)
    for h in range(2):
        for a in range(here):
            at = h * half + a * 64
            dqo_ref[a, h * 64 : (h + 1) * 64, :] = res[at : at + 64]
            send_ref[base + a, h * 64 : (h + 1) * 64, :] = res[at : at + 64]

    @pl.when(step == 0)
    def _():
        pl.semaphore_wait(pltpu.get_barrier_semaphore(), sources - 1)

    for a in range(here):
        @pl.when(base + a != line)
        def _():
            copy(base + a).start()

        @pl.when(base + a == line)
        def _():
            keep().start()

    @pl.when(step == last)
    def _():
        dkv_ref[...] = acc_ref[...].reshape(sources, 128, width).astype(BF16)

        @pl.loop(1, sources)
        def _(k):
            arrival(lax.rem(line + k, sources)).wait()

        keep().wait()


def attention(kvq, here=2, ck=1024):
    sources = kvq.shape[0]
    keys, rows = sources * 128, here * 128
    dma = pltpu.SemaphoreType.DMA

    def block(i):
        here_at = place()
        line = (here_at[0] * 4 + here_at[1]) * 2 + here_at[2]
        return lax.rem(line // here + i + 1, sources // here), 0, 0

    return pl.pallas_call(
        functools.partial(attention_kernel, ck),
        grid=(sources // here,),
        in_specs=[
            pl.BlockSpec((sources, 256, 128), lambda i: (0, 0, 0), pipeline_mode=pl.Buffered(1)),
        ],
        out_specs=[
            pl.BlockSpec((here, 128, 128), block),
            pl.BlockSpec((sources, 128, 128), lambda i: (0, 0, 0)),
            pl.BlockSpec(memory_space=pl.ANY),
        ],
        out_shape=[
            jax.ShapeDtypeStruct((sources, 128, 128), BF16),
            jax.ShapeDtypeStruct((sources, 128, 128), BF16),
            jax.ShapeDtypeStruct((sources, 128, 128), BF16),
        ],
        scratch_shapes=[
            pltpu.VMEM((2 * rows, keys), F32),
            pltpu.VMEM((2 * rows, keys), BF16),
            pltpu.VMEM((2 * rows, 128), BF16),
            pltpu.VMEM((keys, 128), F32),
            pltpu.VMEM((sources, 128, 128), BF16),
            dma((sources,)), dma((sources,)), dma,
        ],
        compiler_params=pltpu.CompilerParams(vmem_limit_bytes=VMEM, collective_id=3, has_side_effects=True),
        cost_estimate=pl.CostEstimate(flops=48 * keys * keys * HEAD, bytes_accessed=4 << 20, transcendentals=keys * keys),
    )(kvq)


def in_weight_kernel(lat_ref, chan_ref, gain_ref, shift_ref, dqo_ref, dkv_ref, out_ref, acc_ref, turned_ref, block_ref):
    step, last = pl.program_id(0), pl.num_programs(0) - 1
    sources, _, channels = lat_ref.shape
    rows = sources * 128

    @pl.when(step == 0)
    def _():
        acc_ref[...] = jnp.zeros_like(acc_ref)

    lat = lat_ref[...].reshape(rows, channels).astype(F32)
    centred = (lat - chan_ref[0:1]) * chan_ref[1:2]
    normed = (centred * gain_ref[...] + shift_ref[...]).astype(BF16)
    grads = jnp.concatenate(
        [dqo_ref[...].reshape(rows, 128), dkv_ref[...].reshape(rows, 128)], axis=1
    )
    acc_ref[...] += lax.dot_general(grads, normed, (((0,), (0,)), ((), ())), preferred_element_type=F32)

    @pl.when(step == last)
    def _():
        turned_ref[...] = acc_ref[...].T
        low = lax.broadcasted_iota(jnp.int32, (5, 128), 1) < HEAD
        for d in range(channels // 10):
            at = d * 10
            block_ref[0:10] = turned_ref[at : at + 10, 128:256]
            first, second = turned_ref[at : at + 5, 0:128], turned_ref[at + 5 : at + 10, 0:128]
            block_ref[10:15] = jnp.where(low, first, pltpu.roll(second, HEAD, 1))
            block_ref[15:16] = jnp.zeros((1, 128), F32)
            out_ref[d] = block_ref[...].astype(BF16)


def in_weight(lat, chan, gain, shift, dqo, dkv, here=4):
    sources, _, channels = lat.shape
    return pl.pallas_call(
        in_weight_kernel,
        grid=(sources // here,),
        in_specs=[
            pl.BlockSpec((here, 128, channels), lambda i: (i, 0, 0)),
            pl.BlockSpec((2, channels), lambda i: (0, 0)),
            pl.BlockSpec((1, channels), lambda i: (0, 0)),
            pl.BlockSpec((1, channels), lambda i: (0, 0)),
            pl.BlockSpec((here, 128, 128), lambda i: (i, 0, 0)),
            pl.BlockSpec((here, 128, 128), lambda i: (i, 0, 0)),
        ],
        out_specs=pl.BlockSpec((channels // 10, 16, 128), lambda i: (0, 0, 0)),
        out_shape=jax.ShapeDtypeStruct((channels // 10, 16, 128), BF16),
        scratch_shapes=[
            pltpu.VMEM((256, channels), F32), pltpu.VMEM((channels, 256), F32), pltpu.VMEM((16, 128), F32),
        ],
        compiler_params=pltpu.CompilerParams(vmem_limit_bytes=VMEM),
        cost_estimate=pl.CostEstimate(flops=2 * 4096 * 1280 * 256, bytes_accessed=14 << 20, transcendentals=0),
    )(lat, chan, gain, shift, dqo, dkv)


def paired(first, second, low, upper):
    if upper:
        return jnp.where(low, pltpu.roll(first.astype(F32), HEAD, 1), second.astype(F32)).astype(BF16)
    return jnp.where(low, first.astype(F32), pltpu.roll(second.astype(F32), HEAD, 1)).astype(BF16)


def shifted(here, k, sign):
    dy, dz, dx = k // 8, (k // 2) % 4, k % 2
    y = (here[0] + (dy if sign > 0 else 4 - dy)) % 4
    z = (here[1] + (dz if sign > 0 else 4 - dz)) % 4
    x = (here[2] + dx) % 2
    return {"y": y, "z": z, "xl": x}, (y * 4 + z) * 2 + x


def tail_kernel(
    count, dqo_ref, dkv_ref, mine_ref, other_ref, halves_ref, lat_ref, cot_ref, cot_far_ref, chan_ref, gain_ref,
    out_ref, weight_ref, mixed_ref, rows_ref, grad_ref, near_ref, far_ref, got_ref, part_ref, att_ref, att_far_ref,
    give_ref, take_ref, part_send, part_recv, sums_send, sums_recv, att_send, att_recv, give_send, give_recv,
):
    here = place()
    own = here[4]
    seqs = far_ref.shape[0]
    line = (here[0] * 4 + here[1]) * 2 + here[2]
    mesh_id = pl.DeviceIdType.MESH

    barrier = pltpu.get_barrier_semaphore()

    @pl.loop(1, seqs)
    def _(k):
        pl.semaphore_signal(barrier, inc=1, device_id=shifted(here, k, 1)[0], device_id_type=mesh_id)

    pl.semaphore_signal(barrier, inc=1, device_id={"own": 1 - own}, device_id_type=mesh_id)
    pl.semaphore_signal(barrier, inc=1, device_id={"rep": 1 - here[3]}, device_id_type=mesh_id)
    pl.semaphore_wait(barrier, seqs + 1)

    def pair(at):
        return pl.ds(at * 2, 2)

    def part_copy(k):
        target, there = shifted(here, k, 1)
        return pltpu.make_async_remote_copy(
            src_ref=part_ref.at[pair(there)], dst_ref=got_ref.at[pair(line)],
            send_sem=part_send.at[k], recv_sem=part_recv.at[k],
            device_id=target, device_id_type=mesh_id,
        )

    def part_arrival(k):
        source, there = shifted(here, k, -1)
        return pltpu.make_async_remote_copy(
            src_ref=part_ref.at[pair(there)], dst_ref=got_ref.at[pair(there)],
            send_sem=part_send.at[k], recv_sem=part_recv.at[k],
            device_id=source, device_id_type=mesh_id,
        )

    def sums_copy(k):
        target, _ = shifted(here, k, 1)
        return pltpu.make_async_remote_copy(
            src_ref=near_ref, dst_ref=far_ref.at[line],
            send_sem=sums_send.at[k], recv_sem=sums_recv.at[k],
            device_id=target, device_id_type=mesh_id,
        )

    def sums_arrival(k):
        source, there = shifted(here, k, -1)
        return pltpu.make_async_remote_copy(
            src_ref=near_ref, dst_ref=far_ref.at[there],
            send_sem=sums_send.at[k], recv_sem=sums_recv.at[k],
            device_id=source, device_id_type=mesh_id,
        )

    inner, half = HEADS * HEAD, mine_ref.shape[0]
    low = lax.broadcasted_iota(jnp.int32, (128, 128), 1) < HEAD
    for h in range(0, HEADS, 2):
        for i in range(2):
            att_ref[i * 128 : (i + 1) * 128, h * HEAD : (h + 2) * HEAD] = paired(dqo_ref[h, i], dqo_ref[h + 1, i], low, True)
    swap = pltpu.make_async_remote_copy(
        src_ref=att_ref, dst_ref=att_far_ref, send_sem=att_send, recv_sem=att_recv,
        device_id={"own": 1 - own}, device_id_type=pl.DeviceIdType.MESH,
    )
    swap.start()
    wide = halves_ref.shape[1]
    near = att_ref[:, pl.ds(pl.multiple_of(own * wide, 128), wide)]
    far = att_ref[:, pl.ds(pl.multiple_of((1 - own) * wide, 128), wide)]
    total = jnp.dot(near, halves_ref[0], preferred_element_type=F32)
    total = total + jnp.dot(far, halves_ref[1], preferred_element_type=F32)
    for i in range(2):
        mixed_ref[i] = (lat_ref[i].astype(F32) + total[i * 128 : (i + 1) * 128]).astype(BF16)
    swap.wait()
    channels = cot_ref.shape[2]
    cot, cot_far = cot_ref[...].reshape(256, channels), cot_far_ref[...].reshape(256, channels)
    def tile(j):
        row = (here[0] + (j + 1)) % 4
        at = pl.ds(pl.multiple_of(row * 256, 256), 256)
        total = lax.dot_general(att_ref[:, at], cot, (((0,), (0,)), ((), ())), preferred_element_type=F32)
        total = total + lax.dot_general(
            att_far_ref[:, at], cot_far, (((0,), (0,)), ((), ())), preferred_element_type=F32
        )
        blocks = total.reshape(16, 2, 8, channels)
        part_ref[pl.ds(row * 16, 16)] = jnp.where(own == 0, blocks[:, 0], blocks[:, 1]).astype(BF16)

        @pl.loop(0 if j < 3 else 1, 8)
        def _(k):
            part_copy(((j + 1) % 4) * 8 + k).start()

    tile(0)
    tile(1)
    for h in range(0, HEADS, 2):
        for i in range(2):
            rows, at = slice(i * 128, (i + 1) * 128), h * HEAD
            dq, dk = (dqo_ref[h, i], dqo_ref[h + 1, i]), (dkv_ref[h, i], dkv_ref[h + 1, i])
            rows_ref[rows, at : at + 128] = paired(*dq, low, False)
            rows_ref[rows, inner + at : inner + at + 128] = paired(*dk, low, False)
            rows_ref[rows, 2 * inner + at : 2 * inner + at + 128] = paired(*dk, low, True)
    grads = rows_ref[...]
    for side, w_ref in ((own, mine_ref), (1 - own, other_ref)):
        part = lax.dot_general(grads, w_ref[...], (((1,), (1,)), ((), ())), preferred_element_type=F32)
        lanes = pl.ds(pl.multiple_of(side * half, 128), half)
        for i in range(2):
            grad_ref[i, :, lanes] = part[i * 128 : (i + 1) * 128]
    ones, twos = [], []
    for i in range(2):
        grad = grad_ref[i] * gain_ref[...]
        grad_ref[i] = grad
        centred = (lat_ref[i].astype(F32) - chan_ref[i : i + 1]) * chan_ref[2 + i : 3 + i]
        ones.append(jnp.sum(grad, axis=0, keepdims=True))
        twos.append(jnp.sum(grad * centred, axis=0, keepdims=True))
    table = members(lat_ref.shape[2])
    sums = by_group(four_rows(ones + twos), table)
    near_ref[...] = sums
    far_ref[line] = sums

    @pl.loop(1, seqs)
    def _(k):
        sums_copy(k).start()

    tile(2)
    tile(3)
    got_ref[pair(line)] = part_ref[pair(line)]

    @pl.loop(1, seqs)
    def _(k):
        sums_arrival(k).wait_recv()

    means = by_channel(jnp.sum(far_ref[...], axis=0) / count, table)
    for i in range(2):
        inv = chan_ref[2 + i : 3 + i]
        centred = (lat_ref[i].astype(F32) - chan_ref[i : i + 1]) * inv
        grad = inv * (grad_ref[i] - means[i : i + 1] - centred * means[2 + i : 3 + i])
        out_ref[i] = (cot_ref[i].astype(F32) + grad).astype(BF16)

    @pl.loop(1, seqs)
    def _(k):
        part_arrival(k).wait_recv()

    total = got_ref[0:8].astype(F32)
    for k in range(8, 2 * seqs, 8):
        total = total + got_ref[k : k + 8].astype(F32)
    pairs = jnp.sum(total.reshape(4, 2, 8, channels), axis=0)
    upper = here[3] == 1
    give_ref[...] = jnp.where(upper, pairs[0], pairs[1])
    give = pltpu.make_async_remote_copy(
        src_ref=give_ref, dst_ref=take_ref, send_sem=give_send, recv_sem=give_recv,
        device_id={"rep": 1 - here[3]}, device_id_type=mesh_id,
    )
    give.start()
    give.wait()
    weight_ref[...] = jnp.where(upper, pairs[1], pairs[0]) + take_ref[...]

    @pl.loop(1, seqs)
    def _(k):
        part_copy(k).wait_send()

    @pl.loop(1, seqs)
    def _(k):
        sums_copy(k).wait_send()


def tail(dqo, dkv, mine, other, halves, lat, cot, cot_far, chan, gain, count):
    channels, wide = lat.shape[2], HEADS * HEAD
    seqs = wide // 32
    dma = pltpu.SemaphoreType.DMA
    return pl.pallas_call(
        functools.partial(tail_kernel, count),
        out_shape=[
            jax.ShapeDtypeStruct(lat.shape, BF16),
            jax.ShapeDtypeStruct((8, channels), F32),
            jax.ShapeDtypeStruct(lat.shape, BF16),
        ],
        scratch_shapes=[
            pltpu.VMEM((256, 3 * HEADS * HEAD), BF16),
            pltpu.VMEM(lat.shape, F32),
            pltpu.VMEM((8, 128), F32),
            pltpu.VMEM((seqs, 8, 128), F32),
            pltpu.VMEM((2 * seqs, 8, channels), BF16),
            pltpu.VMEM((2 * seqs, 8, channels), BF16),
            pltpu.VMEM((256, wide), BF16),
            pltpu.VMEM((256, wide), BF16),
            pltpu.VMEM((8, channels), F32),
            pltpu.VMEM((8, channels), F32),
            dma((seqs,)), dma((seqs,)), dma((seqs,)), dma((seqs,)), dma, dma, dma, dma,
        ],
        compiler_params=pltpu.CompilerParams(vmem_limit_bytes=VMEM, collective_id=1, has_side_effects=True),
        cost_estimate=pl.CostEstimate(flops=2 << 34, bytes_accessed=16 << 20, transcendentals=0),
    )(dqo, dkv, mine, other, halves, lat, cot, cot_far, chan, gain)


def swapped(value, axis):
    return lax.ppermute(value, axis, [(0, 1), (1, 0)])


def exchanged(value, axes):
    return lax.all_to_all(value, axes, 0, 0, tiled=True)


def shards(latent, cotangent, norm_gain, norm_shift, proj_qkv, proj_out):
    local_len, images, channels = latent.shape
    seq_count = lax.axis_size(SEQ)
    count = local_len * seq_count * (channels // GROUPS)
    gain, shift = norm_gain.reshape(1, channels), norm_shift.reshape(1, channels)

    other_out = swapped(proj_out, "own")
    other_qkv = swapped(proj_qkv, "own")
    lat = latent.transpose(1, 0, 2)
    cot = cotangent.transpose(1, 0, 2)
    image = lax.axis_index("xl")
    near = jnp.where(image == 0, lat[0], lat[1])
    far = swapped(jnp.where(image == 0, lat[1], lat[0]), "xl")
    halves_out = jnp.stack([proj_out, other_out])
    cot_far = swapped(cot, "own")
    sums, g = first(lat, cot, proj_out, other_out)
    far, sums = lax.optimization_barrier((far, sums))
    pair_lat = jnp.where(image == 0, jnp.stack([near, far]), jnp.stack([far, near]))
    pair_lat, g = lax.optimization_barrier((pair_lat, g))
    chan, kvqg = project(lat, sums, gain, shift, g, proj_qkv, other_qkv, count)
    pair_lat, kvqg = lax.optimization_barrier((pair_lat, kvqg))
    image_lat = lax.all_gather(pair_lat, ("y", "z"), tiled=True)

    dqo, dkv, dqo_tok = attention(kvqg)

    dkv_tok = exchanged(dkv, SEQ)
    chan_image = jnp.where(image == 0, chan[0:4:2], chan[1:4:2])
    in_part = in_weight(image_lat, chan_image, gain, shift, dqo, dkv)
    dqo_tok, in_part = lax.optimization_barrier((dqo_tok, in_part))
    dqo_tok = dqo_tok.reshape(HEADS, images, 128, 128)
    dkv_tok, in_part = lax.optimization_barrier((dkv_tok, in_part))
    in_blocks = exchanged(in_part, ALL)
    dkv_tok = dkv_tok.reshape(HEADS, images, 128, 128)
    grad_latent, grad_out, mixed = tail(
        dqo_tok, dkv_tok, proj_qkv, other_qkv, halves_out, lat, cot, cot_far, chan, gain, count
    )

    summed = jnp.sum(in_blocks.reshape(HEADS, 8, 16, 128).astype(F32), axis=1)
    dq = summed[:, 10:15].reshape(HEADS, 5, 2, HEAD).transpose(2, 1, 0, 3).reshape(10, HEADS * HEAD)
    dk = summed[:, :10, :HEAD].transpose(1, 0, 2).reshape(10, HEADS * HEAD)
    dv = summed[:, :10, HEAD:].transpose(1, 0, 2).reshape(10, HEADS * HEAD)
    grad_qkv = jnp.concatenate([dq, dk, dv], axis=1)
    return (mixed.transpose(1, 0, 2), grad_latent.transpose(1, 0, 2), grad_qkv, grad_out)


def solution(mesh):
    fine = Mesh(mesh.devices.reshape(4, 4, 2, 2, 2), ALL)
    tokens = P(SEQ, ("rep", "own"), None)
    return jax.shard_map(
        shards,
        mesh=fine,
        in_specs=(tokens, tokens, P(), P(), P("own", None), P("own", None)),
        out_specs=(tokens, tokens, P(ALL, None), P(ALL, None)),
        check_vma=False,
    )
```
